32 devices in a mesh: rep: 8 (over y, x, core), shard: 4 (over z).
Axes of the slice: x: 2, y: 2, z: 4, core: 2. Of those that a mesh axis runs over, the one named last changes fastest.
Arguments:
- hidden_in: float32 [32768, 768], P(('rep', 'shard')), may hold values from -6 to 6
- cotangent: float32 [32768, 768], P(('rep', 'shard')), may hold values from -6 to 6
- seg_ids: int32 [32768], P(('rep', 'shard')), may hold values from 0 to 127, as said below
- first_gain: bfloat16 [768], P('shard'), may hold values from 0.5 to 1.5
- first_shift: bfloat16 [768], P('shard'), may hold values from -1 to 1
- second_gain: bfloat16 [768], P('shard'), may hold values from 0.5 to 1.5
- second_shift: bfloat16 [768], P('shard'), may hold values from -1 to 1
- qkv_weight: bfloat16 [768, 2304], P('shard'), may hold values from -0.21875 to 0.21875
- qkv_bias: bfloat16 [2304], P('shard'), may hold values from -1.5 to 1.5
- out_weight: bfloat16 [768, 768], P('shard'), may hold values from -1.25 to 1.25
- out_bias: bfloat16 [768], P('shard'), may hold values from -1.5 to 1.5
- up_weight: bfloat16 [768, 3072], P('shard'), may hold values from -0.21875 to 0.21875
- up_bias: bfloat16 [3072], P('shard'), may hold values from -1.5 to 1.5
- down_weight: bfloat16 [3072, 768], P('shard'), may hold values from -0.109375 to 0.109375
- down_bias: bfloat16 [768], P('shard'), may hold values from -1.5 to 1.5
Outputs:
- output: float32 [32768, 768], P(('rep', 'shard'))
- input_grad: float32 [32768, 768], P(('rep', 'shard'))
- first_gain_grad: float32 [768], P('shard')
- first_shift_grad: float32 [768], P('shard')
- second_gain_grad: float32 [768], P('shard')
- second_shift_grad: float32 [768], P('shard')
- qkv_weight_grad: float32 [768, 2304], P('shard')
- qkv_bias_grad: float32 [2304], P('shard')
- out_weight_grad: float32 [768, 768], P('shard')
- out_bias_grad: float32 [768], P('shard')
- up_weight_grad: float32 [768, 3072], P('shard')
- up_bias_grad: float32 [3072], P('shard')
- down_weight_grad: float32 [3072, 768], P('shard')
- down_bias_grad: float32 [768], P('shard')
The draws below stay inside these ranges and needn't reach their ends.
Inputs may be any that keep to these rules, and one draw needn't show every extreme that they name: Within each aligned block of 1024 rows (one device's token slots) seg_ids start at 0 on the block's first row, never fall, rise by at most one from row to row and only on rows whose place in the block is a multiple of 8; every slot belongs to a sequence; in every draw some block holds one single sequence of 1024 tokens, and another holds 128 sequences of 8 tokens.
All inputs are finite; a program needn't handle non-finite values.
Results may differ from the reference program's by a relative error of at most 0.0091.
Values may be sent and summed in bfloat16 or wider, within the bound.
No kernel may reach another device: no remote copies, remote signals or barrier semaphores. Data moves between devices by JAX's collectives and lax.ppermute only.
A program may use at most 320 MiB of HBM per device.

```python
import jax
import jax.numpy as jnp
from jax import lax

D = 768
H = 12
HD = 64
ROT = 16
FF = 3072
TOK_DEV = 1024
TOKENS = 32768


def draw_seg_ids(key, part):
    devices_all = TOKENS // TOK_DEV
    key_rate, key_bits, key_whole, key_dense = jax.random.split(jax.random.fold_in(key, 7), 4)
    exponent = jax.random.randint(key_rate, (devices_all, 1), 0, 8)
    period = jnp.left_shift(jnp.ones((devices_all, 1), jnp.int32), exponent)
    raw_bits = jax.random.randint(key_bits, (devices_all, TOK_DEV), 0, 1 << 20)
    col_index = jnp.arange(TOK_DEV, dtype=jnp.int32)[None, :]
    on_grid = col_index % 8 == 0
    breaks = ((raw_bits % period == 0) & on_grid).astype(jnp.int32)
    whole_dev = jax.random.randint(key_whole, (), 0, devices_all)
    dense_dev = (whole_dev + 1 + jax.random.randint(key_dense, (), 0, devices_all - 1)) % devices_all
    dev_rows = jnp.arange(devices_all, dtype=jnp.int32)[:, None]
    breaks = jnp.where(dev_rows == dense_dev, on_grid.astype(jnp.int32), breaks)
    breaks = jnp.where(dev_rows == whole_dev, 0, breaks)
    breaks = jnp.where(col_index == 0, 0, breaks)
    segments = jnp.cumsum(breaks, axis=1)
    return segments.reshape(-1).astype(jnp.int32)


def block_scale(own_key, shape, cuts, low, largest):
    level, own = 1.0, jax.random.fold_in(own_key, 6)
    for dim, parts in cuts:
        steps = jnp.exp(jax.random.uniform(jax.random.fold_in(own, dim), (parts,), jnp.float32, low / len(cuts), largest / len(cuts)))
        level = level * jnp.repeat(steps, shape[dim] // parts).reshape([-1 if axis == dim else 1 for axis in range(len(shape))])
    return level


def gaussian(key, shape, deviation, limit, shards=(), kind=jnp.bfloat16):
    array = jax.random.normal(key, shape, jnp.float32) * deviation
    if len(shards) > 0:
        array = block_scale(key, shape, shards, -0.22, 0.18) * array
    return jnp.clip(array, min=-limit, max=limit).astype(kind)


def setup_inputs(seed: int = 0) -> dict:
    keys = jax.random.split(jax.random.key(seed), 16)
    hidden_in = gaussian(keys[0], (TOKENS, D), 1.0, 6.0, ((0, 32),), jnp.float32)
    cotangent = gaussian(keys[1], (TOKENS, D), 1.0, 6.0, ((0, 32),), jnp.float32)
    seg_ids = draw_seg_ids(jax.random.fold_in(keys[15], 71), 0)
    first_gain = jnp.clip(1.0 + 0.1 * jax.random.normal(keys[3], (D,), jnp.float32), 0.5, 1.5).astype(jnp.bfloat16)
    first_shift = gaussian(keys[4], (D,), 0.2, 1.0, ((0, 4),))
    second_gain = jnp.clip(1.0 + 0.1 * jax.random.normal(keys[5], (D,), jnp.float32), 0.5, 1.5).astype(jnp.bfloat16)
    second_shift = gaussian(keys[6], (D,), 0.2, 1.0, ((0, 4),))
    qkv_weight = gaussian(keys[7], (D, 3 * D), D ** -0.5, 0.21875, ((0, 4),))
    qkv_bias = gaussian(keys[8], (3 * D,), 0.3, 1.5, ((0, 4),))
    out_weight = gaussian(keys[9], (D, D), (max(D // 32, 1)) ** -0.5, 1.25, ((0, 4),))
    out_bias = gaussian(keys[10], (D,), 0.3, 1.5, ((0, 4),))
    up_weight = gaussian(keys[11], (D, FF), D ** -0.5, 0.21875, ((0, 4),))
    up_bias = gaussian(keys[12], (FF,), 0.3, 1.5, ((0, 4),))
    down_weight = gaussian(keys[13], (FF, D), FF ** -0.5, 0.109375, ((0, 4),))
    down_bias = gaussian(keys[14], (D,), 0.3, 1.5, ((0, 4),))
    return {"hidden_in": hidden_in, "cotangent": cotangent, "seg_ids": seg_ids, "first_gain": first_gain, "first_shift": first_shift, "second_gain": second_gain, "second_shift": second_shift, "qkv_weight": qkv_weight, "qkv_bias": qkv_bias, "out_weight": out_weight, "out_bias": out_bias, "up_weight": up_weight, "up_bias": up_bias, "down_weight": down_weight, "down_bias": down_bias}


@jax.custom_vjp
def low(v):
    return lax.optimization_barrier(v.astype(jnp.bfloat16)).astype(jnp.float32)

@jax.custom_vjp
def low_back(v):
    return v

def low_keep(v):
    return (low(v), None)

def low_pass(kept, grad):
    return (grad,)

def back_keep(v):
    return (v, None)

def back_low(kept, grad):
    return (low(grad),)
low.defvjp(low_keep, low_pass)
low_back.defvjp(back_keep, back_low)
norm_eps = 1e-05
highest = lax.Precision.HIGHEST

def layer_norm(values, gain, shift):
    centre = values - lax.optimization_barrier(jnp.mean(values, axis=-1, keepdims=True))
    spread = lax.optimization_barrier(jnp.mean(centre * centre, axis=-1, keepdims=True))
    return centre * lax.rsqrt(spread + norm_eps) * gain + shift

def seq_positions(segments):
    row_index = jnp.arange(segments.shape[0], dtype=jnp.int32)
    previous = jnp.concatenate([jnp.full((1,), -1, jnp.int32), segments[:-1].astype(jnp.int32)])
    starts = jnp.where(segments != previous, row_index, 0).astype(jnp.int32)
    return row_index - lax.cummax(starts, axis=0)

def rotate(heads_in, places):
    half = ROT // 2
    freqs = 1.0 / 10000.0 ** (jnp.arange(half, dtype=jnp.float32) * 2.0 / ROT)
    angles = places.astype(jnp.float32)[:, None] * freqs[None, :]
    cosine = jnp.cos(angles)[:, None, :]
    sine = jnp.sin(angles)[:, None, :]
    first = heads_in[..., :half]
    second = heads_in[..., half:ROT]
    return jnp.concatenate([first * cosine - second * sine, second * cosine + first * sine, heads_in[..., ROT:]], axis=-1)

def layer_block(params, hidden, segments):
    first_gain, first_shift, second_gain, second_shift, qkv_weight, qkv_bias, out_weight, out_bias, up_weight, up_bias, down_weight, down_bias = params
    tokens_here = hidden.shape[0]
    places = seq_positions(segments)
    first_normed = low(layer_norm(hidden, first_gain, first_shift))
    qkv = low_back(jnp.dot(first_normed, qkv_weight, precision=highest) + qkv_bias)
    qkv = qkv.reshape(tokens_here, 3, H, HD)
    query_b = low(rotate(qkv[:, 0], places))
    key_b = low(rotate(qkv[:, 1], places))
    value_b = low(qkv[:, 2])
    scores = low_back(jnp.einsum('qhd,khd->hqk', query_b, key_b, precision=highest) * HD ** (-0.5))
    row_index = jnp.arange(tokens_here, dtype=jnp.int32)
    allowed = (segments[:, None] == segments[None, :]) & (row_index[None, :] <= row_index[:, None])
    scores = jnp.where(allowed[None], scores, -1e+30)
    probs_b = low(jax.nn.softmax(scores, axis=-1))
    mixed = low(low_back(jnp.einsum('hqk,khd->qhd', probs_b, value_b, precision=highest))).reshape(tokens_here, D)
    attn_out = low_back(jnp.dot(mixed, out_weight, precision=highest)) + out_bias
    second_normed = low(layer_norm(hidden, second_gain, second_shift))
    up = low_back(jnp.dot(second_normed, up_weight, precision=highest) + up_bias)
    act = low(jax.nn.gelu(up, approximate=False))
    mlp_out = low_back(jnp.dot(act, down_weight, precision=highest)) + down_bias
    return hidden + attn_out + mlp_out

def reference(hidden_in, cotangent, seg_ids, first_gain, first_shift, second_gain, second_shift, qkv_weight, qkv_bias, out_weight, out_bias, up_weight, up_bias, down_weight, down_bias):
    params = tuple((item.astype(jnp.float32) for item in (first_gain, first_shift, second_gain, second_shift, qkv_weight, qkv_bias, out_weight, out_bias, up_weight, up_bias, down_weight, down_bias)))
    blocks = TOKENS // TOK_DEV
    inputs = hidden_in.reshape(blocks, TOK_DEV, D)
    segments = seg_ids.reshape(blocks, TOK_DEV)

    def forward(weights, values):
        step = jax.checkpoint(lambda pair: layer_block(weights, pair[0], pair[1]))
        return lax.map(step, (values, segments))
    result, pull = jax.vjp(forward, params, inputs)
    grads, input_grad = pull(cotangent.reshape(blocks, TOK_DEV, D))
    return (result.reshape(TOKENS, D), input_grad.reshape(TOKENS, D), grads[0], grads[1], grads[2], grads[3], grads[4], grads[5], grads[6], grads[7], grads[8], grads[9], grads[10], grads[11])
```

```python
import functools

import jax
import jax.numpy as jnp
from jax import lax
from jax.experimental import pallas as pl
from jax.experimental.pallas import tpu as pltpu
from jax.sharding import PartitionSpec as P

D = 768
H = 12
HD = 64
ROT = 16


norm_eps = 1e-05


def layer_norm(values, gain, shift):
    centre = values - jnp.mean(values, axis=-1, keepdims=True)
    spread = jnp.mean(centre * centre, axis=-1, keepdims=True)
    return centre * lax.rsqrt(spread + norm_eps) * gain + shift


def seq_positions(segments):
    row_index = jnp.arange(segments.shape[0], dtype=jnp.int32)
    before = jnp.sum((segments[:, None] > segments[None, :]).astype(jnp.int32), axis=1)
    return row_index - before


def rotate(heads_in, places):
    half = ROT // 2
    freqs = 1.0 / 10000.0 ** (jnp.arange(half, dtype=jnp.float32) * 2.0 / ROT)
    angles = places.astype(jnp.float32)[:, None] * freqs[None, :]
    cosine = jnp.cos(angles)[:, None, :]
    sine = jnp.sin(angles)[:, None, :]
    first = heads_in[..., :half]
    second = heads_in[..., half:ROT]
    return jnp.concatenate(
        [first * cosine - second * sine, second * cosine + first * sine, heads_in[..., ROT:]],
        axis=-1,
    )


def gelu_exact(values):
    return jax.nn.gelu(values, approximate=False)


def block_scores(query_b, key_b, segments, first_row, block_rows, score_scale):
    q_block = query_b[first_row : first_row + block_rows]
    raw_scores = (
        jnp.einsum("qhd,khd->hqk", q_block, key_b, preferred_element_type=jnp.float32) * score_scale
    )
    row_index = jnp.arange(segments.shape[0], dtype=jnp.int32)
    rows_here = row_index[first_row : first_row + block_rows]
    seg_here = segments[first_row : first_row + block_rows]
    allowed = (seg_here[:, None] == segments[None, :]) & (row_index[None, :] <= rows_here[:, None])
    return (jnp.where(allowed[None], raw_scores, -1e30), q_block)


def plane_bits(rep_size):
    bits, b = [], 1
    while b < rep_size:
        bits.append(b)
        b *= 2
    return bits


def swap(value, axis, bit):
    size = lax.axis_size(axis)
    return lax.ppermute(value, axis, [(i, i ^ bit) for i in range(size)])


def place_ids():
    rep = lax.axis_index("rep")
    return lax.axis_index("shard"), (rep // 2) % 4, rep % 2


def gather_start(shard):
    rows, cols = shard.shape
    z, q, c = place_ids()
    piece = lax.dynamic_slice(shard, (q * (rows // 4), c * (cols // 2)), (rows // 4, cols // 2))
    far = jnp.stack([swap(piece, "shard", k) for k in (1, 2, 3)])
    parts = [far] + [swap(far, "rep", j * 2) for j in (1, 2, 3)]
    other = [swap(p, "rep", 1) for p in parts]
    return parts + other


def assemble_body(rows, cols, ids_ref, shard_ref, *refs):
    pieces, out_ref, sem = refs[:8], refs[8], refs[9]
    z, q, c = ids_ref[0], ids_ref[1], ids_ref[2]
    part = rows // 4
    half = cols // 2
    copies = [
        pltpu.make_async_copy(
            shard_ref, out_ref.at[pl.ds(pl.multiple_of(z * rows, rows), rows)], sem
        )
    ]
    for index in range(8):
        j, h = index % 4, index // 4
        col = pl.multiple_of((c ^ h) * half, half)
        for k in (1, 2, 3):
            row = pl.multiple_of((z ^ k) * rows + (q ^ j) * part, part)
            copies.append(
                pltpu.make_async_copy(
                    pieces[index].at[k - 1],
                    out_ref.at[pl.ds(row, part), pl.ds(col, half)],
                    sem,
                )
            )
    for copy in copies:
        copy.start()
    for copy in copies:
        copy.wait()


def assemble(ids, shard, pieces):
    rows, cols = shard.shape
    anywhere = pl.BlockSpec(memory_space=pl.ANY)
    return pl.pallas_call(
        functools.partial(assemble_body, rows, cols),
        out_shape=jax.ShapeDtypeStruct((4 * rows, cols), shard.dtype),
        in_specs=[pl.BlockSpec(memory_space=pltpu.SMEM)] + [anywhere] * 9,
        out_specs=anywhere,
        scratch_shapes=[pltpu.SemaphoreType.DMA],
        name="assemble",
    )(ids, shard, *pieces)


def pair(left, right):
    return left.astype(jnp.float32) + right.astype(jnp.float32)


def reduce_rows(grad):
    total_rows, cols = grad.shape
    rows = total_rows // 4
    z, q, c = place_ids()
    y_bit, x_bit = q // 2, q % 2
    half = cols // 2
    send = lax.dynamic_slice(grad, (0, (1 - c) * half), (total_rows, half))
    keep = lax.dynamic_slice(grad, (0, c * half), (total_rows, half))
    got = swap(send, "rep", 1)
    one = pair(keep, got).astype(jnp.bfloat16).reshape(4, 2, 2, rows // 4, half)

    def halves(block, bit, axis):
        mine = lax.dynamic_index_in_dim(block, bit, axis, keepdims=False)
        theirs = lax.dynamic_index_in_dim(block, 1 - bit, axis, keepdims=False)
        return mine, theirs

    low, high = one[:2], one[2:]
    low_mine, low_theirs = halves(low, x_bit, 2)
    high_mine, high_theirs = halves(high, y_bit, 1)
    low = pair(low_mine, swap(low_theirs, "rep", 2)).astype(jnp.bfloat16)
    high = pair(high_mine, swap(high_theirs, "rep", 4)).astype(jnp.bfloat16)
    low_mine, low_theirs = halves(low, y_bit, 1)
    high_mine, high_theirs = halves(high, x_bit, 1)
    low_got = swap(low_theirs, "rep", 4)
    high_got = swap(high_theirs, "rep", 2)
    two = jnp.concatenate([pair(low_mine, low_got), pair(high_mine, high_got)]).astype(
        jnp.bfloat16
    )
    pieces = [lax.dynamic_index_in_dim(two, z ^ k, 0, keepdims=False) for k in range(4)]
    got = [swap(pieces[k], "shard", k) for k in (1, 2, 3)]
    three = (pair(pieces[0], got[0]) + pair(got[1], got[2])).astype(jnp.bfloat16)
    for bit in plane_bits(lax.axis_size("rep"))[3:]:
        three = pair(three, swap(three, "rep", bit)).astype(jnp.bfloat16)
    parts = [three] + [swap(three, "rep", j * 2) for j in (1, 2, 3)]
    other = [swap(p, "rep", 1) for p in parts]
    return parts + other


def place_body(part, half, ids_ref, *refs):
    pieces, out_ref = refs[:8], refs[8]
    q, c = ids_ref[1], ids_ref[2]
    for index in range(8):
        j, h = index % 4, index // 4
        row = pl.multiple_of((q ^ j) * part, part)
        col = pl.multiple_of((c ^ h) * half, half)
        out_ref[pl.ds(row, part), pl.ds(col, half)] = pieces[index][...].astype(jnp.float32)


def place(ids, pieces):
    part, half = pieces[0].shape
    vmem = pl.BlockSpec(memory_space=pltpu.VMEM)
    return pl.pallas_call(
        functools.partial(place_body, part, half),
        out_shape=jax.ShapeDtypeStruct((4 * part, 2 * half), jnp.float32),
        in_specs=[pl.BlockSpec(memory_space=pltpu.SMEM)] + [vmem] * 8,
        out_specs=vmem,
        compiler_params=pltpu.CompilerParams(vmem_limit_bytes=32 * 2**20),
        name="place",
    )(ids, *pieces)


def sum_small(vector):
    for bit in plane_bits(lax.axis_size("rep")):
        if bit in (2, 4):
            continue
        vector = vector + swap(vector, "rep", bit)
    vector = (vector + swap(vector, "rep", 2)) + (swap(vector, "rep", 4) + swap(vector, "rep", 6))
    return (vector + swap(vector, "shard", 1)) + (swap(vector, "shard", 2) + swap(vector, "shard", 3))


def pack(vectors):
    flat = jnp.concatenate([v.reshape(-1) for v in vectors])
    fill = -flat.shape[0] % 1024
    return jnp.concatenate([flat, jnp.zeros((fill,), flat.dtype)]).reshape(-1, 128)


def gather_small(vectors):
    packed = pack(vectors)
    z = lax.axis_index("shard")
    near = jnp.stack([packed] + [swap(packed, "shard", k) for k in (1, 2, 3)])
    rows = jnp.stack(
        [lax.dynamic_index_in_dim(near, z ^ i, 0, keepdims=False) for i in range(4)]
    ).reshape(4, -1)
    out, at = [], 0
    for v in vectors:
        out.append(rows[:, at : at + v.shape[0]].reshape(-1).astype(jnp.float32))
        at += v.shape[0]
    return out


def body(
    hidden_in,
    cotangent,
    seg_ids,
    first_gain,
    first_shift,
    second_gain,
    second_shift,
    qkv_weight,
    qkv_bias,
    out_weight,
    out_bias,
    up_weight,
    up_bias,
    down_weight,
    down_bias,
):
    ids = jnp.stack(place_ids()).astype(jnp.int32)
    small = gather_small(
        [first_gain, first_shift, second_gain, second_shift, qkv_bias, out_bias, up_bias, down_bias]
    )
    qkv_full = assemble(ids, qkv_weight, gather_start(qkv_weight))
    out_full = assemble(ids, out_weight, gather_start(out_weight))
    up_full = assemble(ids, up_weight, gather_start(up_weight))
    down_full = assemble(ids, down_weight, gather_start(down_weight))
    gathered = (
        small[0],
        small[1],
        small[2],
        small[3],
        qkv_full,
        small[4],
        out_full,
        small[5],
        up_full,
        small[6],
        down_full,
        small[7],
    )
    tokens_here = hidden_in.shape[0]
    score_scale = HD ** (-0.5)
    block_rows = min(512, tokens_here)
    places = seq_positions(seg_ids)
    first_normed, pull_first = jax.vjp(
        layer_norm, hidden_in, gathered[0].astype(jnp.float32), gathered[1].astype(jnp.float32)
    )
    first_b = first_normed.astype(jnp.bfloat16)
    qkv = jnp.dot(first_b, gathered[4], preferred_element_type=jnp.float32) + gathered[5].astype(
        jnp.float32
    )
    qkv = qkv.reshape(tokens_here, 3, H, HD)

    def rotate_pair(query_in, key_in):
        return (rotate(query_in, places), rotate(key_in, places))

    rotated, pull_rotate = jax.vjp(rotate_pair, qkv[:, 0], qkv[:, 1])
    query_b = rotated[0].astype(jnp.bfloat16)
    key_b = rotated[1].astype(jnp.bfloat16)
    value_b = qkv[:, 2].astype(jnp.bfloat16)
    mixed_parts = []
    logsum_parts = []
    for first_row in range(0, tokens_here, block_rows):
        masked, q_block = block_scores(query_b, key_b, seg_ids, first_row, block_rows, score_scale)
        highest_score = jnp.max(masked, axis=-1, keepdims=True)
        expo_scores = jnp.exp(masked - highest_score)
        total = jnp.sum(expo_scores, axis=-1, keepdims=True)
        probs = expo_scores / total
        logsum_parts.append(highest_score + jnp.log(total))
        mixed_parts.append(
            jnp.einsum(
                "hqk,khd->qhd",
                probs.astype(jnp.bfloat16),
                value_b,
                preferred_element_type=jnp.float32,
            )
        )
    mixed_b = jnp.concatenate(mixed_parts, axis=0).astype(jnp.bfloat16).reshape(tokens_here, D)
    attn_out = jnp.dot(mixed_b, gathered[6], preferred_element_type=jnp.float32) + gathered[
        7
    ].astype(jnp.float32)
    second_normed, pull_second = jax.vjp(
        layer_norm, hidden_in, gathered[2].astype(jnp.float32), gathered[3].astype(jnp.float32)
    )
    second_b = second_normed.astype(jnp.bfloat16)
    up_vals = jnp.dot(second_b, gathered[8], preferred_element_type=jnp.float32) + gathered[
        9
    ].astype(jnp.float32)
    act_vals, pull_gelu = jax.vjp(gelu_exact, up_vals)
    act_b = act_vals.astype(jnp.bfloat16)
    mlp_out = jnp.dot(act_b, gathered[10], preferred_element_type=jnp.float32) + gathered[
        11
    ].astype(jnp.float32)
    output = hidden_in + attn_out + mlp_out
    back_weights = gathered
    cot_b = cotangent.astype(jnp.bfloat16)
    bias_out_g = jnp.sum(cotangent, axis=0)
    out_weight_g = jnp.einsum("td,te->de", mixed_b, cot_b, preferred_element_type=jnp.float32)
    down_weight_g = jnp.einsum("tf,te->fe", act_b, cot_b, preferred_element_type=jnp.float32)
    act_grad = jnp.einsum("te,fe->tf", cot_b, back_weights[10], preferred_element_type=jnp.float32)
    up_grad_b = pull_gelu(act_grad)[0].astype(jnp.bfloat16)
    up_bias_g = jnp.sum(up_grad_b.astype(jnp.float32), axis=0)
    up_weight_g = jnp.einsum("td,tf->df", second_b, up_grad_b, preferred_element_type=jnp.float32)
    second_in_grad = jnp.einsum(
        "tf,df->td", up_grad_b, back_weights[8], preferred_element_type=jnp.float32
    )
    second_x_grad, second_gain_g, second_shift_g = pull_second(second_in_grad)
    mixed_grad_b = (
        jnp.einsum("te,de->td", cot_b, back_weights[6], preferred_element_type=jnp.float32)
        .astype(jnp.bfloat16)
        .reshape(tokens_here, H, HD)
    )
    query_parts = []
    key_grad = jnp.zeros((tokens_here, H, HD), jnp.float32)
    value_grad = jnp.zeros((tokens_here, H, HD), jnp.float32)
    for block_number, first_row in enumerate(range(0, tokens_here, block_rows)):
        masked, q_block = block_scores(query_b, key_b, seg_ids, first_row, block_rows, score_scale)
        probs = jnp.exp(masked - logsum_parts[block_number])
        grad_block = mixed_grad_b[first_row : first_row + block_rows]
        probs_grad = jnp.einsum(
            "qhd,khd->hqk", grad_block, value_b, preferred_element_type=jnp.float32
        )
        value_grad = value_grad + jnp.einsum(
            "hqk,qhd->khd",
            probs.astype(jnp.bfloat16),
            grad_block,
            preferred_element_type=jnp.float32,
        )
        scores_grad = (
            probs * (probs_grad - jnp.sum(probs_grad * probs, axis=-1, keepdims=True))
        ).astype(jnp.bfloat16)
        query_parts.append(
            jnp.einsum("hqk,khd->qhd", scores_grad, key_b, preferred_element_type=jnp.float32)
            * score_scale
        )
        key_grad = (
            key_grad
            + jnp.einsum("hqk,qhd->khd", scores_grad, q_block, preferred_element_type=jnp.float32)
            * score_scale
        )
    query_grad = jnp.concatenate(query_parts, axis=0)
    query_in_grad, key_in_grad = pull_rotate((query_grad, key_grad))
    qkv_grad_b = (
        jnp.stack([query_in_grad, key_in_grad, value_grad], axis=1)
        .reshape(tokens_here, 3 * D)
        .astype(jnp.bfloat16)
    )
    qkv_bias_g = jnp.sum(qkv_grad_b.astype(jnp.float32), axis=0)
    qkv_weight_g = jnp.einsum("td,te->de", first_b, qkv_grad_b, preferred_element_type=jnp.float32)
    first_in_grad = jnp.einsum(
        "te,de->td", qkv_grad_b, back_weights[4], preferred_element_type=jnp.float32
    )
    first_x_grad, first_gain_g, first_shift_g = pull_first(first_in_grad)
    input_grad = cotangent + first_x_grad + second_x_grad
    small_sum = sum_small(
        pack(
            [
                first_gain_g,
                first_shift_g,
                second_gain_g,
                second_shift_g,
                qkv_bias_g,
                bias_out_g,
                up_bias_g,
            ]
        )
    ).reshape(-1)
    z = lax.axis_index("shard")
    summed, at = [], 0
    for size in (D, D, D, D, 3 * D, D, up_bias_g.shape[0]):
        summed.append(lax.dynamic_slice(small_sum, (at + z * (size // 4),), (size // 4,)))
        at += size
    weight_sums = [
        place(ids, reduce_rows(g.astype(jnp.bfloat16)))
        for g in (qkv_weight_g, out_weight_g, up_weight_g, down_weight_g)
    ]
    return (
        output,
        input_grad,
        summed[0],
        summed[1],
        summed[2],
        summed[3],
        weight_sums[0],
        summed[4],
        weight_sums[1],
        summed[5],
        weight_sums[2],
        summed[6],
        weight_sums[3],
        summed[5],
    )


def solution(mesh):
    in_specs = (
        P(("rep", "shard"), None),
        P(("rep", "shard"), None),
        P(("rep", "shard")),
        P("shard"),
        P("shard"),
        P("shard"),
        P("shard"),
        P("shard", None),
        P("shard"),
        P("shard", None),
        P("shard"),
        P("shard", None),
        P("shard"),
        P("shard", None),
        P("shard"),
    )
    out_specs = (
        P(("rep", "shard"), None),
        P(("rep", "shard"), None),
        P("shard"),
        P("shard"),
        P("shard"),
        P("shard"),
        P("shard", None),
        P("shard"),
        P("shard", None),
        P("shard"),
        P("shard", None),
        P("shard"),
        P("shard", None),
        P("shard"),
    )
    return jax.shard_map(body, mesh=mesh, in_specs=in_specs, out_specs=out_specs, check_vma=False)
```

```python
import functools

import jax
import jax.numpy as jnp
from jax import lax
from jax.experimental import pallas as pl
from jax.experimental.pallas import tpu as pltpu
from jax.sharding import PartitionSpec as P

D = 768
H = 12
HD = 64
ROT = 16
WIDE = 384
LANES = 128
F32, BF16 = jnp.float32, jnp.bfloat16
norm_eps = 1e-05


def compiler_params(mib):
    return pltpu.CompilerParams(vmem_limit_bytes=mib * 2**20)


VMEM = pl.BlockSpec(memory_space=pltpu.VMEM)
SMEM = pl.BlockSpec(memory_space=pltpu.SMEM)


def swap(value, axis, bit):
    size = lax.axis_size(axis)
    return lax.ppermute(value, axis, [(i, i ^ bit) for i in range(size)])


def place_ids():
    rep = lax.axis_index("rep")
    return lax.axis_index("shard"), (rep // 2) % 4, rep % 2


def gather_far(piece):
    return jnp.stack([swap(piece, "shard", k) for k in (1, 2, 3)])


def gather_near(far):
    parts = jnp.stack([far] + [swap(far, "rep", j * 2) for j in (1, 2, 3)])
    return parts, swap(parts, "rep", 1)


def pair(left, right):
    return left.astype(F32) + right.astype(F32)


def reduce_pack(send, keep):
    z, q, c = place_ids()
    y_bit, x_bit = q // 2, q % 2
    rows = keep.shape[2]
    got = swap(send, "rep", 1)
    one = pair(keep, got).astype(BF16).reshape(4, 2, 2, rows, WIDE)

    def halves(block, bit, axis):
        mine = lax.dynamic_index_in_dim(block, bit, axis, keepdims=False)
        theirs = lax.dynamic_index_in_dim(block, 1 - bit, axis, keepdims=False)
        return mine, theirs

    low_mine, low_theirs = halves(one[:2], x_bit, 2)
    high_mine, high_theirs = halves(one[2:], y_bit, 1)
    low = pair(low_mine, swap(low_theirs, "rep", 2)).astype(BF16)
    high = pair(high_mine, swap(high_theirs, "rep", 4)).astype(BF16)
    low_mine, low_theirs = halves(low, y_bit, 1)
    high_mine, high_theirs = halves(high, x_bit, 1)
    low_got = swap(low_theirs, "rep", 4)
    high_got = swap(high_theirs, "rep", 2)
    two = jnp.concatenate([pair(low_mine, low_got), pair(high_mine, high_got)]).astype(BF16)
    pieces = [lax.dynamic_index_in_dim(two, z ^ k, 0, keepdims=False) for k in range(4)]
    got = [swap(pieces[k], "shard", k) for k in (1, 2, 3)]
    three = (pair(pieces[0], got[0]) + pair(got[1], got[2])).astype(BF16)
    bit = 8
    while bit < lax.axis_size("rep"):
        three = pair(three, swap(three, "rep", bit)).astype(BF16)
        bit *= 2
    parts = jnp.stack([three] + [swap(three, "rep", j * 2) for j in (1, 2, 3)])
    return parts, swap(parts, "rep", 1)


def sum_small(vector):
    bit = 1
    while bit < lax.axis_size("rep"):
        if bit not in (2, 4):
            vector = vector + swap(vector, "rep", bit)
        bit *= 2
    vector = (vector + swap(vector, "rep", 2)) + (swap(vector, "rep", 4) + swap(vector, "rep", 6))
    return (vector + swap(vector, "shard", 1)) + (swap(vector, "shard", 2) + swap(vector, "shard", 3))


def pack(vectors):
    flat = jnp.concatenate([v.reshape(-1) for v in vectors])
    fill = -flat.shape[0] % 1024
    return jnp.concatenate([flat, jnp.zeros((fill,), flat.dtype)]).reshape(-1, LANES)


def gather_small(vectors):
    packed = pack(vectors)
    z = lax.axis_index("shard")
    near = jnp.stack([packed] + [swap(packed, "shard", k) for k in (1, 2, 3)])
    rows = jnp.stack(
        [lax.dynamic_index_in_dim(near, z ^ i, 0, keepdims=False) for i in range(4)]
    ).reshape(4, -1)
    out, at = [], 0
    for v in vectors:
        out.append(rows[:, at : at + v.shape[0]].reshape(-1).astype(F32))
        at += v.shape[0]
    return out


def assemble_body(plan, ids_ref, *refs):
    count = len(plan)
    shards, (parts_ref, other_ref), outs = refs[:count], refs[count : count + 2], refs[count + 2 :]
    z, q, c = ids_ref[0], ids_ref[1], ids_ref[2]
    for shard_ref, out_ref, (rows, part, first, blocks) in zip(shards, outs, plan):
        half = blocks * WIDE
        out_ref[pl.ds(pl.multiple_of(z * rows, rows), rows), :] = shard_ref[...]
        for h, pieces in ((c, parts_ref), (1 - c, other_ref)):
            for j in range(4):
                for k in (1, 2, 3):
                    row = pl.multiple_of((z ^ k) * rows + (q ^ j) * part, part)
                    for b in range(blocks):
                        col = pl.multiple_of(h * half + b * WIDE, WIDE)
                        at = first + b * part
                        out_ref[pl.ds(row, part), pl.ds(col, WIDE)] = pieces[j, k - 1, at : at + part, :]


def assemble(ids, shards, plan, parts, other):
    shapes = [
        jax.ShapeDtypeStruct((4 * rows, 2 * blocks * WIDE), BF16) for rows, _, _, blocks in plan
    ]
    return pl.pallas_call(
        functools.partial(assemble_body, plan),
        out_shape=shapes,
        in_specs=[SMEM] + [VMEM] * (len(shards) + 2),
        out_specs=[VMEM] * len(shards),
        compiler_params=compiler_params(40),
        name="assemble",
    )(ids, *shards, parts, other)


def place_body(plan, ids_ref, parts_ref, other_ref, *outs):
    q, c = ids_ref[1], ids_ref[2]
    for out_ref, (rows, part, first, blocks) in zip(outs, plan):
        half = blocks * WIDE
        for h, pieces in ((c, parts_ref), (1 - c, other_ref)):
            for j in range(4):
                row = pl.multiple_of((q ^ j) * part, part)
                for b in range(blocks):
                    col = pl.multiple_of(h * half + b * WIDE, WIDE)
                    at = first + b * part
                    out_ref[pl.ds(row, part), pl.ds(col, WIDE)] = pieces[j, at : at + part, :].astype(F32)


def place(ids, plan, parts, other):
    shapes = [jax.ShapeDtypeStruct((rows, 2 * blocks * WIDE), F32) for rows, _, _, blocks in plan]
    return pl.pallas_call(
        functools.partial(place_body, plan),
        out_shape=shapes,
        in_specs=[SMEM, VMEM, VMEM],
        out_specs=[VMEM] * len(plan),
        compiler_params=compiler_params(40),
        name="place",
    )(ids, parts, other)


def dot(left, right, left_dim=1, right_dim=0):
    return lax.dot_general(
        left, right, (((left_dim,), (right_dim,)), ((), ())), preferred_element_type=F32
    )


def turn(values, cosine, early, late):
    width = values.shape[1]
    return (
        values * cosine
        + pltpu.roll(values, width - ROT // 2, 1) * early
        + pltpu.roll(values, ROT // 2, 1) * late
    )


def qkv_body(x_ref, w_ref, bias_ref, cos_ref, early_ref, late_ref, out_ref):
    values = dot(x_ref[...], w_ref[...]) + bias_ref[...]

    @pl.when(pl.program_id(0) < 4)
    def rotate_block():
        for b in range(WIDE // LANES):
            cols = slice(b * LANES, (b + 1) * LANES)
            out_ref[:, cols] = turn(
                values[:, cols], cos_ref[...], early_ref[...], late_ref[...]
            ).astype(BF16)

    @pl.when(pl.program_id(0) >= 4)
    def plain_block():
        out_ref[...] = values.astype(BF16)


def qkv_call(first_b, weight, bias, tables):
    tokens = first_b.shape[0]
    whole = lambda r, c: pl.BlockSpec((r, c), lambda i: (0, 0))
    return pl.pallas_call(
        qkv_body,
        grid=(3 * D // WIDE,),
        out_shape=jax.ShapeDtypeStruct((tokens, 3 * D), BF16),
        in_specs=[
            whole(tokens, D),
            pl.BlockSpec((D, WIDE), lambda i: (0, i)),
            pl.BlockSpec((1, WIDE), lambda i: (0, i)),
        ]
        + [whole(tokens, LANES)] * 3,
        out_specs=pl.BlockSpec((tokens, WIDE), lambda i: (0, i)),
        compiler_params=compiler_params(40),
        name="qkv",
    )(first_b, weight, bias, *tables)


def attention_body(
    q_ref, k_ref, v_ref, cot_ref, w_ref, seg_col_ref, seg_row_ref, cos_ref, early_ref, late_ref,
    mixed_ref, grad_ref, mask_ref, key_t_ref, value_t_ref,
):
    tokens = q_ref.shape[0]
    step = min(256, tokens)

    @pl.when(pl.program_id(0) == 0)
    def make_mask():
        for first in range(0, tokens, step):
            rows = first + lax.broadcasted_iota(jnp.int32, (step, tokens), 0)
            cols = lax.broadcasted_iota(jnp.int32, (step, tokens), 1)
            same = seg_col_ref[first : first + step, :] == seg_row_ref[...]
            mask_ref[first : first + step, :] = jnp.where(same & (cols <= rows), 0.0, -1e30)

    out_grad = dot(cot_ref[...], w_ref[...], 1, 1).astype(BF16)
    lane = lax.broadcasted_iota(jnp.int32, (tokens, LANES), 1)
    query_t = q_ref[...].astype(F32).T.astype(BF16)
    out_grad_t = out_grad.astype(F32).T.astype(BF16)
    nothing = jnp.zeros((tokens, LANES), BF16)
    keys = k_ref[...] * BF16(HD**-0.5)
    heads = []
    for h in range(2):
        here = (lane // HD) == h
        heads.append((jnp.where(here, keys, nothing), jnp.where(here, v_ref[...], nothing)))
    key_t_ref[...] = jnp.zeros_like(key_t_ref)
    value_t_ref[...] = jnp.zeros_like(value_t_ref)
    for first in range(0, tokens, step):
        last = first + step
        block = slice(first, last)
        mixed = jnp.zeros((step, LANES), F32)
        query_grad = jnp.zeros((step, LANES), F32)
        for h in range(2):
            key, value = heads[h][0][:last], heads[h][1][:last]
            rows = slice(h * HD, (h + 1) * HD)
            scores = dot(q_ref[block, :], key, 1, 1) + mask_ref[block, :last]
            expo = jnp.exp(scores - jnp.max(scores, axis=1, keepdims=True))
            probs = expo * (1.0 / jnp.sum(expo, axis=1, keepdims=True))
            probs_b = probs.astype(BF16)
            mixed += dot(probs_b, value)
            probs_grad = dot(out_grad[block], value, 1, 1)
            weighted = probs_grad * probs
            scores_grad = (weighted - probs * jnp.sum(weighted, axis=1, keepdims=True)).astype(BF16)
            query_grad += dot(scores_grad, key)
            key_t_ref[rows, :last] += dot(query_t[rows, block], scores_grad)
            value_t_ref[rows, :last] += dot(out_grad_t[rows, block], probs_b)
        mixed_ref[block, :] = mixed.astype(BF16)
        grad_ref[0, block, :] = turn(
            query_grad, cos_ref[block, :], -early_ref[block, :], -late_ref[block, :]
        ).astype(BF16)
    grad_ref[1, :, :] = turn(
        key_t_ref[...].T * HD**-0.5, cos_ref[...], -early_ref[...], -late_ref[...]
    ).astype(BF16)
    grad_ref[2, :, :] = value_t_ref[...].T.astype(BF16)


def attention_call(qkv_b, cot_b, out_weight, segments, tables):
    tokens = qkv_b.shape[0]
    pairs = D // LANES
    whole = lambda r, c: pl.BlockSpec((r, c), lambda i: (0, 0))
    part = lambda n: pl.BlockSpec((tokens, LANES), lambda i: (0, n * pairs + i))
    return pl.pallas_call(
        attention_body,
        grid=(pairs,),
        out_shape=[
            jax.ShapeDtypeStruct((tokens, D), BF16),
            jax.ShapeDtypeStruct((3, tokens, D), BF16),
        ],
        in_specs=[
            part(0),
            part(1),
            part(2),
            whole(tokens, D),
            pl.BlockSpec((LANES, D), lambda i: (i, 0)),
            whole(tokens, 1),
            whole(1, tokens),
        ]
        + [whole(tokens, LANES)] * 3,
        out_specs=[
            pl.BlockSpec((tokens, LANES), lambda i: (0, i)),
            pl.BlockSpec((3, tokens, LANES), lambda i: (0, 0, i)),
        ],
        scratch_shapes=[
            pltpu.VMEM((tokens, tokens), F32),
            pltpu.VMEM((LANES, tokens), F32),
            pltpu.VMEM((LANES, tokens), F32),
        ],
        compiler_params=compiler_params(56),
        name="attention",
    )(
        qkv_b, qkv_b, qkv_b, cot_b, out_weight, segments[:, None], segments[None, :], *tables
    )


def qkv_grad_body(grad_ref, first_t_ref, w_ref, mixed_ref, cot_ref, pack_ref, bias_ref, in_ref):
    step = pl.program_id(0)
    grad = grad_ref[0]
    h, b = step // 3, step % 3
    block = dot(first_t_ref[...], grad).astype(BF16).reshape(4, 4, D // 16, WIDE)
    pack_ref[h, :, :, pl.ds(pl.multiple_of(b * (D // 16), D // 16), D // 16), :] = block
    bias_ref[...] = jnp.sum(grad.astype(F32), axis=0, keepdims=True)
    back = dot(grad, w_ref[...], 1, 1)

    @pl.when(step == 0)
    def first_step():
        in_ref[...] = back

    @pl.when(step > 0)
    def later_step():
        in_ref[...] += back

    @pl.when(b == 0)
    def out_part():
        block = dot(mixed_ref[...], cot_ref[...], 0, 0).astype(BF16)
        pack_ref[h, :, :, 3 * (D // 16) :, :] = block.reshape(4, 4, D // 16, WIDE)


def qkv_grad_call(grads, first_t, weight, mixed_b, cot_b):
    tokens = cot_b.shape[0]
    whole = lambda r, c: pl.BlockSpec((r, c), lambda i: (0, 0))
    return pl.pallas_call(
        qkv_grad_body,
        grid=(3 * D // WIDE,),
        out_shape=[
            jax.ShapeDtypeStruct((2, 4, 4, D // 4, WIDE), BF16),
            jax.ShapeDtypeStruct((1, 3 * D), F32),
            jax.ShapeDtypeStruct((tokens, D), F32),
        ],
        in_specs=[
            pl.BlockSpec((1, tokens, WIDE), lambda i: (i // 2, 0, i % 2)),
            whole(D, tokens),
            pl.BlockSpec((D, WIDE), lambda i: (0, i)),
            whole(tokens, D),
            pl.BlockSpec((tokens, WIDE), lambda i: (0, i // 3)),
        ],
        out_specs=[
            pl.BlockSpec((2, 4, 4, D // 4, WIDE), lambda i: (0, 0, 0, 0, 0)),
            pl.BlockSpec((1, WIDE), lambda i: (0, i)),
            whole(tokens, D),
        ],
        compiler_params=compiler_params(56),
        name="qkv_grad",
    )(grads, first_t, weight, mixed_b, cot_b)


def mlp_body(x_ref, x_t_ref, cot_ref, up_ref, down_ref, bias_ref, out_in_ref, back_in_ref, out_ref, back_ref, pack_ref, bias_grad_ref, act_ref, grad_ref):
    step = pl.program_id(0)
    tokens = x_ref.shape[0]
    rows = min(256, tokens)
    total = jnp.zeros((1, WIDE), F32)

    @pl.when(step == 0)
    def first_step():
        out_ref[...] = out_in_ref[...]
        back_ref[...] = back_in_ref[...]

    for first in range(0, tokens, rows):
        block = slice(first, first + rows)
        up = dot(x_ref[block, :], up_ref[...]) + bias_ref[...]
        act_grad = dot(cot_ref[block, :], down_ref[...], 1, 1)
        below = 0.5 + 0.5 * lax.erf(up * (0.5**0.5))
        act = (up * below).astype(BF16)
        slope = below + up * (jnp.exp(-0.5 * up * up) * 0.3989422804014327)
        up_grad = (act_grad * slope).astype(BF16)
        act_ref[block, :] = act
        grad_ref[block, :] = up_grad
        out_ref[block, :] += dot(act, down_ref[...])
        back_ref[block, :] += dot(up_grad, up_ref[...], 1, 1)
        total += jnp.sum(up_grad.astype(F32), axis=0, keepdims=True)
    bias_grad_ref[...] = total
    part = D // 16
    block = dot(x_t_ref[...], grad_ref[...]).astype(BF16).reshape(4, 4, part, WIDE)
    pack_ref[step // 2, :, :, pl.ds(pl.multiple_of((step % 2) * part, part), part), :] = block
    down = dot(act_ref[...], cot_ref[...], 0, 0).astype(BF16)
    for h in range(2):
        pack_ref[h, step, :, 2 * part :, :] = down[:, h * WIDE : (h + 1) * WIDE].reshape(
            4, WIDE // 4, WIDE
        )


def mlp_call(second_b, second_t, cot_b, up_weight, down_weight, bias, out_in, back_in):
    tokens = cot_b.shape[0]
    whole = lambda r, c: pl.BlockSpec((r, c), lambda i: (0, 0))
    return pl.pallas_call(
        mlp_body,
        grid=(4,),
        out_shape=[
            jax.ShapeDtypeStruct((tokens, D), F32),
            jax.ShapeDtypeStruct((tokens, D), F32),
            jax.ShapeDtypeStruct((2, 4, 4, D // 4, WIDE), BF16),
            jax.ShapeDtypeStruct((1, 4 * WIDE), F32),
        ],
        in_specs=[
            whole(tokens, D),
            whole(D, tokens),
            whole(tokens, D),
            pl.BlockSpec((D, WIDE), lambda i: (0, i)),
            pl.BlockSpec((WIDE, D), lambda i: (i, 0)),
            pl.BlockSpec((1, WIDE), lambda i: (0, i)),
            whole(tokens, D),
            whole(tokens, D),
        ],
        out_specs=[
            whole(tokens, D),
            whole(tokens, D),
            pl.BlockSpec((2, 4, 4, D // 4, WIDE), lambda i: (0, 0, 0, 0, 0)),
            pl.BlockSpec((1, WIDE), lambda i: (0, i)),
        ],
        scratch_shapes=[pltpu.VMEM((tokens, WIDE), BF16), pltpu.VMEM((tokens, WIDE), BF16)],
        input_output_aliases={6: 0, 7: 1},
        compiler_params=compiler_params(60),
        name="mlp",
    )(second_b, second_t, cot_b, up_weight, down_weight, bias, out_in, back_in)


def normalize(values):
    centre = values - jnp.mean(values, axis=-1, keepdims=True)
    scale = lax.rsqrt(jnp.mean(centre * centre, axis=-1, keepdims=True) + norm_eps)
    return centre * scale, scale


def norm_back(normed, scale, gain, grad):
    inner = grad * gain
    return scale * (
        inner
        - jnp.mean(inner, axis=-1, keepdims=True)
        - normed * jnp.mean(inner * normed, axis=-1, keepdims=True)
    )


def rotary_tables(segments):
    tokens = segments.shape[0]
    before = jnp.sum((segments[:, None] > segments[None, :]).astype(jnp.int32), axis=1)
    places = jnp.arange(tokens, dtype=jnp.int32) - before
    half = ROT // 2
    lane = jnp.arange(LANES, dtype=jnp.int32) % HD
    freqs = 1.0 / 10000.0 ** ((lane % half).astype(F32) * 2.0 / ROT)
    angles = places.astype(F32)[:, None] * freqs[None, :]
    cosine, sine = jnp.cos(angles), jnp.sin(angles)
    turned, early = (lane < ROT)[None, :], (lane < half)[None, :]
    return (
        jnp.where(turned, cosine, 1.0),
        jnp.where(early, -sine, 0.0),
        jnp.where(turned & ~early, sine, 0.0),
    )


def take(array, row, col, rows, cols):
    return lax.dynamic_slice(array, (row, col), (rows, cols))


def body(
    hidden_in,
    cotangent,
    seg_ids,
    first_gain,
    first_shift,
    second_gain,
    second_shift,
    qkv_weight,
    qkv_bias,
    out_weight,
    out_bias,
    up_weight,
    up_bias,
    down_weight,
    down_bias,
):
    z, q, c = place_ids()
    ids = jnp.stack([z, q, c]).astype(jnp.int32)
    own = qkv_weight.shape[0]
    part = own // 4
    hidden_units = up_weight.shape[1]
    own_hidden = down_weight.shape[0]
    chunks = own_hidden // WIDE
    small = gather_small(
        [first_gain, first_shift, second_gain, second_shift, qkv_bias, out_bias, up_bias, down_bias]
    )
    gain_1, shift_1, gain_2, shift_2, qkv_b0, out_b0, up_b0, down_b0 = small

    attention_piece = jnp.concatenate(
        [take(qkv_weight, q * part, c * 3 * WIDE + b * WIDE, part, WIDE) for b in range(3)]
        + [take(out_weight, q * part, c * WIDE, part, WIDE)]
    )
    attention_plan = ((own, part, 0, 3), (own, part, 3 * part, 1))
    deep = WIDE // 4
    mlp_plan = ((own, part, 0, 2), (WIDE, deep, 2 * part, 1))
    far = gather_far(attention_piece)
    qkv_full, out_full = assemble(
        ids, (qkv_weight, out_weight), attention_plan, *gather_near(far)
    )
    mlp_weights = []
    for j in range(chunks):
        piece = jnp.concatenate(
            [take(up_weight, q * part, (2 * c + b) * own_hidden + j * WIDE, part, WIDE) for b in range(2)]
            + [take(down_weight, j * WIDE + q * deep, c * WIDE, deep, WIDE)]
        )
        piece, far = lax.optimization_barrier((piece, far))
        far = gather_far(piece)
        own_up = up_weight.reshape(own, 4, chunks, WIDE)[:, :, j].reshape(own, 4 * WIDE)
        own_down = down_weight[j * WIDE : (j + 1) * WIDE]
        mlp_weights.append(assemble(ids, (own_up, own_down), mlp_plan, *gather_near(far)))

    normed_1, scale = normalize(hidden_in)
    first_b = (normed_1 * gain_1 + shift_1).astype(BF16)
    second_b = (normed_1 * gain_2 + shift_2).astype(BF16)
    cot_b = cotangent.astype(BF16)
    column_sum = jnp.sum(cotangent, axis=0)
    tables = rotary_tables(seg_ids)

    qkv_b = qkv_call(first_b, qkv_full, qkv_b0[None, :], tables)
    mixed_b, grads = attention_call(qkv_b, cot_b, out_full, seg_ids, tables)
    packed, qkv_bias_g, first_in_grad = qkv_grad_call(grads, first_b.T, qkv_full, mixed_b, cot_b)

    def half_sums(packed):
        send = lax.dynamic_index_in_dim(packed, 1 - c, 0, keepdims=False)
        keep = lax.dynamic_index_in_dim(packed, c, 0, keepdims=False)
        return reduce_pack(send, keep)

    qkv_weight_g, out_weight_g = place(ids, attention_plan, *half_sums(packed))

    attention_out = jnp.dot(mixed_b, out_full, preferred_element_type=F32)
    output = hidden_in + (attention_out + out_b0) + down_b0
    second_in_grad = jnp.zeros(hidden_in.shape, F32)
    second_t = second_b.T
    up_parts, down_parts, bias_parts = [], [], []
    bias_blocks = up_b0.reshape(4, chunks, WIDE)
    for j in range(chunks):
        output, second_in_grad, packed, bias_g = mlp_call(
            second_b,
            second_t,
            cot_b,
            *mlp_weights[j],
            bias_blocks[:, j].reshape(1, 4 * WIDE),
            output,
            second_in_grad,
        )
        up_g, down_g = place(ids, mlp_plan, *half_sums(packed))
        up_parts.append(up_g.reshape(own, 4, WIDE))
        down_parts.append(down_g)
        bias_parts.append(bias_g.reshape(4, WIDE))
    up_weight_g = jnp.stack(up_parts, axis=2).reshape(own, hidden_units)
    down_weight_g = jnp.concatenate(down_parts)
    up_bias_g = jnp.stack(bias_parts, axis=1).reshape(-1)

    input_grad = (
        cotangent
        + norm_back(normed_1, scale, gain_1, first_in_grad)
        + norm_back(normed_1, scale, gain_2, second_in_grad)
    )
    sums = [
        jnp.sum(first_in_grad * normed_1, axis=0),
        jnp.sum(first_in_grad, axis=0),
        jnp.sum(second_in_grad * normed_1, axis=0),
        jnp.sum(second_in_grad, axis=0),
        qkv_bias_g.reshape(-1),
        column_sum,
        up_bias_g,
    ]
    total = sum_small(pack(sums)).reshape(-1)
    summed, at = [], 0
    for s in sums:
        size = s.shape[0] // 4
        summed.append(lax.dynamic_slice(total, (at + z * size,), (size,)))
        at += s.shape[0]
    return (
        output,
        input_grad,
        summed[0],
        summed[1],
        summed[2],
        summed[3],
        qkv_weight_g,
        summed[4],
        out_weight_g,
        summed[5],
        up_weight_g,
        summed[6],
        down_weight_g,
        summed[5],
    )


def solution(mesh):
    tokens = P(("rep", "shard"), None)
    matrix, vector = P("shard", None), P("shard")
    params = (vector,) * 4 + (matrix, vector) * 4
    in_specs = (tokens, tokens, P(("rep", "shard"))) + params
    out_specs = (tokens, tokens) + params
    return jax.shard_map(body, mesh=mesh, in_specs=in_specs, out_specs=out_specs, check_vma=False)
```

```python
import functools

import jax
import jax.numpy as jnp
from jax import lax
from jax.experimental import pallas as pl
from jax.experimental.pallas import tpu as pltpu
from jax.sharding import PartitionSpec as P

D = 768
H = 12
HD = 64
ROT = 16
WIDE = 384
LANES = 128
F32, BF16 = jnp.float32, jnp.bfloat16
norm_eps = 1e-05


def compiler_params(mib):
    return pltpu.CompilerParams(vmem_limit_bytes=mib * 2**20)


def cost(microseconds):
    return pl.CostEstimate(
        flops=int(microseconds * 1.1e9), bytes_accessed=int(microseconds * 1e5), transcendentals=0
    )


VMEM = pl.BlockSpec(memory_space=pltpu.VMEM)
SMEM = pl.BlockSpec(memory_space=pltpu.SMEM)


def swap(value, axis, bit):
    size = lax.axis_size(axis)
    return lax.ppermute(value, axis, [(i, i ^ bit) for i in range(size)])


def place_ids():
    rep = lax.axis_index("rep")
    return lax.axis_index("shard"), (rep // 2) % 4, rep % 2


def after(value, *others):
    return lax.optimization_barrier((value, *others))[0]


def gather_far(piece):
    return jnp.stack([swap(piece, "shard", k) for k in (1, 2, 3)])


def gather_near(far):
    parts = [far] + [swap(far, "rep", j * 2) for j in (1, 2, 3)]
    return parts + [swap(p, "rep", 1) for p in parts]


def total_of(arrays):
    return (
        (arrays[0].astype(F32) + arrays[1].astype(F32))
        + (arrays[2].astype(F32) + arrays[3].astype(F32))
    ).astype(BF16)


def at(block, index):
    return lax.dynamic_index_in_dim(block, index, 0, keepdims=False)


def plane_sends(keep, got, q):
    return [(at(keep, q ^ j).astype(F32) + at(got, q ^ j).astype(F32)).astype(BF16) for j in range(4)]


def plane_swap(sends):
    return [sends[0]] + [swap(sends[j], "rep", j * 2) for j in (1, 2, 3)]


def shard_sends(groups, z):
    return [
        jnp.concatenate([total_of([at(term, z ^ k) for term in terms]) for terms in groups])
        for k in range(4)
    ]


def shard_sum(sends):
    owned = total_of([sends[0]] + [swap(sends[k], "shard", k) for k in (1, 2, 3)])
    bit = 8
    while bit < lax.axis_size("rep"):
        owned = (owned.astype(F32) + swap(owned, "rep", bit).astype(F32)).astype(BF16)
        bit *= 2
    return owned


def share_plane(owned):
    return jnp.stack([owned] + [swap(owned, "rep", j * 2) for j in (1, 2, 3)])


def sum_small(vector):
    bit = 1
    while bit < lax.axis_size("rep"):
        if bit not in (2, 4):
            vector = vector + swap(vector, "rep", bit)
        bit *= 2
    vector = (vector + swap(vector, "rep", 2)) + (swap(vector, "rep", 4) + swap(vector, "rep", 6))
    return (vector + swap(vector, "shard", 1)) + (swap(vector, "shard", 2) + swap(vector, "shard", 3))


def pack(vectors):
    flat = jnp.concatenate([v.reshape(-1) for v in vectors])
    fill = -flat.shape[0] % 1024
    return jnp.concatenate([flat, jnp.zeros((fill,), flat.dtype)]).reshape(-1, LANES)


def gather_small(vectors):
    packed = pack(vectors)
    z = lax.axis_index("shard")
    near = jnp.stack([packed] + [swap(packed, "shard", k) for k in (1, 2, 3)])
    rows = jnp.stack(
        [lax.dynamic_index_in_dim(near, z ^ i, 0, keepdims=False) for i in range(4)]
    ).reshape(4, -1)
    out, at = [], 0
    for v in vectors:
        out.append(rows[:, at : at + v.shape[0]].reshape(-1).astype(F32))
        at += v.shape[0]
    return out


def assemble_body(plan, ids_ref, *refs):
    count = len(plan)
    shards, pieces, outs = refs[:count], refs[count : count + 8], refs[count + 8 :]
    z, q, c = ids_ref[0], ids_ref[1], ids_ref[2]
    for shard_ref, out_ref, (rows, part, first, blocks) in zip(shards, outs, plan):
        half = blocks * WIDE
        out_ref[pl.ds(pl.multiple_of(z * rows, rows), rows), :] = shard_ref[...]
        for index in range(8):
            j, h = index % 4, (c if index < 4 else 1 - c)
            for k in (1, 2, 3):
                row = pl.multiple_of((z ^ k) * rows + (q ^ j) * part, part)
                for b in range(blocks):
                    col = pl.multiple_of(h * half + b * WIDE, WIDE)
                    start = first + b * part
                    out_ref[pl.ds(row, part), pl.ds(col, WIDE)] = pieces[index][
                        k - 1, start : start + part, :
                    ]


def assemble(ids, shards, plan, pieces):
    shapes = [
        jax.ShapeDtypeStruct((4 * rows, 2 * blocks * WIDE), BF16) for rows, _, _, blocks in plan
    ]
    return pl.pallas_call(
        functools.partial(assemble_body, plan),
        out_shape=shapes,
        in_specs=[SMEM] + [VMEM] * (len(shards) + 8),
        out_specs=[VMEM] * len(shards),
        compiler_params=compiler_params(40),
        cost_estimate=cost(3),
        name="assemble",
    )(ids, *shards, *pieces)


def place_body(plan, ids_ref, parts_ref, other_ref, *outs):
    q, c = ids_ref[1], ids_ref[2]
    for out, rows, part, first, blocks in plan:
        for h, pieces in ((c, parts_ref), (1 - c, other_ref)):
            for j in range(4):
                row = pl.multiple_of(rows + (q ^ j) * part, part)
                for b, (scale, offset) in enumerate(blocks):
                    col = pl.multiple_of(h * scale + offset, WIDE)
                    start = first + b * part
                    outs[out][pl.ds(row, part), pl.ds(col, WIDE)] = pieces[
                        j, start : start + part, :
                    ].astype(F32)


def place(ids, shapes, plan, parts, other):
    return pl.pallas_call(
        functools.partial(place_body, plan),
        out_shape=[jax.ShapeDtypeStruct(s, F32) for s in shapes],
        in_specs=[SMEM, VMEM, VMEM],
        out_specs=[VMEM] * len(shapes),
        compiler_params=compiler_params(40),
        cost_estimate=cost(3),
        name="place",
    )(ids, parts, other)


def dot(left, right, left_dim=1, right_dim=0):
    return lax.dot_general(
        left, right, (((left_dim,), (right_dim,)), ((), ())), preferred_element_type=F32
    )


def turn(values, cosine, early, late):
    width = values.shape[1]
    return (
        values * cosine
        + pltpu.roll(values, width - ROT // 2, 1) * early
        + pltpu.roll(values, ROT // 2, 1) * late
    )


def qkv_body(x_ref, w_ref, bias_ref, cos_ref, early_ref, late_ref, out_ref):
    values = dot(x_ref[...], w_ref[...]) + bias_ref[...]

    @pl.when(pl.program_id(0) < 4)
    def rotate_block():
        for b in range(WIDE // LANES):
            cols = slice(b * LANES, (b + 1) * LANES)
            out_ref[:, cols] = turn(
                values[:, cols], cos_ref[...], early_ref[...], late_ref[...]
            ).astype(BF16)

    @pl.when(pl.program_id(0) >= 4)
    def plain_block():
        out_ref[...] = values.astype(BF16)


def qkv_call(first_b, weight, bias, tables):
    tokens = first_b.shape[0]
    whole = lambda r, c: pl.BlockSpec((r, c), lambda i: (0, 0))
    return pl.pallas_call(
        qkv_body,
        grid=(3 * D // WIDE,),
        out_shape=jax.ShapeDtypeStruct((tokens, 3 * D), BF16),
        in_specs=[
            whole(tokens, D),
            pl.BlockSpec((D, WIDE), lambda i: (0, i)),
            pl.BlockSpec((1, WIDE), lambda i: (0, i)),
        ]
        + [whole(tokens, LANES)] * 3,
        out_specs=pl.BlockSpec((tokens, WIDE), lambda i: (0, i)),
        compiler_params=compiler_params(40),
        cost_estimate=cost(11),
        name="qkv",
    )(first_b, weight, bias, *tables)


def attention_body(
    first_call, q_ref, k_ref, v_ref, cot_ref, w_ref, mask_ref, cos_ref, early_ref, late_ref, *refs
):
    mixed_ref, grad_ref, key_t_ref, value_t_ref = refs if first_call else refs[2:]
    tokens = q_ref.shape[0]
    step = min(256, tokens)
    out_grad = dot(cot_ref[...], w_ref[...], 1, 1).astype(BF16)
    lane = lax.broadcasted_iota(jnp.int32, (tokens, LANES), 1)
    query_t = q_ref[...].astype(F32).T.astype(BF16)
    out_grad_t = out_grad.astype(F32).T.astype(BF16)
    nothing = jnp.zeros((tokens, LANES), BF16)
    keys = k_ref[...] * BF16(HD**-0.5)
    heads = []
    for h in range(2):
        here = (lane // HD) == h
        heads.append((jnp.where(here, keys, nothing), jnp.where(here, v_ref[...], nothing)))
    key_t_ref[...] = jnp.zeros_like(key_t_ref)
    value_t_ref[...] = jnp.zeros_like(value_t_ref)
    for first in range(0, tokens, step):
        last = first + step
        block = slice(first, last)
        mixed = jnp.zeros((step, LANES), F32)
        query_grad = jnp.zeros((step, LANES), F32)
        for h in range(2):
            key, value = heads[h][0][:last], heads[h][1][:last]
            rows = slice(h * HD, (h + 1) * HD)
            scores = dot(q_ref[block, :], key, 1, 1) + mask_ref[block, :last]
            expo = jnp.exp(scores - jnp.max(scores, axis=1, keepdims=True))
            probs = expo * (1.0 / jnp.sum(expo, axis=1, keepdims=True))
            probs_b = probs.astype(BF16)
            mixed += dot(probs_b, value)
            probs_grad = dot(out_grad[block], value, 1, 1)
            weighted = probs_grad * probs
            scores_grad = (weighted - probs * jnp.sum(weighted, axis=1, keepdims=True)).astype(BF16)
            query_grad += dot(scores_grad, key)
            key_t_ref[rows, :last] += dot(query_t[rows, block], scores_grad)
            value_t_ref[rows, :last] += dot(out_grad_t[rows, block], probs_b)
        mixed_ref[block, :] = mixed.astype(BF16)
        grad_ref[0, block, :] = turn(
            query_grad, cos_ref[block, :], -early_ref[block, :], -late_ref[block, :]
        ).astype(BF16)
    grad_ref[1, :, :] = turn(
        key_t_ref[...].T * HD**-0.5, cos_ref[...], -early_ref[...], -late_ref[...]
    ).astype(BF16)
    grad_ref[2, :, :] = value_t_ref[...].T.astype(BF16)


def attention_call(start, pairs, qkv_b, cot_b, out_weight, mask, tables, earlier):
    tokens = qkv_b.shape[0]
    every = D // LANES
    whole = lambda r, c: pl.BlockSpec((r, c), lambda i: (0, 0))
    part = lambda n: pl.BlockSpec((tokens, LANES), lambda i: (0, n * every + start + i))
    anywhere = pl.BlockSpec(memory_space=pl.ANY)
    return pl.pallas_call(
        functools.partial(attention_body, not earlier),
        grid=(pairs,),
        out_shape=[
            jax.ShapeDtypeStruct((tokens, D), BF16),
            jax.ShapeDtypeStruct((3, tokens, D), BF16),
        ],
        in_specs=[
            part(0),
            part(1),
            part(2),
            whole(tokens, D),
            pl.BlockSpec((LANES, D), lambda i: (start + i, 0)),
            whole(tokens, tokens),
        ]
        + [whole(tokens, LANES)] * 3
        + [anywhere] * len(earlier),
        out_specs=[
            pl.BlockSpec((tokens, LANES), lambda i: (0, start + i)),
            pl.BlockSpec((3, tokens, LANES), lambda i: (0, 0, start + i)),
        ],
        scratch_shapes=[
            pltpu.VMEM((LANES, tokens), F32),
            pltpu.VMEM((LANES, tokens), F32),
        ],
        input_output_aliases={9: 0, 10: 1} if earlier else {},
        compiler_params=compiler_params(56),
        cost_estimate=cost(9 * pairs),
        name="attention",
    )(qkv_b, qkv_b, qkv_b, cot_b, out_weight, mask, *tables, *earlier)


def store_block(keep_ref, send_ref, here, block, part, row):
    def store(ref):
        for z in range(4):
            for q in range(4):
                start = (z * 4 + q) * part
                ref[q, z, pl.ds(row, part), :] = block[start : start + part, :]

    pl.when(here)(lambda: store(keep_ref))
    pl.when(jnp.logical_not(here))(lambda: store(send_ref))


def qkv_grad_body(ids_ref, grad_ref, first_t_ref, mixed_ref, cot_ref, keep_ref, send_ref, bias_ref):
    step = pl.program_id(0)
    grad = grad_ref[0]
    h, b = step // 3, step % 3
    here = h == ids_ref[2]
    part = D // 16
    block = dot(first_t_ref[...], grad).astype(BF16)
    store_block(keep_ref, send_ref, here, block, part, pl.multiple_of(b * part, part))
    bias_ref[...] = jnp.sum(grad.astype(F32), axis=0, keepdims=True)

    @pl.when(b == 0)
    def out_part():
        block = dot(mixed_ref[...], cot_ref[...], 0, 0).astype(BF16)
        store_block(keep_ref, send_ref, here, block, part, 3 * part)


def qkv_grad_call(ids, grads, first_t, mixed_b, cot_b):
    tokens = cot_b.shape[0]
    whole = lambda r, c: pl.BlockSpec((r, c), lambda i: (0, 0))
    pack_spec = pl.BlockSpec((4, 4, D // 4, WIDE), lambda i: (0, 0, 0, 0))
    return pl.pallas_call(
        qkv_grad_body,
        grid=(3 * D // WIDE,),
        out_shape=[
            jax.ShapeDtypeStruct((4, 4, D // 4, WIDE), BF16),
            jax.ShapeDtypeStruct((4, 4, D // 4, WIDE), BF16),
            jax.ShapeDtypeStruct((1, 3 * D), F32),
        ],
        in_specs=[
            SMEM,
            pl.BlockSpec((1, tokens, WIDE), lambda i: (i // 2, 0, i % 2)),
            whole(D, tokens),
            whole(tokens, D),
            pl.BlockSpec((tokens, WIDE), lambda i: (0, i // 3)),
        ],
        out_specs=[pack_spec, pack_spec, pl.BlockSpec((1, WIDE), lambda i: (0, i))],
        compiler_params=compiler_params(56),
        cost_estimate=cost(14),
        name="qkv_grad",
    )(ids, grads, first_t, mixed_b, cot_b)


def mlp_body(
    ids_ref, x_ref, x_t_ref, cot_ref, up_ref, down_ref, bias_ref,
    act_ref, grad_ref, keep_ref, send_ref, bias_grad_ref,
):
    step = pl.program_id(0)
    tokens = x_ref.shape[0]
    rows = min(256, tokens)
    total = jnp.zeros((1, WIDE), F32)
    for first in range(0, tokens, rows):
        block = slice(first, first + rows)
        up = dot(x_ref[block, :], up_ref[...]) + bias_ref[...]
        act_grad = dot(cot_ref[block, :], down_ref[...], 1, 1)
        below = 0.5 + 0.5 * lax.erf(up * (0.5**0.5))
        slope = below + up * (jnp.exp(-0.5 * up * up) * 0.3989422804014327)
        up_grad = (act_grad * slope).astype(BF16)
        act_ref[block, :] = (up * below).astype(BF16)
        grad_ref[block, :] = up_grad
        total += jnp.sum(up_grad.astype(F32), axis=0, keepdims=True)
    bias_grad_ref[...] = total
    part = D // 16
    c = ids_ref[2]
    block = dot(x_t_ref[...], grad_ref[...]).astype(BF16)
    store_block(
        keep_ref, send_ref, step // 2 == c, block, part, pl.multiple_of((step % 2) * part, part)
    )
    down = dot(act_ref[...], cot_ref[...], 0, 0).astype(BF16)
    deep = WIDE // 4

    def store_down(keep, send):
        for q in range(4):
            rows_here = slice(q * deep, (q + 1) * deep)
            keep_ref[q, step, 2 * part :, :] = down[rows_here, keep * WIDE : (keep + 1) * WIDE]
            send_ref[q, step, 2 * part :, :] = down[rows_here, send * WIDE : (send + 1) * WIDE]

    pl.when(c == 0)(lambda: store_down(0, 1))
    pl.when(c == 1)(lambda: store_down(1, 0))


def mlp_call(ids, second_b, second_t, cot_b, up_weight, down_weight, bias):
    tokens = cot_b.shape[0]
    whole = lambda r, c: pl.BlockSpec((r, c), lambda i: (0, 0))
    column = pl.BlockSpec((tokens, WIDE), lambda i: (0, i))
    pack_spec = pl.BlockSpec((4, 4, D // 4, WIDE), lambda i: (0, 0, 0, 0))
    return pl.pallas_call(
        mlp_body,
        grid=(4,),
        out_shape=[
            jax.ShapeDtypeStruct((tokens, 4 * WIDE), BF16),
            jax.ShapeDtypeStruct((tokens, 4 * WIDE), BF16),
            jax.ShapeDtypeStruct((4, 4, D // 4, WIDE), BF16),
            jax.ShapeDtypeStruct((4, 4, D // 4, WIDE), BF16),
            jax.ShapeDtypeStruct((1, 4 * WIDE), F32),
        ],
        in_specs=[
            SMEM,
            whole(tokens, D),
            whole(D, tokens),
            whole(tokens, D),
            pl.BlockSpec((D, WIDE), lambda i: (0, i)),
            pl.BlockSpec((WIDE, D), lambda i: (i, 0)),
            pl.BlockSpec((1, WIDE), lambda i: (0, i)),
        ],
        out_specs=[column, column, pack_spec, pack_spec, pl.BlockSpec((1, WIDE), lambda i: (0, i))],
        compiler_params=compiler_params(56),
        cost_estimate=cost(20),
        name="mlp",
    )(ids, second_b, second_t, cot_b, up_weight, down_weight, bias)


def output_body(count, hidden_ref, mixed_ref, out_w_ref, out_bias_ref, down_bias_ref, *refs):
    acts, downs, out_ref = refs[:count], refs[count : 2 * count], refs[2 * count]
    wide = dot(acts[0][...], downs[0][...])
    for a, w in zip(acts[1:], downs[1:]):
        wide += dot(a[...], w[...])
    attention = dot(mixed_ref[...], out_w_ref[...]) + out_bias_ref[...]
    out_ref[...] = hidden_ref[...] + attention + (wide + down_bias_ref[...])


def output_call(hidden, mixed_b, out_weight, out_bias, down_bias, acts, downs):
    tokens = hidden.shape[0]
    rows = min(256, tokens)
    row = lambda c: pl.BlockSpec((rows, c), lambda i: (i, 0))
    whole = lambda a: pl.BlockSpec(a.shape, lambda i: (0, 0))
    return pl.pallas_call(
        functools.partial(output_body, len(acts)),
        grid=(tokens // rows,),
        out_shape=jax.ShapeDtypeStruct((tokens, D), F32),
        in_specs=[row(D), row(D), whole(out_weight), whole(out_bias), whole(down_bias)]
        + [row(a.shape[1]) for a in acts]
        + [whole(w) for w in downs],
        out_specs=row(D),
        compiler_params=compiler_params(56),
        cost_estimate=cost(10),
        name="output",
    )(hidden, mixed_b, out_weight, out_bias, down_bias, *acts, *downs)


def input_grad_body(count, hidden_ref, cot_ref, grad_ref, w_ref, gain_1_ref, gain_2_ref, *refs):
    ups, weights, out_ref, sums_ref = refs[:count], refs[count : 2 * count], refs[2 * count], refs[2 * count + 1]
    first = dot(grad_ref[0], w_ref[:, :D], 1, 1)
    for n in (1, 2):
        first += dot(grad_ref[n], w_ref[:, n * D : (n + 1) * D], 1, 1)
    second = dot(ups[0][...], weights[0][...], 1, 1)
    for u, w in zip(ups[1:], weights[1:]):
        second += dot(u[...], w[...], 1, 1)
    normed, scale = normalize(hidden_ref[...])
    cot = cot_ref[...]
    inner = first * gain_1_ref[...] + second * gain_2_ref[...]
    out_ref[...] = cot + scale * (
        inner
        - jnp.mean(inner, axis=-1, keepdims=True)
        - normed * jnp.mean(inner * normed, axis=-1, keepdims=True)
    )

    @pl.when(pl.program_id(0) == 0)
    def clear():
        sums_ref[...] = jnp.zeros_like(sums_ref)

    for n, value in enumerate((first * normed, first, second * normed, second, cot)):
        sums_ref[n : n + 1, :] += jnp.sum(value, axis=0, keepdims=True)


def input_grad_call(hidden, cotangent, grads, weight, gain_1, gain_2, ups, weights):
    tokens = hidden.shape[0]
    rows = min(256, tokens)
    row = lambda c: pl.BlockSpec((rows, c), lambda i: (i, 0))
    whole = lambda a: pl.BlockSpec(a.shape, lambda i: (0, 0))
    return pl.pallas_call(
        functools.partial(input_grad_body, len(ups)),
        grid=(tokens // rows,),
        out_shape=[jax.ShapeDtypeStruct((tokens, D), F32), jax.ShapeDtypeStruct((8, D), F32)],
        in_specs=[
            row(D),
            row(D),
            pl.BlockSpec((3, rows, D), lambda i: (0, i, 0)),
            whole(weight),
            whole(gain_1),
            whole(gain_2),
        ]
        + [row(u.shape[1]) for u in ups]
        + [whole(w) for w in weights],
        out_specs=[row(D), pl.BlockSpec((8, D), lambda i: (0, 0))],
        compiler_params=compiler_params(56),
        cost_estimate=cost(14),
        name="input_grad",
    )(hidden, cotangent, grads, weight, gain_1, gain_2, *ups, *weights)


def normalize(values):
    centre = values - jnp.mean(values, axis=-1, keepdims=True)
    scale = lax.rsqrt(jnp.mean(centre * centre, axis=-1, keepdims=True) + norm_eps)
    return centre * scale, scale


def rotary_tables(segments):
    tokens = segments.shape[0]
    before = jnp.sum((segments[:, None] > segments[None, :]).astype(jnp.int32), axis=1)
    places = jnp.arange(tokens, dtype=jnp.int32) - before
    half = ROT // 2
    lane = jnp.arange(LANES, dtype=jnp.int32) % HD
    freqs = 1.0 / 10000.0 ** ((lane % half).astype(F32) * 2.0 / ROT)
    angles = places.astype(F32)[:, None] * freqs[None, :]
    cosine, sine = jnp.cos(angles), jnp.sin(angles)
    turned, early = (lane < ROT)[None, :], (lane < half)[None, :]
    tables = (
        jnp.where(turned, cosine, 1.0),
        jnp.where(early, -sine, 0.0),
        jnp.where(turned & ~early, sine, 0.0),
    )
    rows = jnp.arange(tokens)
    allowed = (segments[:, None] == segments[None, :]) & (rows[:, None] >= rows[None, :])
    return tables, jnp.where(allowed, 0.0, -1e30).astype(F32)


def take(array, row, col, rows, cols):
    return lax.dynamic_slice(array, (row, col), (rows, cols))


def body(
    hidden_in,
    cotangent,
    seg_ids,
    first_gain,
    first_shift,
    second_gain,
    second_shift,
    qkv_weight,
    qkv_bias,
    out_weight,
    out_bias,
    up_weight,
    up_bias,
    down_weight,
    down_bias,
):
    z, q, c = place_ids()
    ids = jnp.stack([z, q, c]).astype(jnp.int32)
    own = qkv_weight.shape[0]
    part = own // 4
    hidden_units = up_weight.shape[1]
    own_hidden = down_weight.shape[0]
    chunks = own_hidden // WIDE
    small = gather_small(
        [first_gain, first_shift, second_gain, second_shift, qkv_bias, out_bias, up_bias, down_bias]
    )
    gain_1, shift_1, gain_2, shift_2, qkv_b0, out_b0, up_b0, down_b0 = small

    deep = WIDE // 4
    mlp_plan = ((own, part, 0, 2), (WIDE, deep, 2 * part, 1))
    mlp_weights, far = [], None
    for j in range(chunks):
        piece = jnp.concatenate(
            [take(up_weight, q * part, (2 * c + b) * own_hidden + j * WIDE, part, WIDE) for b in range(2)]
            + [take(down_weight, j * WIDE + q * deep, c * WIDE, deep, WIDE)]
        )
        far = gather_far(piece if far is None else after(piece, far))
        own_up = up_weight.reshape(own, 4, chunks, WIDE)[:, :, j].reshape(own, 4 * WIDE)
        own_down = down_weight[j * WIDE : (j + 1) * WIDE]
        mlp_weights.append(((own_up, own_down), gather_near(far)))
    piece = jnp.concatenate(
        [take(qkv_weight, q * part, c * 3 * WIDE + b * WIDE, part, WIDE) for b in range(3)]
        + [take(out_weight, q * part, c * WIDE, part, WIDE)]
    )
    attention_plan = ((own, part, 0, 3), (own, part, 3 * part, 1))
    attention_pieces = gather_near(gather_far(after(piece, far)))

    normed, _ = normalize(hidden_in)
    first_b = (normed * gain_1 + shift_1).astype(BF16)
    second_b = (normed * gain_2 + shift_2).astype(BF16)
    cot_b = cotangent.astype(BF16)
    tables, mask = rotary_tables(seg_ids)
    first_t, second_t = first_b.T, second_b.T

    bias_blocks = up_b0.reshape(4, chunks, WIDE)
    acts, ups, downs, up_weights, bias_parts, plane_terms, pending = [], [], [], [], [], [], None
    order = second_b
    for j in range(chunks):
        up_full, down_full = assemble(ids, mlp_weights[j][0], mlp_plan, mlp_weights[j][1])
        act, up_grad, keep, send, bias_g = mlp_call(
            ids,
            order,
            second_t,
            cot_b,
            up_full,
            down_full,
            bias_blocks[:, j].reshape(1, 4 * WIDE),
        )
        acts.append(act)
        ups.append(up_grad)
        downs.append(down_full)
        up_weights.append(up_full)
        bias_parts.append(bias_g.reshape(4, WIDE))
        if pending is not None:
            keep_before, got_before = pending
            keep_before = after(keep_before, keep)
            sends = plane_sends(keep_before, got_before, q)
            plane_terms.append(plane_swap(sends))
            order_next = sends
        pending = (keep, swap(send, "rep", 1))
        order = after(second_b, keep, send)
    qkv_full, out_full = assemble(ids, (qkv_weight, out_weight), attention_plan, attention_pieces)
    first_b = after(first_b, *order_next) if chunks > 1 else after(first_b, pending[0])
    qkv_b = qkv_call(first_b, qkv_full, qkv_b0[None, :], tables)
    keep, got = pending
    sends = plane_sends(after(keep, qkv_b), got, q)
    plane_terms.append(plane_swap(sends))

    pairs = D // LANES // 3
    earlier = attention_call(0, pairs, after(qkv_b, *sends), cot_b, out_full, mask, tables, ())
    earlier = attention_call(pairs, pairs, qkv_b, cot_b, out_full, mask, tables, tuple(earlier))
    gate = earlier[0]
    plane_terms = [[after(terms[0], gate)] + terms[1:] for terms in plane_terms]
    sends = shard_sends(plane_terms, z)
    earlier = attention_call(
        2 * pairs, pairs, after(qkv_b, *sends), cot_b, out_full, mask, tables, tuple(earlier)
    )
    owned = shard_sum([after(sends[0], earlier[0])] + sends[1:])
    mixed_b, grads = earlier
    keep, send, qkv_bias_g = qkv_grad_call(ids, after(grads, owned), first_t, mixed_b, cot_b)
    mlp_parts = share_plane(owned)
    mlp_parts = after(mlp_parts, keep)
    mlp_other = swap(mlp_parts, "rep", 1)

    got = swap(send, "rep", 1)
    output = output_call(
        after(hidden_in, send, mlp_parts),
        mixed_b,
        out_full,
        out_b0[None, :],
        down_b0[None, :],
        acts,
        downs,
    )
    sends = plane_sends(after(keep, output), got, q)
    input_grad, row_sums = input_grad_call(
        after(hidden_in, *sends),
        cotangent,
        grads,
        qkv_full,
        gain_1[None, :],
        gain_2[None, :],
        ups,
        up_weights,
    )
    terms = plane_swap(sends)
    terms[0] = after(terms[0], input_grad)
    sends = shard_sends([terms], z)
    up_bias_g = jnp.stack(bias_parts, axis=1).reshape(-1)
    sums = [row_sums[0], row_sums[1], row_sums[2], row_sums[3], qkv_bias_g.reshape(-1), row_sums[4], up_bias_g]
    total = sum_small(pack(sums)).reshape(-1)

    mlp_place = []
    for j in range(chunks):
        first = j * (D // 4)
        mlp_place.append(
            (0, 0, part, first, tuple((2 * own_hidden, b * own_hidden + j * WIDE) for b in range(2)))
        )
        mlp_place.append((1, j * WIDE, deep, first + 2 * part, ((WIDE, 0),)))
    up_weight_g, down_weight_g = place(
        ids, [(own, hidden_units), (own_hidden, D)], mlp_place, after(mlp_parts, *sends), mlp_other
    )
    attention_place = [
        (0, 0, part, 0, tuple((3 * WIDE, b * WIDE) for b in range(3))),
        (1, 0, part, 3 * part, ((WIDE, 0),)),
    ]
    parts = share_plane(shard_sum(sends))
    qkv_weight_g, out_weight_g = place(
        ids, [(own, 3 * D), (own, D)], attention_place, parts, swap(parts, "rep", 1)
    )
    summed, at_row = [], 0
    for s in sums:
        size = s.shape[0] // 4
        summed.append(lax.dynamic_slice(total, (at_row + z * size,), (size,)))
        at_row += s.shape[0]
    return (
        output,
        input_grad,
        summed[0],
        summed[1],
        summed[2],
        summed[3],
        qkv_weight_g,
        summed[4],
        out_weight_g,
        summed[5],
        up_weight_g,
        summed[6],
        down_weight_g,
        summed[5],
    )


def solution(mesh):
    tokens = P(("rep", "shard"), None)
    matrix, vector = P("shard", None), P("shard")
    params = (vector,) * 4 + (matrix, vector) * 4
    in_specs = (tokens, tokens, P(("rep", "shard"))) + params
    out_specs = (tokens, tokens) + params
    return jax.shard_map(body, mesh=mesh, in_specs=in_specs, out_specs=out_specs, check_vma=False)
```

```python
import functools

import jax
import jax.numpy as jnp
from jax import lax
from jax.experimental import pallas as pl
from jax.experimental.pallas import tpu as pltpu
from jax.sharding import PartitionSpec as P

D = 768
H = 12
HD = 64
ROT = 16
WIDE = 384
LANES = 128
F32, BF16 = jnp.float32, jnp.bfloat16
norm_eps = 1e-05


def compiler_params(mib):
    return pltpu.CompilerParams(vmem_limit_bytes=mib * 2**20)


def cost(microseconds):
    return pl.CostEstimate(
        flops=int(microseconds * 1.1e9), bytes_accessed=int(microseconds * 1e5), transcendentals=0
    )


VMEM = pl.BlockSpec(memory_space=pltpu.VMEM)
SMEM = pl.BlockSpec(memory_space=pltpu.SMEM)


def swap(value, axis, bit):
    size = lax.axis_size(axis)
    return lax.ppermute(value, axis, [(i, i ^ bit) for i in range(size)])


def place_ids():
    rep = lax.axis_index("rep").astype(jnp.uint32)
    return lax.axis_index("shard").astype(jnp.uint32), (rep >> 1) & 3, rep & 1


def after(value, *others):
    return lax.optimization_barrier((value, *others))[0]


def gather_far(piece):
    return jnp.stack([swap(piece, "shard", k) for k in (1, 2, 3)])


def gather_plane(far):
    return [far] + [swap(far, "rep", j * 2) for j in (1, 2, 3)]


def gather_core(parts):
    return parts + [swap(p, "rep", 1) for p in parts]


def total_of(arrays):
    return (
        (arrays[0].astype(F32) + arrays[1].astype(F32))
        + (arrays[2].astype(F32) + arrays[3].astype(F32))
    ).astype(BF16)


def at(block, index):
    return lax.dynamic_index_in_dim(block, index, 0, keepdims=False)


def plane_sum_body(ids_ref, keep_ref, got_ref, *outs):
    q = ids_ref[1]
    for j in range(4):
        total = keep_ref[q ^ j].astype(F32) + got_ref[q ^ j].astype(F32)
        outs[j][...] = total.astype(BF16)


def plane_sends(ids, keep, got):
    rows = keep.shape[2]
    block = pl.BlockSpec((4, 1, rows, WIDE), lambda i: (0, i, 0, 0))
    return pl.pallas_call(
        plane_sum_body,
        grid=(4,),
        out_shape=[jax.ShapeDtypeStruct((4, rows, WIDE), BF16)] * 4,
        in_specs=[SMEM, block, block],
        out_specs=[pl.BlockSpec((1, rows, WIDE), lambda i: (i, 0, 0))] * 4,
        compiler_params=compiler_params(40),
        cost_estimate=cost(3),
        name="plane_sum",
    )(ids, keep, got)


def plane_swap(sends):
    return [sends[0]] + [swap(sends[j], "rep", j * 2) for j in (1, 2, 3)]


def shard_sends(groups, z):
    return [
        jnp.concatenate([total_of([at(term, z ^ k) for term in terms]) for terms in groups])
        for k in range(4)
    ]


def shard_sum(sends):
    owned = total_of([sends[0]] + [swap(sends[k], "shard", k) for k in (1, 2, 3)])
    bit = 8
    while bit < lax.axis_size("rep"):
        owned = (owned.astype(F32) + swap(owned, "rep", bit).astype(F32)).astype(BF16)
        bit *= 2
    return owned


def share_plane(owned):
    return jnp.stack([owned] + [swap(owned, "rep", j * 2) for j in (1, 2, 3)])


def sum_small(vector):
    bit = 1
    while bit < lax.axis_size("rep"):
        if bit not in (2, 4):
            vector = vector + swap(vector, "rep", bit)
        bit *= 2
    vector = (vector + swap(vector, "rep", 2)) + (swap(vector, "rep", 4) + swap(vector, "rep", 6))
    return (vector + swap(vector, "shard", 1)) + (swap(vector, "shard", 2) + swap(vector, "shard", 3))


def pack(vectors):
    flat = jnp.concatenate([v.reshape(-1) for v in vectors])
    fill = -flat.shape[0] % 1024
    return jnp.concatenate([flat, jnp.zeros((fill,), flat.dtype)]).reshape(-1, LANES)


def gather_small(vectors):
    packed = pack(vectors)
    z = lax.axis_index("shard")
    near = jnp.stack([packed] + [swap(packed, "shard", k) for k in (1, 2, 3)])
    rows = jnp.stack(
        [lax.dynamic_index_in_dim(near, z ^ i, 0, keepdims=False) for i in range(4)]
    ).reshape(4, -1)
    out, at = [], 0
    for v in vectors:
        out.append(rows[:, at : at + v.shape[0]].reshape(-1).astype(F32))
        at += v.shape[0]
    return out


def assemble_body(plan, ids_ref, *refs):
    count = len(plan)
    shards, pieces, outs = refs[:count], refs[count : count + 8], refs[count + 8 :]
    z, q, c = ids_ref[0], ids_ref[1], ids_ref[2]
    for shard_ref, out_ref, (rows, part, first, blocks) in zip(shards, outs, plan):
        half = blocks * WIDE
        out_ref[pl.ds(pl.multiple_of(z * rows, rows), rows), :] = shard_ref[...]
        for index in range(8):
            j, h = index % 4, (c if index < 4 else 1 - c)
            for k in (1, 2, 3):
                row = pl.multiple_of((z ^ k) * rows + (q ^ j) * part, part)
                for b in range(blocks):
                    col = pl.multiple_of(h * half + b * WIDE, WIDE)
                    start = first + b * part
                    out_ref[pl.ds(row, part), pl.ds(col, WIDE)] = pieces[index][
                        k - 1, start : start + part, :
                    ]


def assemble(ids, shards, plan, pieces):
    shapes = [
        jax.ShapeDtypeStruct((4 * rows, 2 * blocks * WIDE), BF16) for rows, _, _, blocks in plan
    ]
    return pl.pallas_call(
        functools.partial(assemble_body, plan),
        out_shape=shapes,
        in_specs=[SMEM] + [VMEM] * (len(shards) + 8),
        out_specs=[VMEM] * len(shards),
        compiler_params=compiler_params(40),
        cost_estimate=cost(3),
        name="assemble",
    )(ids, *shards, *pieces)


def place_body(plan, ids_ref, parts_ref, other_ref, *outs):
    q, c = ids_ref[1], ids_ref[2]
    for out, rows, part, first, blocks in plan:
        for h, pieces in ((c, parts_ref), (1 - c, other_ref)):
            for j in range(4):
                row = pl.multiple_of(rows + (q ^ j) * part, part)
                for b, (scale, offset) in enumerate(blocks):
                    col = pl.multiple_of(h * scale + offset, WIDE)
                    start = first + b * part
                    outs[out][pl.ds(row, part), pl.ds(col, WIDE)] = pieces[
                        j, start : start + part, :
                    ].astype(F32)


def place(ids, shapes, plan, parts, other):
    return pl.pallas_call(
        functools.partial(place_body, plan),
        out_shape=[jax.ShapeDtypeStruct(s, F32) for s in shapes],
        in_specs=[SMEM, VMEM, VMEM],
        out_specs=[VMEM] * len(shapes),
        compiler_params=compiler_params(40),
        cost_estimate=cost(3),
        name="place",
    )(ids, parts, other)


def dot(left, right, left_dim=1, right_dim=0):
    return lax.dot_general(
        left, right, (((left_dim,), (right_dim,)), ((), ())), preferred_element_type=F32
    )


def turn(values, cosine, early, late):
    width = values.shape[1]
    return (
        values * cosine
        + pltpu.roll(values, width - ROT // 2, 1) * early
        + pltpu.roll(values, ROT // 2, 1) * late
    )


def qkv_body(gate_ref, x_ref, w_ref, bias_ref, cos_ref, early_ref, late_ref, out_ref):
    values = dot(x_ref[...], w_ref[...]) + bias_ref[...]

    @pl.when(pl.program_id(0) < 4)
    def rotate_block():
        for b in range(WIDE // LANES):
            cols = slice(b * LANES, (b + 1) * LANES)
            out_ref[:, cols] = turn(
                values[:, cols], cos_ref[...], early_ref[...], late_ref[...]
            ).astype(BF16)

    @pl.when(pl.program_id(0) >= 4)
    def plain_block():
        out_ref[...] = values.astype(BF16)


def qkv_call(gate, first_b, weight, bias, tables):
    tokens = first_b.shape[0]
    whole = lambda r, c: pl.BlockSpec((r, c), lambda i: (0, 0))
    return pl.pallas_call(
        qkv_body,
        grid=(3 * D // WIDE,),
        out_shape=jax.ShapeDtypeStruct((tokens, 3 * D), BF16),
        in_specs=[
            SMEM,
            whole(tokens, D),
            pl.BlockSpec((D, WIDE), lambda i: (0, i)),
            pl.BlockSpec((1, WIDE), lambda i: (0, i)),
        ]
        + [whole(tokens, LANES)] * 3,
        out_specs=pl.BlockSpec((tokens, WIDE), lambda i: (0, i)),
        compiler_params=compiler_params(40),
        cost_estimate=cost(11),
        name="qkv",
    )(gate, first_b, weight, bias, *tables)


def attention_body(
    first_call, gate_ref, q_ref, k_ref, v_ref, cot_ref, w_ref, mask_ref, cos_ref, early_ref, late_ref, *refs
):
    mixed_ref, grad_ref, key_t_ref, value_t_ref = refs if first_call else refs[2:]
    tokens = q_ref.shape[0]
    step = min(256, tokens)
    out_grad = dot(cot_ref[...], w_ref[...], 1, 1).astype(BF16)
    lane = lax.broadcasted_iota(jnp.int32, (tokens, LANES), 1)
    query_t = q_ref[...].astype(F32).T.astype(BF16)
    out_grad_t = out_grad.astype(F32).T.astype(BF16)
    nothing = jnp.zeros((tokens, LANES), BF16)
    keys = k_ref[...] * BF16(HD**-0.5)
    heads = []
    for h in range(2):
        here = (lane // HD) == h
        heads.append((jnp.where(here, keys, nothing), jnp.where(here, v_ref[...], nothing)))
    key_t_ref[...] = jnp.zeros_like(key_t_ref)
    value_t_ref[...] = jnp.zeros_like(value_t_ref)
    for first in range(0, tokens, step):
        last = first + step
        block = slice(first, last)
        mixed = jnp.zeros((step, LANES), F32)
        query_grad = jnp.zeros((step, LANES), F32)
        for h in range(2):
            key, value = heads[h][0][:last], heads[h][1][:last]
            rows = slice(h * HD, (h + 1) * HD)
            scores = dot(q_ref[block, :], key, 1, 1) + mask_ref[block, :last]
            expo = jnp.exp(scores - jnp.max(scores, axis=1, keepdims=True))
            probs = expo * (1.0 / jnp.sum(expo, axis=1, keepdims=True))
            probs_b = probs.astype(BF16)
            mixed += dot(probs_b, value)
            probs_grad = dot(out_grad[block], value, 1, 1)
            weighted = probs_grad * probs
            scores_grad = (weighted - probs * jnp.sum(weighted, axis=1, keepdims=True)).astype(BF16)
            query_grad += dot(scores_grad, key)
            key_t_ref[rows, :last] += dot(query_t[rows, block], scores_grad)
            value_t_ref[rows, :last] += dot(out_grad_t[rows, block], probs_b)
        mixed_ref[block, :] = mixed.astype(BF16)
        grad_ref[0, block, :] = turn(
            query_grad, cos_ref[block, :], -early_ref[block, :], -late_ref[block, :]
        ).astype(BF16)
    grad_ref[1, :, :] = turn(
        key_t_ref[...].T * HD**-0.5, cos_ref[...], -early_ref[...], -late_ref[...]
    ).astype(BF16)
    grad_ref[2, :, :] = value_t_ref[...].T.astype(BF16)


def attention_call(gate, start, pairs, qkv_b, cot_b, out_weight, mask, tables, earlier):
    tokens = qkv_b.shape[0]
    every = D // LANES
    whole = lambda r, c: pl.BlockSpec((r, c), lambda i: (0, 0))
    part = lambda n: pl.BlockSpec((tokens, LANES), lambda i: (0, n * every + start + i))
    anywhere = pl.BlockSpec(memory_space=pl.ANY)
    return pl.pallas_call(
        functools.partial(attention_body, not earlier),
        grid=(pairs,),
        out_shape=[
            jax.ShapeDtypeStruct((tokens, D), BF16),
            jax.ShapeDtypeStruct((3, tokens, D), BF16),
        ],
        in_specs=[
            SMEM,
            part(0),
            part(1),
            part(2),
            whole(tokens, D),
            pl.BlockSpec((LANES, D), lambda i: (start + i, 0)),
            whole(tokens, tokens),
        ]
        + [whole(tokens, LANES)] * 3
        + [anywhere] * len(earlier),
        out_specs=[
            pl.BlockSpec((tokens, LANES), lambda i: (0, start + i)),
            pl.BlockSpec((3, tokens, LANES), lambda i: (0, 0, start + i)),
        ],
        scratch_shapes=[
            pltpu.VMEM((LANES, tokens), F32),
            pltpu.VMEM((LANES, tokens), F32),
        ],
        input_output_aliases={10: 0, 11: 1} if earlier else {},
        compiler_params=compiler_params(56),
        cost_estimate=cost(9 * pairs),
        name="attention",
    )(gate, qkv_b, qkv_b, qkv_b, cot_b, out_weight, mask, *tables, *earlier)


def store_block(keep_ref, send_ref, here, block, part, row):
    def store(ref):
        for z in range(4):
            for q in range(4):
                start = (z * 4 + q) * part
                ref[q, z, pl.ds(row, part), :] = block[start : start + part, :]

    pl.when(here)(lambda: store(keep_ref))
    pl.when(jnp.logical_not(here))(lambda: store(send_ref))


def qkv_grad_body(ids_ref, grad_ref, first_t_ref, mixed_ref, cot_ref, keep_ref, send_ref, bias_ref):
    step = pl.program_id(0)
    grad = grad_ref[0]
    h, b = step // 3, step % 3
    here = h == ids_ref[2]
    part = D // 16
    block = dot(first_t_ref[...], grad).astype(BF16)
    store_block(keep_ref, send_ref, here, block, part, pl.multiple_of(b * part, part))
    bias_ref[...] = jnp.sum(grad.astype(F32), axis=0, keepdims=True)

    @pl.when(b == 0)
    def out_part():
        block = dot(mixed_ref[...], cot_ref[...], 0, 0).astype(BF16)
        store_block(keep_ref, send_ref, here, block, part, 3 * part)


def qkv_grad_call(ids, grads, first_t, mixed_b, cot_b):
    tokens = cot_b.shape[0]
    whole = lambda r, c: pl.BlockSpec((r, c), lambda i: (0, 0))
    pack_spec = pl.BlockSpec((4, 4, D // 4, WIDE), lambda i: (0, 0, 0, 0))
    return pl.pallas_call(
        qkv_grad_body,
        grid=(3 * D // WIDE,),
        out_shape=[
            jax.ShapeDtypeStruct((4, 4, D // 4, WIDE), BF16),
            jax.ShapeDtypeStruct((4, 4, D // 4, WIDE), BF16),
            jax.ShapeDtypeStruct((1, 3 * D), F32),
        ],
        in_specs=[
            SMEM,
            pl.BlockSpec((1, tokens, WIDE), lambda i: (i // 2, 0, i % 2)),
            whole(D, tokens),
            whole(tokens, D),
            pl.BlockSpec((tokens, WIDE), lambda i: (0, i // 3)),
        ],
        out_specs=[pack_spec, pack_spec, pl.BlockSpec((1, WIDE), lambda i: (0, i))],
        compiler_params=compiler_params(56),
        cost_estimate=cost(14),
        name="qkv_grad",
    )(ids, grads, first_t, mixed_b, cot_b)


def mlp_body(
    ids_ref, x_ref, x_t_ref, cot_ref, up_ref, down_ref, bias_ref,
    act_ref, grad_ref, keep_ref, send_ref, bias_grad_ref,
):
    step = pl.program_id(0)
    tokens = x_ref.shape[0]
    rows = min(256, tokens)
    total = jnp.zeros((1, WIDE), F32)
    for first in range(0, tokens, rows):
        block = slice(first, first + rows)
        up = dot(x_ref[block, :], up_ref[...]) + bias_ref[...]
        act_grad = dot(cot_ref[block, :], down_ref[...], 1, 1)
        below = 0.5 + 0.5 * lax.erf(up * (0.5**0.5))
        slope = below + up * (jnp.exp(-0.5 * up * up) * 0.3989422804014327)
        up_grad = (act_grad * slope).astype(BF16)
        act_ref[block, :] = (up * below).astype(BF16)
        grad_ref[block, :] = up_grad
        total += jnp.sum(up_grad.astype(F32), axis=0, keepdims=True)
    bias_grad_ref[...] = total
    part = D // 16
    c = ids_ref[2]
    block = dot(x_t_ref[...], grad_ref[...]).astype(BF16)
    store_block(
        keep_ref, send_ref, step // 2 == c, block, part, pl.multiple_of((step % 2) * part, part)
    )
    down = dot(act_ref[...], cot_ref[...], 0, 0).astype(BF16)
    deep = WIDE // 4

    def store_down(keep, send):
        for q in range(4):
            rows_here = slice(q * deep, (q + 1) * deep)
            keep_ref[q, step, 2 * part :, :] = down[rows_here, keep * WIDE : (keep + 1) * WIDE]
            send_ref[q, step, 2 * part :, :] = down[rows_here, send * WIDE : (send + 1) * WIDE]

    pl.when(c == 0)(lambda: store_down(0, 1))
    pl.when(c == 1)(lambda: store_down(1, 0))


def mlp_call(ids, second_b, second_t, cot_b, up_weight, down_weight, bias):
    tokens = cot_b.shape[0]
    whole = lambda r, c: pl.BlockSpec((r, c), lambda i: (0, 0))
    column = pl.BlockSpec((tokens, WIDE), lambda i: (0, i))
    pack_spec = pl.BlockSpec((4, 4, D // 4, WIDE), lambda i: (0, 0, 0, 0))
    return pl.pallas_call(
        mlp_body,
        grid=(4,),
        out_shape=[
            jax.ShapeDtypeStruct((tokens, 4 * WIDE), BF16),
            jax.ShapeDtypeStruct((tokens, 4 * WIDE), BF16),
            jax.ShapeDtypeStruct((4, 4, D // 4, WIDE), BF16),
            jax.ShapeDtypeStruct((4, 4, D // 4, WIDE), BF16),
            jax.ShapeDtypeStruct((1, 4 * WIDE), F32),
        ],
        in_specs=[
            SMEM,
            whole(tokens, D),
            whole(D, tokens),
            whole(tokens, D),
            pl.BlockSpec((D, WIDE), lambda i: (0, i)),
            pl.BlockSpec((WIDE, D), lambda i: (i, 0)),
            pl.BlockSpec((1, WIDE), lambda i: (0, i)),
        ],
        out_specs=[column, column, pack_spec, pack_spec, pl.BlockSpec((1, WIDE), lambda i: (0, i))],
        compiler_params=compiler_params(56),
        cost_estimate=cost(20),
        name="mlp",
    )(ids, second_b, second_t, cot_b, up_weight, down_weight, bias)


def output_body(count, gate_ref, hidden_ref, mixed_ref, out_w_ref, out_bias_ref, down_bias_ref, *refs):
    acts, downs, out_ref = refs[:count], refs[count : 2 * count], refs[2 * count]
    wide = dot(acts[0][...], downs[0][...])
    for a, w in zip(acts[1:], downs[1:]):
        wide += dot(a[...], w[...])
    attention = dot(mixed_ref[...], out_w_ref[...]) + out_bias_ref[...]
    out_ref[...] = hidden_ref[...] + attention + (wide + down_bias_ref[...])


def output_call(gate, hidden, mixed_b, out_weight, out_bias, down_bias, acts, downs):
    tokens = hidden.shape[0]
    rows = min(256, tokens)
    row = lambda c: pl.BlockSpec((rows, c), lambda i: (i, 0))
    whole = lambda a: pl.BlockSpec(a.shape, lambda i: (0, 0))
    return pl.pallas_call(
        functools.partial(output_body, len(acts)),
        grid=(tokens // rows,),
        out_shape=jax.ShapeDtypeStruct((tokens, D), F32),
        in_specs=[SMEM, row(D), row(D), whole(out_weight), whole(out_bias), whole(down_bias)]
        + [row(a.shape[1]) for a in acts]
        + [whole(w) for w in downs],
        out_specs=row(D),
        compiler_params=compiler_params(56),
        cost_estimate=cost(10),
        name="output",
    )(gate, hidden, mixed_b, out_weight, out_bias, down_bias, *acts, *downs)


def input_grad_body(count, gate_ref, hidden_ref, cot_ref, grad_ref, w_ref, gain_1_ref, gain_2_ref, *refs):
    ups, weights, out_ref, sums_ref = refs[:count], refs[count : 2 * count], refs[2 * count], refs[2 * count + 1]
    first = dot(grad_ref[0], w_ref[:, :D], 1, 1)
    for n in (1, 2):
        first += dot(grad_ref[n], w_ref[:, n * D : (n + 1) * D], 1, 1)
    second = dot(ups[0][...], weights[0][...], 1, 1)
    for u, w in zip(ups[1:], weights[1:]):
        second += dot(u[...], w[...], 1, 1)
    normed, scale = normalize(hidden_ref[...])
    cot = cot_ref[...]
    inner = first * gain_1_ref[...] + second * gain_2_ref[...]
    out_ref[...] = cot + scale * (
        inner
        - jnp.mean(inner, axis=-1, keepdims=True)
        - normed * jnp.mean(inner * normed, axis=-1, keepdims=True)
    )

    @pl.when(pl.program_id(0) == 0)
    def clear():
        sums_ref[...] = jnp.zeros_like(sums_ref)

    for n, value in enumerate((first * normed, first, second * normed, second, cot)):
        sums_ref[n : n + 1, :] += jnp.sum(value, axis=0, keepdims=True)


def input_grad_call(gate, hidden, cotangent, grads, weight, gain_1, gain_2, ups, weights):
    tokens = hidden.shape[0]
    rows = min(256, tokens)
    row = lambda c: pl.BlockSpec((rows, c), lambda i: (i, 0))
    whole = lambda a: pl.BlockSpec(a.shape, lambda i: (0, 0))
    return pl.pallas_call(
        functools.partial(input_grad_body, len(ups)),
        grid=(tokens // rows,),
        out_shape=[jax.ShapeDtypeStruct((tokens, D), F32), jax.ShapeDtypeStruct((8, D), F32)],
        in_specs=[
            SMEM,
            row(D),
            row(D),
            pl.BlockSpec((3, rows, D), lambda i: (0, i, 0)),
            whole(weight),
            whole(gain_1),
            whole(gain_2),
        ]
        + [row(u.shape[1]) for u in ups]
        + [whole(w) for w in weights],
        out_specs=[row(D), pl.BlockSpec((8, D), lambda i: (0, 0))],
        compiler_params=compiler_params(56),
        cost_estimate=cost(14),
        name="input_grad",
    )(gate, hidden, cotangent, grads, weight, gain_1, gain_2, *ups, *weights)


def normalize(values):
    centre = values - jnp.mean(values, axis=-1, keepdims=True)
    scale = lax.rsqrt(jnp.mean(centre * centre, axis=-1, keepdims=True) + norm_eps)
    return centre * scale, scale


def first_body(
    gate_ref, hidden_ref, cot_ref, seg_col_ref, seg_row_ref, gain_1_ref, shift_1_ref, gain_2_ref, shift_2_ref,
    first_ref, second_ref, first_t_ref, second_t_ref, cot_b_ref, mask_ref, places_ref,
):
    normed, _ = normalize(hidden_ref[...])
    first = (normed * gain_1_ref[...] + shift_1_ref[...]).astype(BF16)
    second = (normed * gain_2_ref[...] + shift_2_ref[...]).astype(BF16)
    first_ref[...] = first
    second_ref[...] = second
    first_t_ref[...] = first.astype(F32).T.astype(BF16)
    second_t_ref[...] = second.astype(F32).T.astype(BF16)
    cot_b_ref[...] = cot_ref[...].astype(BF16)
    rows, tokens = mask_ref.shape
    row = pl.program_id(0) * rows + lax.broadcasted_iota(jnp.int32, (rows, tokens), 0)
    col = lax.broadcasted_iota(jnp.int32, (rows, tokens), 1)
    mine, others = seg_col_ref[...], seg_row_ref[...]
    mask_ref[...] = jnp.where((mine == others) & (col <= row), 0.0, -1e30)
    before = jnp.sum(jnp.where(mine > others, 1.0, 0.0), axis=1, keepdims=True)
    places_ref[...] = row[:, :LANES].astype(F32) - before


def first_call(gate, hidden, cotangent, segments, vectors):
    tokens = hidden.shape[0]
    rows = min(256, tokens)
    row = lambda c: pl.BlockSpec((rows, c), lambda i: (i, 0))
    turned = pl.BlockSpec((D, rows), lambda i: (0, i))
    whole = lambda r, c: pl.BlockSpec((r, c), lambda i: (0, 0))
    wide = jax.ShapeDtypeStruct((tokens, D), BF16)
    tall = jax.ShapeDtypeStruct((D, tokens), BF16)
    return pl.pallas_call(
        first_body,
        grid=(tokens // rows,),
        out_shape=[
            wide,
            wide,
            tall,
            tall,
            wide,
            jax.ShapeDtypeStruct((tokens, tokens), F32),
            jax.ShapeDtypeStruct((tokens, LANES), F32),
        ],
        in_specs=[SMEM, row(D), row(D), row(1), whole(1, tokens)] + [whole(1, D)] * 4,
        out_specs=[row(D), row(D), turned, turned, row(D), row(tokens), row(LANES)],
        compiler_params=compiler_params(40),
        cost_estimate=cost(12),
        name="first",
    )(
        gate,
        hidden,
        cotangent,
        segments[:, None],
        segments[None, :],
        *[v[None, :] for v in vectors],
    )


def rotary_tables(places):
    half = ROT // 2
    lane = jnp.arange(LANES, dtype=jnp.int32) % HD
    freqs = 1.0 / 10000.0 ** ((lane % half).astype(F32) * 2.0 / ROT)
    angles = places * freqs[None, :]
    cosine, sine = jnp.cos(angles), jnp.sin(angles)
    turned, early = (lane < ROT)[None, :], (lane < half)[None, :]
    return (
        jnp.where(turned, cosine, 1.0),
        jnp.where(early, -sine, 0.0),
        jnp.where(turned & ~early, sine, 0.0),
    )


def take(array, row, col, rows, cols):
    return lax.dynamic_slice(array, (row, col), (rows, cols))


def body(
    hidden_in,
    cotangent,
    seg_ids,
    first_gain,
    first_shift,
    second_gain,
    second_shift,
    qkv_weight,
    qkv_bias,
    out_weight,
    out_bias,
    up_weight,
    up_bias,
    down_weight,
    down_bias,
):
    z, q, c = place_ids()
    ids = jnp.stack([z, q, c]).astype(jnp.int32)
    own = qkv_weight.shape[0]
    part = own // 4
    hidden_units = up_weight.shape[1]
    own_hidden = down_weight.shape[0]
    chunks = own_hidden // WIDE
    deep = WIDE // 4
    mlp_plan = ((own, part, 0, 2), (WIDE, deep, 2 * part, 1))
    mlp_weights, parts = [], None
    for j in range(chunks):
        piece = jnp.concatenate(
            [take(up_weight, q * part, (2 * c + b) * own_hidden + j * WIDE, part, WIDE) for b in range(2)]
            + [take(down_weight, j * WIDE + q * deep, c * WIDE, deep, WIDE)]
        )
        far = gather_far(piece if parts is None else after(piece, *parts[1:]))
        parts = gather_plane(far)
        if j == 0:
            small = gather_small(
                [after(first_gain, piece), first_shift, second_gain, second_shift]
                + [qkv_bias, out_bias, up_bias, down_bias]
            )
            gain_1, shift_1, gain_2, shift_2, qkv_b0, out_b0, up_b0, down_b0 = small
            first_b, second_b, first_t, second_t, cot_b, mask, places = first_call(
                after(ids, far), hidden_in, cotangent, seg_ids, small[:4]
            )
            parts = [far] + [after(p, first_b) for p in parts[1:]]
        own_up = up_weight.reshape(own, 4, chunks, WIDE)[:, :, j].reshape(own, 4 * WIDE)
        own_down = down_weight[j * WIDE : (j + 1) * WIDE]
        mlp_weights.append(((own_up, own_down), gather_core(parts)))
    piece = jnp.concatenate(
        [take(qkv_weight, q * part, c * 3 * WIDE + b * WIDE, part, WIDE) for b in range(3)]
        + [take(out_weight, q * part, c * WIDE, part, WIDE)]
    )
    attention_plan = ((own, part, 0, 3), (own, part, 3 * part, 1))
    attention_pieces = gather_core(gather_plane(gather_far(after(piece, *parts[1:]))))
    tables = rotary_tables(places)

    bias_blocks = up_b0.reshape(4, chunks, WIDE)
    acts, ups, downs, up_weights, bias_parts, plane_terms, pending = [], [], [], [], [], [], None
    order = ids
    for j in range(chunks):
        up_full, down_full = assemble(ids, mlp_weights[j][0], mlp_plan, mlp_weights[j][1])
        act, up_grad, keep, send, bias_g = mlp_call(
            order,
            second_b,
            second_t,
            cot_b,
            up_full,
            down_full,
            bias_blocks[:, j].reshape(1, 4 * WIDE),
        )
        acts.append(act)
        ups.append(up_grad)
        downs.append(down_full)
        up_weights.append(up_full)
        bias_parts.append(bias_g.reshape(4, WIDE))
        if pending is not None:
            keep_before, got_before = pending
            sends = plane_sends(after(ids, keep), keep_before, got_before)
            plane_terms.append(plane_swap(sends))
            order_next = sends
        pending = (keep, swap(send, "rep", 1))
        order = after(ids, keep, send)
    qkv_full, out_full = assemble(ids, (qkv_weight, out_weight), attention_plan, attention_pieces)
    gate = after(ids, *order_next) if chunks > 1 else order
    qkv_b = qkv_call(gate, first_b, qkv_full, qkv_b0[None, :], tables)
    keep, got = pending
    sends = plane_sends(after(ids, qkv_b), keep, got)
    plane_terms.append(plane_swap(sends))

    pairs = D // LANES // 3
    earlier = attention_call(after(ids, *sends), 0, pairs, qkv_b, cot_b, out_full, mask, tables, ())
    earlier = attention_call(ids, pairs, pairs, qkv_b, cot_b, out_full, mask, tables, tuple(earlier))
    gate = earlier[0]
    plane_terms = [[after(terms[0], gate)] + terms[1:] for terms in plane_terms]
    sends = shard_sends(plane_terms, z)
    earlier = attention_call(
        after(ids, *sends), 2 * pairs, pairs, qkv_b, cot_b, out_full, mask, tables, tuple(earlier)
    )
    owned = shard_sum([after(sends[0], earlier[0])] + sends[1:])
    mixed_b, grads = earlier
    keep, send, qkv_bias_g = qkv_grad_call(after(ids, owned), grads, first_t, mixed_b, cot_b)
    mlp_parts = share_plane(owned)
    mlp_parts = after(mlp_parts, keep)
    mlp_other = swap(mlp_parts, "rep", 1)

    got = swap(send, "rep", 1)
    output = output_call(
        after(ids, send, mlp_parts),
        hidden_in,
        mixed_b,
        out_full,
        out_b0[None, :],
        down_b0[None, :],
        acts,
        downs,
    )
    sends = plane_sends(after(ids, output), keep, got)
    input_grad, row_sums = input_grad_call(
        after(ids, *sends),
        hidden_in,
        cotangent,
        grads,
        qkv_full,
        gain_1[None, :],
        gain_2[None, :],
        ups,
        up_weights,
    )
    terms = plane_swap(sends)
    terms[0] = after(terms[0], input_grad)
    sends = shard_sends([terms], z)
    up_bias_g = jnp.stack(bias_parts, axis=1).reshape(-1)
    sums = [row_sums[0], row_sums[1], row_sums[2], row_sums[3], qkv_bias_g.reshape(-1), row_sums[4], up_bias_g]
    total = sum_small(pack(sums)).reshape(-1)

    mlp_place = []
    for j in range(chunks):
        first = j * (D // 4)
        mlp_place.append(
            (0, 0, part, first, tuple((2 * own_hidden, b * own_hidden + j * WIDE) for b in range(2)))
        )
        mlp_place.append((1, j * WIDE, deep, first + 2 * part, ((WIDE, 0),)))
    up_weight_g, down_weight_g = place(
        ids, [(own, hidden_units), (own_hidden, D)], mlp_place, after(mlp_parts, *sends), mlp_other
    )
    attention_place = [
        (0, 0, part, 0, tuple((3 * WIDE, b * WIDE) for b in range(3))),
        (1, 0, part, 3 * part, ((WIDE, 0),)),
    ]
    parts = share_plane(shard_sum(sends))
    qkv_weight_g, out_weight_g = place(
        ids, [(own, 3 * D), (own, D)], attention_place, parts, swap(parts, "rep", 1)
    )
    summed, at_row = [], 0
    for s in sums:
        size = s.shape[0] // 4
        summed.append(lax.dynamic_slice(total, (at_row + z * size,), (size,)))
        at_row += s.shape[0]
    return (
        output,
        input_grad,
        summed[0],
        summed[1],
        summed[2],
        summed[3],
        qkv_weight_g,
        summed[4],
        out_weight_g,
        summed[5],
        up_weight_g,
        summed[6],
        down_weight_g,
        summed[5],
    )


def solution(mesh):
    tokens = P(("rep", "shard"), None)
    matrix, vector = P("shard", None), P("shard")
    params = (vector,) * 4 + (matrix, vector) * 4
    in_specs = (tokens, tokens, P(("rep", "shard"))) + params
    out_specs = (tokens, tokens) + params
    return jax.shard_map(body, mesh=mesh, in_specs=in_specs, out_specs=out_specs, check_vma=False)
```

```python
import functools

import jax
import jax.numpy as jnp
from jax import lax
from jax.experimental import pallas as pl
from jax.experimental.pallas import tpu as pltpu
from jax.sharding import PartitionSpec as P

D = 768
H = 12
HD = 64
ROT = 16
WIDE = 384
LANES = 128
F32, BF16 = jnp.float32, jnp.bfloat16
norm_eps = 1e-05


def compiler_params(mib):
    return pltpu.CompilerParams(vmem_limit_bytes=mib * 2**20)


def cost(microseconds):
    return pl.CostEstimate(
        flops=int(microseconds * 1.1e9), bytes_accessed=int(microseconds * 1e5), transcendentals=0
    )


VMEM = pl.BlockSpec(memory_space=pltpu.VMEM)
SMEM = pl.BlockSpec(memory_space=pltpu.SMEM)


def swap(value, axis, bit):
    size = lax.axis_size(axis)
    return lax.ppermute(value, axis, [(i, i ^ bit) for i in range(size)])


def place_ids():
    rep = lax.axis_index("rep").astype(jnp.uint32)
    return lax.axis_index("shard").astype(jnp.uint32), (rep >> 1) & 3, rep & 1


def after(value, *others):
    return lax.optimization_barrier((value, *others))[0]


def gather_far(piece):
    return jnp.stack([swap(piece, "shard", k) for k in (1, 2, 3)])


def far_of(near, rest):
    return jnp.concatenate([near[None], rest])


def gather_plane(far):
    return [far] + [swap(far, "rep", j * 2) for j in (1, 2, 3)]


def gather_core(parts):
    parts = jnp.stack(parts)
    return parts, swap(parts, "rep", 1)


def total_of(arrays):
    return (
        (arrays[0].astype(F32) + arrays[1].astype(F32))
        + (arrays[2].astype(F32) + arrays[3].astype(F32))
    ).astype(BF16)


def at(block, index):
    return lax.dynamic_index_in_dim(block, index, 0, keepdims=False)


def plane_sum_body(ids_ref, keep_ref, got_ref, *outs):
    q = ids_ref[1]
    for j in range(4):
        total = keep_ref[q ^ j].astype(F32) + got_ref[q ^ j].astype(F32)
        outs[j][...] = total.astype(BF16)


def plane_sends(ids, keep, got):
    rows = keep.shape[2]
    block = pl.BlockSpec((4, 1, rows, WIDE), lambda i: (0, i, 0, 0))
    return pl.pallas_call(
        plane_sum_body,
        grid=(4,),
        out_shape=[jax.ShapeDtypeStruct((4, rows, WIDE), BF16)] * 4,
        in_specs=[SMEM, block, block],
        out_specs=[pl.BlockSpec((1, rows, WIDE), lambda i: (i, 0, 0))] * 4,
        compiler_params=compiler_params(40),
        cost_estimate=cost(3),
        name="plane_sum",
    )(ids, keep, got)


def plane_swap(sends):
    return [sends[0]] + [swap(sends[j], "rep", j * 2) for j in (1, 2, 3)]


def shard_sends(groups, z):
    return [
        jnp.concatenate([total_of([at(term, z ^ k) for term in terms]) for terms in groups])
        for k in range(4)
    ]


def shard_sum(sends):
    owned = total_of([sends[0]] + [swap(sends[k], "shard", k) for k in (1, 2, 3)])
    bit = 8
    while bit < lax.axis_size("rep"):
        owned = (owned.astype(F32) + swap(owned, "rep", bit).astype(F32)).astype(BF16)
        bit *= 2
    return owned


def share_plane(owned):
    return jnp.stack([owned] + [swap(owned, "rep", j * 2) for j in (1, 2, 3)])


def sum_small(vector):
    bit = 1
    while bit < lax.axis_size("rep"):
        if bit not in (2, 4):
            vector = vector + swap(vector, "rep", bit)
        bit *= 2
    vector = (vector + swap(vector, "rep", 2)) + (swap(vector, "rep", 4) + swap(vector, "rep", 6))
    return (vector + swap(vector, "shard", 1)) + (swap(vector, "shard", 2) + swap(vector, "shard", 3))


def pack(vectors):
    flat = jnp.concatenate([v.reshape(-1) for v in vectors])
    fill = -flat.shape[0] % 1024
    return jnp.concatenate([flat, jnp.zeros((fill,), flat.dtype)]).reshape(-1, LANES)


def assemble_body(plan, ids_ref, *refs):
    count = len(plan)
    shards, pieces, outs = refs[:count], refs[count : count + 2], refs[count + 2 :]
    z, q, c = ids_ref[0], ids_ref[1], ids_ref[2]
    for shard_ref, out_ref, (rows, part, first, blocks, row_0, columns) in zip(shards, outs, plan):
        half = blocks * WIDE
        own = pl.ds(pl.multiple_of(z * rows, rows), rows)
        for b, col_0 in enumerate(columns):
            out_ref[own, b * WIDE : (b + 1) * WIDE] = shard_ref[row_0 : row_0 + rows, col_0 : col_0 + WIDE]
        for h, piece in ((c, pieces[0]), (1 - c, pieces[1])):
            for j in range(4):
                for k in (1, 2, 3):
                    row = pl.multiple_of((z ^ k) * rows + (q ^ j) * part, part)
                    for b in range(blocks):
                        col = pl.multiple_of(h * half + b * WIDE, WIDE)
                        start = first + b * part
                        out_ref[pl.ds(row, part), pl.ds(col, WIDE)] = piece[
                            j, k - 1, start : start + part, :
                        ]


def assemble(ids, shards, plan, pieces):
    shapes = [jax.ShapeDtypeStruct((4 * p[0], 2 * p[3] * WIDE), BF16) for p in plan]
    return pl.pallas_call(
        functools.partial(assemble_body, plan),
        out_shape=shapes,
        in_specs=[SMEM] + [VMEM] * (len(shards) + 2),
        out_specs=[VMEM] * len(shards),
        compiler_params=compiler_params(40),
        cost_estimate=cost(3),
        name="assemble",
    )(ids, *shards, *pieces)


def pack_small_body(*refs):
    out_ref = refs[-1]
    out_ref[...] = jnp.zeros_like(out_ref)
    for n, ref in enumerate(refs[:-1]):
        out_ref[n : n + 1, : ref.shape[1]] = ref[...].astype(F32)


def unpack_small_body(lengths, ids_ref, *refs):
    near, outs = refs[:4], refs[4:]
    z = ids_ref[0]
    for shard in range(4):
        rows = near[0][...].astype(F32)
        for k in (1, 2, 3):
            rows = jnp.where((z ^ k) == shard, near[k][...].astype(F32), rows)
        for n, (out_ref, length) in enumerate(zip(outs, lengths)):
            out_ref[:, shard * length : (shard + 1) * length] = rows[n : n + 1, :length]


def gather_small(ids, vectors):
    lengths = [v.shape[0] for v in vectors]
    widest = max(lengths)
    packed = pl.pallas_call(
        pack_small_body,
        out_shape=jax.ShapeDtypeStruct((len(vectors), widest), F32),
        in_specs=[VMEM] * len(vectors),
        out_specs=VMEM,
        cost_estimate=cost(1),
        name="pack_small",
    )(*[v[None, :] for v in vectors])
    near = [packed] + [swap(packed, "shard", k) for k in (1, 2, 3)]
    return pl.pallas_call(
        functools.partial(unpack_small_body, lengths),
        out_shape=[jax.ShapeDtypeStruct((1, 4 * n), F32) for n in lengths],
        in_specs=[SMEM] + [VMEM] * 4,
        out_specs=[VMEM] * len(vectors),
        cost_estimate=cost(1),
        name="unpack_small",
    )(ids, *near)


def place_body(plan, ids_ref, parts_ref, other_ref, *outs):
    q, c = ids_ref[1], ids_ref[2]
    for out, rows, part, first, blocks in plan:
        for h, pieces in ((c, parts_ref), (1 - c, other_ref)):
            for j in range(4):
                row = pl.multiple_of(rows + (q ^ j) * part, part)
                for b, (scale, offset) in enumerate(blocks):
                    col = pl.multiple_of(h * scale + offset, WIDE)
                    start = first + b * part
                    outs[out][pl.ds(row, part), pl.ds(col, WIDE)] = pieces[
                        j, start : start + part, :
                    ].astype(F32)


def place(ids, shapes, plan, parts, other):
    return pl.pallas_call(
        functools.partial(place_body, plan),
        out_shape=[jax.ShapeDtypeStruct(s, F32) for s in shapes],
        in_specs=[SMEM, VMEM, VMEM],
        out_specs=[VMEM] * len(shapes),
        compiler_params=compiler_params(40),
        cost_estimate=cost(3),
        name="place",
    )(ids, parts, other)


def dot(left, right, left_dim=1, right_dim=0):
    return lax.dot_general(
        left, right, (((left_dim,), (right_dim,)), ((), ())), preferred_element_type=F32
    )


def turn(values, cosine, early, late):
    width = values.shape[1]
    return (
        values * cosine
        + pltpu.roll(values, width - ROT // 2, 1) * early
        + pltpu.roll(values, ROT // 2, 1) * late
    )


def qkv_body(gate_ref, x_ref, w_ref, bias_ref, cos_ref, early_ref, late_ref, out_ref):
    values = dot(x_ref[...], w_ref[...]) + bias_ref[...]

    @pl.when(pl.program_id(0) < 4)
    def rotate_block():
        for b in range(WIDE // LANES):
            cols = slice(b * LANES, (b + 1) * LANES)
            out_ref[:, cols] = turn(
                values[:, cols], cos_ref[...], early_ref[...], late_ref[...]
            ).astype(BF16)

    @pl.when(pl.program_id(0) >= 4)
    def plain_block():
        out_ref[...] = values.astype(BF16)


def qkv_call(gate, first_b, weight, bias, tables):
    tokens = first_b.shape[0]
    whole = lambda r, c: pl.BlockSpec((r, c), lambda i: (0, 0))
    return pl.pallas_call(
        qkv_body,
        grid=(3 * D // WIDE,),
        out_shape=jax.ShapeDtypeStruct((tokens, 3 * D), BF16),
        in_specs=[
            SMEM,
            whole(tokens, D),
            pl.BlockSpec((D, WIDE), lambda i: (0, i)),
            pl.BlockSpec((1, WIDE), lambda i: (0, i)),
        ]
        + [whole(tokens, LANES)] * 3,
        out_specs=pl.BlockSpec((tokens, WIDE), lambda i: (0, i)),
        compiler_params=compiler_params(40),
        cost_estimate=cost(11),
        name="qkv",
    )(gate, first_b, weight, bias, *tables)


def attention_body(
    first_call, gate_ref, q_ref, k_ref, v_ref, cot_ref, w_ref, mask_ref, cos_ref, early_ref, late_ref, *refs
):
    mixed_ref, grad_ref, key_t_ref, value_t_ref = refs if first_call else refs[2:]
    tokens = q_ref.shape[0]
    step = min(256, tokens)
    out_grad = dot(cot_ref[...], w_ref[...], 1, 1).astype(BF16)
    lane = lax.broadcasted_iota(jnp.int32, (tokens, LANES), 1)
    query_t = q_ref[...].astype(F32).T.astype(BF16)
    out_grad_t = out_grad.astype(F32).T.astype(BF16)
    nothing = jnp.zeros((tokens, LANES), BF16)
    keys = k_ref[...] * BF16(HD**-0.5)
    heads = []
    for h in range(2):
        here = (lane // HD) == h
        heads.append((jnp.where(here, keys, nothing), jnp.where(here, v_ref[...], nothing)))
    key_t_ref[...] = jnp.zeros_like(key_t_ref)
    value_t_ref[...] = jnp.zeros_like(value_t_ref)
    for first in range(0, tokens, step):
        last = first + step
        block = slice(first, last)
        mixed = jnp.zeros((step, LANES), F32)
        query_grad = jnp.zeros((step, LANES), F32)
        for h in range(2):
            key, value = heads[h][0][:last], heads[h][1][:last]
            rows = slice(h * HD, (h + 1) * HD)
            scores = dot(q_ref[block, :], key, 1, 1) + mask_ref[block, :last]
            expo = jnp.exp(scores - jnp.max(scores, axis=1, keepdims=True))
            probs = expo * (1.0 / jnp.sum(expo, axis=1, keepdims=True))
            probs_b = probs.astype(BF16)
            mixed += dot(probs_b, value)
            probs_grad = dot(out_grad[block], value, 1, 1)
            weighted = probs_grad * probs
            scores_grad = (weighted - probs * jnp.sum(weighted, axis=1, keepdims=True)).astype(BF16)
            query_grad += dot(scores_grad, key)
            key_t_ref[rows, :last] += dot(query_t[rows, block], scores_grad)
            value_t_ref[rows, :last] += dot(out_grad_t[rows, block], probs_b)
        mixed_ref[block, :] = mixed.astype(BF16)
        grad_ref[0, block, :] = turn(
            query_grad, cos_ref[block, :], -early_ref[block, :], -late_ref[block, :]
        ).astype(BF16)
    grad_ref[1, :, :] = turn(
        key_t_ref[...].T * HD**-0.5, cos_ref[...], -early_ref[...], -late_ref[...]
    ).astype(BF16)
    grad_ref[2, :, :] = value_t_ref[...].T.astype(BF16)


def attention_call(gate, start, pairs, qkv_b, cot_b, out_weight, mask, tables, earlier):
    tokens = qkv_b.shape[0]
    every = D // LANES
    whole = lambda r, c: pl.BlockSpec((r, c), lambda i: (0, 0))
    part = lambda n: pl.BlockSpec((tokens, LANES), lambda i: (0, n * every + start + i))
    anywhere = pl.BlockSpec(memory_space=pl.ANY)
    return pl.pallas_call(
        functools.partial(attention_body, not earlier),
        grid=(pairs,),
        out_shape=[
            jax.ShapeDtypeStruct((tokens, D), BF16),
            jax.ShapeDtypeStruct((3, tokens, D), BF16),
        ],
        in_specs=[
            SMEM,
            part(0),
            part(1),
            part(2),
            whole(tokens, D),
            pl.BlockSpec((LANES, D), lambda i: (start + i, 0)),
            whole(tokens, tokens),
        ]
        + [whole(tokens, LANES)] * 3
        + [anywhere] * len(earlier),
        out_specs=[
            pl.BlockSpec((tokens, LANES), lambda i: (0, start + i)),
            pl.BlockSpec((3, tokens, LANES), lambda i: (0, 0, start + i)),
        ],
        scratch_shapes=[
            pltpu.VMEM((LANES, tokens), F32),
            pltpu.VMEM((LANES, tokens), F32),
        ],
        input_output_aliases={10: 0, 11: 1} if earlier else {},
        compiler_params=compiler_params(56),
        cost_estimate=cost(9 * pairs),
        name="attention",
    )(gate, qkv_b, qkv_b, qkv_b, cot_b, out_weight, mask, *tables, *earlier)


def store_block(keep_ref, send_ref, here, block, part, row):
    def store(ref):
        for z in range(4):
            for q in range(4):
                start = (z * 4 + q) * part
                ref[q, z, pl.ds(row, part), :] = block[start : start + part, :]

    pl.when(here)(lambda: store(keep_ref))
    pl.when(jnp.logical_not(here))(lambda: store(send_ref))


def qkv_grad_body(ids_ref, grad_ref, first_t_ref, mixed_ref, cot_ref, keep_ref, send_ref, bias_ref):
    step = pl.program_id(0)
    grad = grad_ref[0]
    h, b = step // 3, step % 3
    here = h == ids_ref[2]
    part = D // 16
    block = dot(first_t_ref[...], grad).astype(BF16)
    store_block(keep_ref, send_ref, here, block, part, pl.multiple_of(b * part, part))
    bias_ref[...] = jnp.sum(grad.astype(F32), axis=0, keepdims=True)

    @pl.when(b == 0)
    def out_part():
        block = dot(mixed_ref[...], cot_ref[...], 0, 0).astype(BF16)
        store_block(keep_ref, send_ref, here, block, part, 3 * part)


def qkv_grad_call(ids, grads, first_t, mixed_b, cot_b):
    tokens = cot_b.shape[0]
    whole = lambda r, c: pl.BlockSpec((r, c), lambda i: (0, 0))
    pack_spec = pl.BlockSpec((4, 4, D // 4, WIDE), lambda i: (0, 0, 0, 0))
    return pl.pallas_call(
        qkv_grad_body,
        grid=(3 * D // WIDE,),
        out_shape=[
            jax.ShapeDtypeStruct((4, 4, D // 4, WIDE), BF16),
            jax.ShapeDtypeStruct((4, 4, D // 4, WIDE), BF16),
            jax.ShapeDtypeStruct((1, 3 * D), F32),
        ],
        in_specs=[
            SMEM,
            pl.BlockSpec((1, tokens, WIDE), lambda i: (i // 2, 0, i % 2)),
            whole(D, tokens),
            whole(tokens, D),
            pl.BlockSpec((tokens, WIDE), lambda i: (0, i // 3)),
        ],
        out_specs=[pack_spec, pack_spec, pl.BlockSpec((1, WIDE), lambda i: (0, i))],
        compiler_params=compiler_params(56),
        cost_estimate=cost(14),
        name="qkv_grad",
    )(ids, grads, first_t, mixed_b, cot_b)


def mlp_body(
    ids_ref, x_ref, x_t_ref, cot_ref, up_ref, down_ref, bias_ref,
    act_ref, grad_ref, keep_ref, send_ref, bias_grad_ref,
):
    step = pl.program_id(0)
    tokens = x_ref.shape[0]
    rows = min(256, tokens)
    total = jnp.zeros((1, WIDE), F32)
    for first in range(0, tokens, rows):
        block = slice(first, first + rows)
        up = dot(x_ref[block, :], up_ref[...]) + bias_ref[...]
        act_grad = dot(cot_ref[block, :], down_ref[...], 1, 1)
        below = 0.5 + 0.5 * lax.erf(up * (0.5**0.5))
        slope = below + up * (jnp.exp(-0.5 * up * up) * 0.3989422804014327)
        up_grad = (act_grad * slope).astype(BF16)
        act_ref[block, :] = (up * below).astype(BF16)
        grad_ref[block, :] = up_grad
        total += jnp.sum(up_grad.astype(F32), axis=0, keepdims=True)
    bias_grad_ref[...] = total
    part = D // 16
    c = ids_ref[2]
    block = dot(x_t_ref[...], grad_ref[...]).astype(BF16)
    store_block(
        keep_ref, send_ref, step // 2 == c, block, part, pl.multiple_of((step % 2) * part, part)
    )
    down = dot(act_ref[...], cot_ref[...], 0, 0).astype(BF16)
    deep = WIDE // 4

    def store_down(keep, send):
        for q in range(4):
            rows_here = slice(q * deep, (q + 1) * deep)
            keep_ref[q, step, 2 * part :, :] = down[rows_here, keep * WIDE : (keep + 1) * WIDE]
            send_ref[q, step, 2 * part :, :] = down[rows_here, send * WIDE : (send + 1) * WIDE]

    pl.when(c == 0)(lambda: store_down(0, 1))
    pl.when(c == 1)(lambda: store_down(1, 0))


def mlp_call(ids, second_b, second_t, cot_b, up_weight, down_weight, bias, chunk, chunks):
    tokens = cot_b.shape[0]
    whole = lambda r, c: pl.BlockSpec((r, c), lambda i: (0, 0))
    column = pl.BlockSpec((tokens, WIDE), lambda i: (0, i))
    pack_spec = pl.BlockSpec((4, 4, D // 4, WIDE), lambda i: (0, 0, 0, 0))
    return pl.pallas_call(
        mlp_body,
        grid=(4,),
        out_shape=[
            jax.ShapeDtypeStruct((tokens, 4 * WIDE), BF16),
            jax.ShapeDtypeStruct((tokens, 4 * WIDE), BF16),
            jax.ShapeDtypeStruct((4, 4, D // 4, WIDE), BF16),
            jax.ShapeDtypeStruct((4, 4, D // 4, WIDE), BF16),
            jax.ShapeDtypeStruct((1, 4 * WIDE), F32),
        ],
        in_specs=[
            SMEM,
            whole(tokens, D),
            whole(D, tokens),
            whole(tokens, D),
            pl.BlockSpec((D, WIDE), lambda i: (0, i)),
            pl.BlockSpec((WIDE, D), lambda i: (i, 0)),
            pl.BlockSpec((1, WIDE), lambda i: (0, i * chunks + chunk)),
        ],
        out_specs=[column, column, pack_spec, pack_spec, pl.BlockSpec((1, WIDE), lambda i: (0, i))],
        compiler_params=compiler_params(56),
        cost_estimate=cost(20),
        name="mlp",
    )(ids, second_b, second_t, cot_b, up_weight, down_weight, bias)


def output_body(count, gate_ref, hidden_ref, mixed_ref, out_w_ref, out_bias_ref, down_bias_ref, *refs):
    acts, downs, out_ref = refs[:count], refs[count : 2 * count], refs[2 * count]
    wide = dot(acts[0][...], downs[0][...])
    for a, w in zip(acts[1:], downs[1:]):
        wide += dot(a[...], w[...])
    attention = dot(mixed_ref[...], out_w_ref[...]) + out_bias_ref[...]
    out_ref[...] = hidden_ref[...] + attention + (wide + down_bias_ref[...])


def output_call(gate, hidden, mixed_b, out_weight, out_bias, down_bias, acts, downs):
    tokens = hidden.shape[0]
    rows = min(256, tokens)
    row = lambda c: pl.BlockSpec((rows, c), lambda i: (i, 0))
    whole = lambda a: pl.BlockSpec(a.shape, lambda i: (0, 0))
    return pl.pallas_call(
        functools.partial(output_body, len(acts)),
        grid=(tokens // rows,),
        out_shape=jax.ShapeDtypeStruct((tokens, D), F32),
        in_specs=[SMEM, row(D), row(D), whole(out_weight), whole(out_bias), whole(down_bias)]
        + [row(a.shape[1]) for a in acts]
        + [whole(w) for w in downs],
        out_specs=row(D),
        compiler_params=compiler_params(56),
        cost_estimate=cost(10),
        name="output",
    )(gate, hidden, mixed_b, out_weight, out_bias, down_bias, *acts, *downs)


def input_grad_body(count, gate_ref, hidden_ref, cot_ref, grad_ref, w_ref, gain_1_ref, gain_2_ref, *refs):
    ups, weights, out_ref, sums_ref = refs[:count], refs[count : 2 * count], refs[2 * count], refs[2 * count + 1]
    first = dot(grad_ref[0], w_ref[:, :D], 1, 1)
    for n in (1, 2):
        first += dot(grad_ref[n], w_ref[:, n * D : (n + 1) * D], 1, 1)
    second = dot(ups[0][...], weights[0][...], 1, 1)
    for u, w in zip(ups[1:], weights[1:]):
        second += dot(u[...], w[...], 1, 1)
    normed, scale = normalize(hidden_ref[...])
    cot = cot_ref[...]
    inner = first * gain_1_ref[...] + second * gain_2_ref[...]
    out_ref[...] = cot + scale * (
        inner
        - jnp.mean(inner, axis=-1, keepdims=True)
        - normed * jnp.mean(inner * normed, axis=-1, keepdims=True)
    )

    @pl.when(pl.program_id(0) == 0)
    def clear():
        sums_ref[...] = jnp.zeros_like(sums_ref)

    for n, value in enumerate((first * normed, first, second * normed, second, cot)):
        sums_ref[n : n + 1, :] += jnp.sum(value, axis=0, keepdims=True)


def input_grad_call(gate, hidden, cotangent, grads, weight, gain_1, gain_2, ups, weights):
    tokens = hidden.shape[0]
    rows = min(256, tokens)
    row = lambda c: pl.BlockSpec((rows, c), lambda i: (i, 0))
    whole = lambda a: pl.BlockSpec(a.shape, lambda i: (0, 0))
    return pl.pallas_call(
        functools.partial(input_grad_body, len(ups)),
        grid=(tokens // rows,),
        out_shape=[jax.ShapeDtypeStruct((tokens, D), F32), jax.ShapeDtypeStruct((8, D), F32)],
        in_specs=[
            SMEM,
            row(D),
            row(D),
            pl.BlockSpec((3, rows, D), lambda i: (0, i, 0)),
            whole(weight),
            whole(gain_1),
            whole(gain_2),
        ]
        + [row(u.shape[1]) for u in ups]
        + [whole(w) for w in weights],
        out_specs=[row(D), pl.BlockSpec((8, D), lambda i: (0, 0))],
        compiler_params=compiler_params(56),
        cost_estimate=cost(14),
        name="input_grad",
    )(gate, hidden, cotangent, grads, weight, gain_1, gain_2, *ups, *weights)


def normalize(values):
    centre = values - jnp.mean(values, axis=-1, keepdims=True)
    scale = lax.rsqrt(jnp.mean(centre * centre, axis=-1, keepdims=True) + norm_eps)
    return centre * scale, scale


def first_body(
    gate_ref, hidden_ref, cot_ref, seg_col_ref, seg_row_ref, gain_1_ref, shift_1_ref, gain_2_ref, shift_2_ref,
    first_ref, second_ref, first_t_ref, second_t_ref, cot_b_ref, mask_ref, places_ref,
):
    normed, _ = normalize(hidden_ref[...])
    first = (normed * gain_1_ref[...] + shift_1_ref[...]).astype(BF16)
    second = (normed * gain_2_ref[...] + shift_2_ref[...]).astype(BF16)
    first_ref[...] = first
    second_ref[...] = second
    first_t_ref[...] = first.astype(F32).T.astype(BF16)
    second_t_ref[...] = second.astype(F32).T.astype(BF16)
    cot_b_ref[...] = cot_ref[...].astype(BF16)
    rows, tokens = mask_ref.shape
    row = pl.program_id(0) * rows + lax.broadcasted_iota(jnp.int32, (rows, tokens), 0)
    col = lax.broadcasted_iota(jnp.int32, (rows, tokens), 1)
    mine, others = seg_col_ref[...], seg_row_ref[...]
    mask_ref[...] = jnp.where((mine == others) & (col <= row), 0.0, -1e30)
    before = jnp.sum(jnp.where(mine > others, 1.0, 0.0), axis=1, keepdims=True)
    places_ref[...] = row[:, :LANES].astype(F32) - before


def first_call(gate, hidden, cotangent, segments, vectors):
    tokens = hidden.shape[0]
    rows = min(256, tokens)
    row = lambda c: pl.BlockSpec((rows, c), lambda i: (i, 0))
    turned = pl.BlockSpec((D, rows), lambda i: (0, i))
    whole = lambda r, c: pl.BlockSpec((r, c), lambda i: (0, 0))
    wide = jax.ShapeDtypeStruct((tokens, D), BF16)
    tall = jax.ShapeDtypeStruct((D, tokens), BF16)
    return pl.pallas_call(
        first_body,
        grid=(tokens // rows,),
        out_shape=[
            wide,
            wide,
            tall,
            tall,
            wide,
            jax.ShapeDtypeStruct((tokens, tokens), F32),
            jax.ShapeDtypeStruct((tokens, LANES), F32),
        ],
        in_specs=[SMEM, row(D), row(D), row(1), whole(1, tokens)] + [whole(1, D)] * 4,
        out_specs=[row(D), row(D), turned, turned, row(D), row(tokens), row(LANES)],
        compiler_params=compiler_params(40),
        cost_estimate=cost(12),
        name="first",
    )(
        gate,
        hidden,
        cotangent,
        segments[:, None],
        segments[None, :],
        *vectors,
    )


def rotary_tables(places):
    half = ROT // 2
    lane = jnp.arange(LANES, dtype=jnp.int32) % HD
    freqs = 1.0 / 10000.0 ** ((lane % half).astype(F32) * 2.0 / ROT)
    angles = places * freqs[None, :]
    cosine, sine = jnp.cos(angles), jnp.sin(angles)
    turned, early = (lane < ROT)[None, :], (lane < half)[None, :]
    return (
        jnp.where(turned, cosine, 1.0),
        jnp.where(early, -sine, 0.0),
        jnp.where(turned & ~early, sine, 0.0),
    )


def take(array, row, col, rows, cols):
    return lax.dynamic_slice(array, (row, col), (rows, cols))


def body(
    hidden_in,
    cotangent,
    seg_ids,
    first_gain,
    first_shift,
    second_gain,
    second_shift,
    qkv_weight,
    qkv_bias,
    out_weight,
    out_bias,
    up_weight,
    up_bias,
    down_weight,
    down_bias,
):
    z, q, c = place_ids()
    ids = jnp.stack([z, q, c]).astype(jnp.int32)
    own = qkv_weight.shape[0]
    part = own // 4
    hidden_units = up_weight.shape[1]
    own_hidden = down_weight.shape[0]
    chunks = own_hidden // WIDE
    deep = WIDE // 4
    weight_pieces = []
    for j in range(chunks):
        weight_pieces.append(
            jnp.concatenate(
                [take(up_weight, q * part, (2 * c + b) * own_hidden + j * WIDE, part, WIDE) for b in range(2)]
                + [take(down_weight, j * WIDE + q * deep, c * WIDE, deep, WIDE)]
            )
        )
    weight_pieces.append(
        jnp.concatenate(
            [take(qkv_weight, q * part, c * 3 * WIDE + b * WIDE, part, WIDE) for b in range(3)]
            + [take(out_weight, q * part, c * WIDE, part, WIDE)]
        )
    )
    attention_plan = (
        (own, part, 0, 3, 0, tuple(b * WIDE for b in range(6))),
        (own, part, 3 * part, 1, 0, (0, WIDE)),
    )
    small = gather_small(
        ids,
        [after(first_gain, weight_pieces[0]), first_shift, second_gain, second_shift]
        + [qkv_bias, out_bias, up_bias, down_bias]
    )
    gain_1, shift_1, gain_2, shift_2, qkv_b0, out_b0, up_b0, down_b0 = small

    far = gather_far(weight_pieces[0])
    parts = gather_plane(far)
    weight_pieces = [after(p, far) for p in weight_pieces[1:]]
    near = [swap(p, "shard", 1) for p in weight_pieces]
    onward = [jnp.stack([p, n]) for p, n in zip(weight_pieces, near)]
    first_b, second_b, first_t, second_t, cot_b, mask, places = first_call(
        after(ids, far, *onward), hidden_in, cotangent, seg_ids, small[:4]
    )
    coming = swap(onward[0], "shard", 2)
    done = first_b
    tables = rotary_tables(places)

    acts, ups, downs, up_weights, bias_parts, plane_terms, pending = [], [], [], [], [], [], None
    order = ids
    for j in range(chunks):
        coming = after(coming, done)
        pieces = gather_core([after(p, done, coming) for p in parts])
        far = far_of(near[j], coming)
        parts = gather_plane(far)
        if j + 1 < len(near):
            coming = swap(after(onward[j + 1], far), "shard", 2)
        order = after(order, far)
        mlp_plan = (
            (own, part, 0, 2, 0, tuple(b * own_hidden + j * WIDE for b in range(4))),
            (WIDE, deep, 2 * part, 1, j * WIDE, (0, WIDE)),
        )
        up_full, down_full = assemble(ids, (up_weight, down_weight), mlp_plan, pieces)
        act, up_grad, keep, send, bias_g = mlp_call(
            order,
            second_b,
            second_t,
            cot_b,
            up_full,
            down_full,
            up_b0,
            j,
            chunks,
        )
        done = keep
        acts.append(act)
        ups.append(up_grad)
        downs.append(down_full)
        up_weights.append(up_full)
        bias_parts.append(bias_g.reshape(4, WIDE))
        if pending is not None:
            keep_before, got_before = pending
            sends = plane_sends(after(ids, keep), keep_before, got_before)
            plane_terms.append(plane_swap(sends))
            order_next = sends
        pending = (keep, swap(send, "rep", 1))
        order = after(ids, keep, send)
    pieces = gather_core([after(p, done) for p in parts])
    qkv_full, out_full = assemble(ids, (qkv_weight, out_weight), attention_plan, pieces)
    gate = after(ids, *order_next) if chunks > 1 else order
    qkv_b = qkv_call(gate, first_b, qkv_full, qkv_b0, tables)
    keep, got = pending
    sends = plane_sends(after(ids, qkv_b), keep, got)
    plane_terms.append(plane_swap(sends))

    pairs = D // LANES // 3
    earlier = attention_call(after(ids, *sends), 0, pairs, qkv_b, cot_b, out_full, mask, tables, ())
    earlier = attention_call(ids, pairs, pairs, qkv_b, cot_b, out_full, mask, tables, tuple(earlier))
    gate = earlier[0]
    plane_terms = [[after(terms[0], gate)] + terms[1:] for terms in plane_terms]
    sends = shard_sends(plane_terms, z)
    earlier = attention_call(
        after(ids, *sends), 2 * pairs, pairs, qkv_b, cot_b, out_full, mask, tables, tuple(earlier)
    )
    owned = shard_sum([after(sends[0], earlier[0])] + sends[1:])
    mixed_b, grads = earlier
    keep, send, qkv_bias_g = qkv_grad_call(after(ids, owned), grads, first_t, mixed_b, cot_b)
    owned = after(owned, keep)
    shared = [owned] + [swap(owned, "rep", j * 2) for j in (1, 2, 3)]
    got = swap(send, "rep", 1)
    input_grad, row_sums = input_grad_call(
        after(ids, send, owned),
        hidden_in,
        cotangent,
        grads,
        qkv_full,
        gain_1,
        gain_2,
        ups,
        up_weights,
    )
    sends = plane_sends(after(ids, input_grad), keep, got)
    terms = plane_swap(sends)
    mlp_parts = jnp.stack([after(s, input_grad) for s in shared])
    mlp_other = swap(mlp_parts, "rep", 1)
    output = output_call(
        after(ids, mlp_parts, *sends), hidden_in, mixed_b, out_full, out_b0, down_b0, acts, downs
    )
    terms[0] = after(terms[0], output)
    sends = shard_sends([terms], z)
    row_sums = after(row_sums, *sends)
    up_bias_g = jnp.stack(after(bias_parts, row_sums), axis=1).reshape(-1)
    qkv_bias_g = after(qkv_bias_g, row_sums).reshape(-1)
    sums = [row_sums[0], row_sums[1], row_sums[2], row_sums[3], qkv_bias_g, row_sums[4], up_bias_g]
    total = sum_small(pack(sums)).reshape(-1)

    mlp_place = []
    for j in range(chunks):
        first = j * (D // 4)
        mlp_place.append(
            (0, 0, part, first, tuple((2 * own_hidden, b * own_hidden + j * WIDE) for b in range(2)))
        )
        mlp_place.append((1, j * WIDE, deep, first + 2 * part, ((WIDE, 0),)))
    up_weight_g, down_weight_g = place(
        ids, [(own, hidden_units), (own_hidden, D)], mlp_place, after(mlp_parts, *sends), mlp_other
    )
    attention_place = [
        (0, 0, part, 0, tuple((3 * WIDE, b * WIDE) for b in range(3))),
        (1, 0, part, 3 * part, ((WIDE, 0),)),
    ]
    parts = share_plane(shard_sum(sends))
    qkv_weight_g, out_weight_g = place(
        ids, [(own, 3 * D), (own, D)], attention_place, parts, swap(parts, "rep", 1)
    )
    summed, at_row = [], 0
    for s in sums:
        size = s.shape[0] // 4
        summed.append(lax.dynamic_slice(total, (at_row + z * size,), (size,)))
        at_row += s.shape[0]
    return (
        output,
        input_grad,
        summed[0],
        summed[1],
        summed[2],
        summed[3],
        qkv_weight_g,
        summed[4],
        out_weight_g,
        summed[5],
        up_weight_g,
        summed[6],
        down_weight_g,
        summed[5],
    )


def solution(mesh):
    tokens = P(("rep", "shard"), None)
    matrix, vector = P("shard", None), P("shard")
    params = (vector,) * 4 + (matrix, vector) * 4
    in_specs = (tokens, tokens, P(("rep", "shard"))) + params
    out_specs = (tokens, tokens) + params
    return jax.shard_map(body, mesh=mesh, in_specs=in_specs, out_specs=out_specs, check_vma=False)
```

```python
import functools

import jax
import jax.numpy as jnp
from jax import lax
from jax.experimental import pallas as pl
from jax.experimental.pallas import tpu as pltpu
from jax.sharding import PartitionSpec as P

D = 768
H = 12
HD = 64
ROT = 16
WIDE = 384
LANES = 128
F32, BF16 = jnp.float32, jnp.bfloat16
norm_eps = 1e-05


def compiler_params(mib):
    return pltpu.CompilerParams(vmem_limit_bytes=mib * 2**20)


def cost(microseconds):
    return pl.CostEstimate(
        flops=int(microseconds * 1.1e9), bytes_accessed=int(microseconds * 1e5), transcendentals=0
    )


VMEM = pl.BlockSpec(memory_space=pltpu.VMEM)
SMEM = pl.BlockSpec(memory_space=pltpu.SMEM)


def swap(value, axis, bit):
    size = lax.axis_size(axis)
    return lax.ppermute(value, axis, [(i, i ^ bit) for i in range(size)])


def place_ids():
    rep = lax.axis_index("rep").astype(jnp.uint32)
    return lax.axis_index("shard").astype(jnp.uint32), (rep >> 1) & 3, rep & 1


def after(value, *others):
    return lax.optimization_barrier((value, *others))[0]


def gather_far(piece):
    return jnp.stack([swap(piece, "shard", k) for k in (1, 2, 3)])


def far_of(near, rest):
    return jnp.concatenate([near[None], rest])


def gather_plane(far):
    return [far] + [swap(far, "rep", j * 2) for j in (1, 2, 3)]


def gather_core(parts):
    parts = jnp.stack(parts)
    return parts, swap(parts, "rep", 1)


def total_of(arrays):
    return (
        (arrays[0].astype(F32) + arrays[1].astype(F32))
        + (arrays[2].astype(F32) + arrays[3].astype(F32))
    ).astype(BF16)


def at(block, index):
    return lax.dynamic_index_in_dim(block, index, 0, keepdims=False)


def plane_sum_body(ids_ref, keep_ref, got_ref, *outs):
    q = ids_ref[1]
    for j in range(4):
        total = keep_ref[q ^ j].astype(F32) + got_ref[q ^ j].astype(F32)
        outs[j][...] = total.astype(BF16)


def plane_sends(ids, keep, got):
    rows = keep.shape[2]
    block = pl.BlockSpec((4, 1, rows, WIDE), lambda i: (0, i, 0, 0))
    return pl.pallas_call(
        plane_sum_body,
        grid=(4,),
        out_shape=[jax.ShapeDtypeStruct((4, rows, WIDE), BF16)] * 4,
        in_specs=[SMEM, block, block],
        out_specs=[pl.BlockSpec((1, rows, WIDE), lambda i: (i, 0, 0))] * 4,
        compiler_params=compiler_params(40),
        cost_estimate=cost(3),
        name="plane_sum",
    )(ids, keep, got)


def plane_swap(sends):
    return [sends[0]] + [swap(sends[j], "rep", j * 2) for j in (1, 2, 3)]


def shard_sends(groups, z):
    return [
        jnp.concatenate([total_of([at(term, z ^ k) for term in terms]) for terms in groups])
        for k in range(4)
    ]


def shard_sum(sends):
    owned = total_of([sends[0]] + [swap(sends[k], "shard", k) for k in (1, 2, 3)])
    bit = 8
    while bit < lax.axis_size("rep"):
        owned = (owned.astype(F32) + swap(owned, "rep", bit).astype(F32)).astype(BF16)
        bit *= 2
    return owned


def share_plane(owned):
    return jnp.stack([owned] + [swap(owned, "rep", j * 2) for j in (1, 2, 3)])


def sum_small(vector):
    bit = 1
    while bit < lax.axis_size("rep"):
        if bit not in (2, 4):
            vector = vector + swap(vector, "rep", bit)
        bit *= 2
    vector = (vector + swap(vector, "rep", 2)) + (swap(vector, "rep", 4) + swap(vector, "rep", 6))
    return (vector + swap(vector, "shard", 1)) + (swap(vector, "shard", 2) + swap(vector, "shard", 3))


def pack(vectors):
    flat = jnp.concatenate([v.reshape(-1) for v in vectors])
    fill = -flat.shape[0] % 1024
    return jnp.concatenate([flat, jnp.zeros((fill,), flat.dtype)]).reshape(-1, LANES)


def assemble_body(plan, ids_ref, *refs):
    count = len(plan)
    shards, pieces, outs = refs[:count], refs[count : count + 2], refs[count + 2 :]
    z, q, c = ids_ref[0], ids_ref[1], ids_ref[2]
    for shard_ref, out_ref, (rows, part, first, blocks, row_0, columns) in zip(shards, outs, plan):
        half = blocks * WIDE
        own = pl.ds(pl.multiple_of(z * rows, rows), rows)
        for b, col_0 in enumerate(columns):
            out_ref[own, b * WIDE : (b + 1) * WIDE] = shard_ref[row_0 : row_0 + rows, col_0 : col_0 + WIDE]
        for h, piece in ((c, pieces[0]), (1 - c, pieces[1])):
            for j in range(4):
                for k in (1, 2, 3):
                    row = pl.multiple_of((z ^ k) * rows + (q ^ j) * part, part)
                    for b in range(blocks):
                        col = pl.multiple_of(h * half + b * WIDE, WIDE)
                        start = first + b * part
                        out_ref[pl.ds(row, part), pl.ds(col, WIDE)] = piece[
                            j, k - 1, start : start + part, :
                        ]


def assemble(ids, shards, plan, pieces):
    shapes = [jax.ShapeDtypeStruct((4 * p[0], 2 * p[3] * WIDE), BF16) for p in plan]
    return pl.pallas_call(
        functools.partial(assemble_body, plan),
        out_shape=shapes,
        in_specs=[SMEM] + [VMEM] * (len(shards) + 2),
        out_specs=[VMEM] * len(shards),
        compiler_params=compiler_params(40),
        cost_estimate=cost(3),
        name="assemble",
    )(ids, *shards, *pieces)


def pack_small_body(*refs):
    out_ref = refs[-1]
    out_ref[...] = jnp.zeros_like(out_ref)
    for n, ref in enumerate(refs[:-1]):
        out_ref[n : n + 1, : ref.shape[1]] = ref[...].astype(F32)


def unpack_small_body(lengths, ids_ref, *refs):
    near, outs = refs[:4], refs[4:]
    z = ids_ref[0]
    for shard in range(4):
        rows = near[0][...].astype(F32)
        for k in (1, 2, 3):
            rows = jnp.where((z ^ k) == shard, near[k][...].astype(F32), rows)
        for n, (out_ref, length) in enumerate(zip(outs, lengths)):
            out_ref[:, shard * length : (shard + 1) * length] = rows[n : n + 1, :length]


def gather_small(ids, vectors, gate):
    lengths = [v.shape[0] for v in vectors]
    widest = max(lengths)
    packed = pl.pallas_call(
        pack_small_body,
        out_shape=jax.ShapeDtypeStruct((len(vectors), widest), F32),
        in_specs=[VMEM] * len(vectors),
        out_specs=VMEM,
        cost_estimate=cost(1),
        name="pack_small",
    )(*[v.astype(F32)[None, :] for v in vectors])
    packed = after(packed, gate)
    near = [packed] + [swap(packed, "shard", k) for k in (1, 2, 3)]
    return pl.pallas_call(
        functools.partial(unpack_small_body, lengths),
        out_shape=[jax.ShapeDtypeStruct((1, 4 * n), F32) for n in lengths],
        in_specs=[SMEM] + [VMEM] * 4,
        out_specs=[VMEM] * len(vectors),
        cost_estimate=cost(1),
        name="unpack_small",
    )(ids, *near)


def place_body(plan, ids_ref, parts_ref, other_ref, *outs):
    q, c = ids_ref[1], ids_ref[2]
    for out, rows, part, first, blocks in plan:
        for h, pieces in ((c, parts_ref), (1 - c, other_ref)):
            for j in range(4):
                row = pl.multiple_of(rows + (q ^ j) * part, part)
                for b, (scale, offset) in enumerate(blocks):
                    col = pl.multiple_of(h * scale + offset, WIDE)
                    start = first + b * part
                    outs[out][pl.ds(row, part), pl.ds(col, WIDE)] = pieces[
                        j, start : start + part, :
                    ].astype(F32)


def place(ids, shapes, plan, parts, other):
    return pl.pallas_call(
        functools.partial(place_body, plan),
        out_shape=[jax.ShapeDtypeStruct(s, F32) for s in shapes],
        in_specs=[SMEM, VMEM, VMEM],
        out_specs=[VMEM] * len(shapes),
        compiler_params=compiler_params(40),
        cost_estimate=cost(3),
        name="place",
    )(ids, parts, other)


def dot(left, right, left_dim=1, right_dim=0):
    return lax.dot_general(
        left, right, (((left_dim,), (right_dim,)), ((), ())), preferred_element_type=F32
    )


def turn(values, cosine, early, late):
    width = values.shape[1]
    return (
        values * cosine
        + pltpu.roll(values, width - ROT // 2, 1) * early
        + pltpu.roll(values, ROT // 2, 1) * late
    )


def qkv_body(gate_ref, x_ref, w_ref, bias_ref, cos_ref, early_ref, late_ref, out_ref):
    values = dot(x_ref[...], w_ref[...]) + bias_ref[...]

    @pl.when(pl.program_id(0) < 4)
    def rotate_block():
        for b in range(WIDE // LANES):
            cols = slice(b * LANES, (b + 1) * LANES)
            out_ref[:, cols] = turn(
                values[:, cols], cos_ref[...], early_ref[...], late_ref[...]
            ).astype(BF16)

    @pl.when(pl.program_id(0) >= 4)
    def plain_block():
        out_ref[...] = values.astype(BF16)


def qkv_call(gate, first_b, weight, bias, tables):
    tokens = first_b.shape[0]
    whole = lambda r, c: pl.BlockSpec((r, c), lambda i: (0, 0))
    return pl.pallas_call(
        qkv_body,
        grid=(3 * D // WIDE,),
        out_shape=jax.ShapeDtypeStruct((tokens, 3 * D), BF16),
        in_specs=[
            SMEM,
            whole(tokens, D),
            pl.BlockSpec((D, WIDE), lambda i: (0, i)),
            pl.BlockSpec((1, WIDE), lambda i: (0, i)),
        ]
        + [whole(tokens, LANES)] * 3,
        out_specs=pl.BlockSpec((tokens, WIDE), lambda i: (0, i)),
        compiler_params=compiler_params(40),
        cost_estimate=cost(11),
        name="qkv",
    )(gate, first_b, weight, bias, *tables)


def attention_body(
    first_call, gate_ref, q_ref, k_ref, v_ref, cot_ref, w_ref, mask_ref, cos_ref, early_ref, late_ref, *refs
):
    mixed_ref, grad_ref, key_t_ref, value_t_ref = refs if first_call else refs[2:]
    tokens = q_ref.shape[0]
    step = min(256, tokens)
    out_grad = dot(cot_ref[...], w_ref[...], 1, 1).astype(BF16)
    lane = lax.broadcasted_iota(jnp.int32, (tokens, LANES), 1)
    query_t = q_ref[...].astype(F32).T.astype(BF16)
    out_grad_t = out_grad.astype(F32).T.astype(BF16)
    nothing = jnp.zeros((tokens, LANES), BF16)
    keys = k_ref[...] * BF16(HD**-0.5)
    heads = []
    for h in range(2):
        here = (lane // HD) == h
        heads.append((jnp.where(here, keys, nothing), jnp.where(here, v_ref[...], nothing)))
    key_t_ref[...] = jnp.zeros_like(key_t_ref)
    value_t_ref[...] = jnp.zeros_like(value_t_ref)
    for first in range(0, tokens, step):
        last = first + step
        block = slice(first, last)
        mixed = jnp.zeros((step, LANES), F32)
        query_grad = jnp.zeros((step, LANES), F32)
        both = range(2)
        keys_h = [heads[h][0][:last] for h in both]
        values_h = [heads[h][1][:last] for h in both]
        bias = mask_ref[block, :last]
        scores = [dot(q_ref[block, :], keys_h[h], 1, 1) + bias for h in both]
        probs_grad = [dot(out_grad[block], values_h[h], 1, 1) for h in both]
        expo = [jnp.exp(s - jnp.max(s, axis=1, keepdims=True)) for s in scores]
        probs = [e * (1.0 / jnp.sum(e, axis=1, keepdims=True)) for e in expo]
        probs_b = [p.astype(BF16) for p in probs]
        weighted = [g * p for g, p in zip(probs_grad, probs)]
        scores_grad = [
            (w - p * jnp.sum(w, axis=1, keepdims=True)).astype(BF16)
            for w, p in zip(weighted, probs)
        ]
        for h in both:
            rows = slice(h * HD, (h + 1) * HD)
            mixed += dot(probs_b[h], values_h[h])
            query_grad += dot(scores_grad[h], keys_h[h])
            key_t_ref[rows, :last] += dot(query_t[rows, block], scores_grad[h])
            value_t_ref[rows, :last] += dot(out_grad_t[rows, block], probs_b[h])
        mixed_ref[block, :] = mixed.astype(BF16)
        grad_ref[0, block, :] = turn(
            query_grad, cos_ref[block, :], -early_ref[block, :], -late_ref[block, :]
        ).astype(BF16)
    grad_ref[1, :, :] = turn(
        key_t_ref[...].T * HD**-0.5, cos_ref[...], -early_ref[...], -late_ref[...]
    ).astype(BF16)
    grad_ref[2, :, :] = value_t_ref[...].T.astype(BF16)


def attention_call(gate, start, pairs, qkv_b, cot_b, out_weight, mask, tables, earlier):
    tokens = qkv_b.shape[0]
    every = D // LANES
    whole = lambda r, c: pl.BlockSpec((r, c), lambda i: (0, 0))
    part = lambda n: pl.BlockSpec((tokens, LANES), lambda i: (0, n * every + start + i))
    anywhere = pl.BlockSpec(memory_space=pl.ANY)
    return pl.pallas_call(
        functools.partial(attention_body, not earlier),
        grid=(pairs,),
        out_shape=[
            jax.ShapeDtypeStruct((tokens, D), BF16),
            jax.ShapeDtypeStruct((3, tokens, D), BF16),
        ],
        in_specs=[
            SMEM,
            part(0),
            part(1),
            part(2),
            whole(tokens, D),
            pl.BlockSpec((LANES, D), lambda i: (start + i, 0)),
            whole(tokens, tokens),
        ]
        + [whole(tokens, LANES)] * 3
        + [anywhere] * len(earlier),
        out_specs=[
            pl.BlockSpec((tokens, LANES), lambda i: (0, start + i)),
            pl.BlockSpec((3, tokens, LANES), lambda i: (0, 0, start + i)),
        ],
        scratch_shapes=[
            pltpu.VMEM((LANES, tokens), F32),
            pltpu.VMEM((LANES, tokens), F32),
        ],
        input_output_aliases={10: 0, 11: 1} if earlier else {},
        compiler_params=compiler_params(56),
        cost_estimate=cost(9 * pairs),
        name="attention",
    )(gate, qkv_b, qkv_b, qkv_b, cot_b, out_weight, mask, *tables, *earlier)


def store_block(keep_ref, send_ref, here, block, part, row):
    def store(ref):
        for z in range(4):
            for q in range(4):
                start = (z * 4 + q) * part
                ref[q, z, pl.ds(row, part), :] = block[start : start + part, :]

    pl.when(here)(lambda: store(keep_ref))
    pl.when(jnp.logical_not(here))(lambda: store(send_ref))


def qkv_grad_body(ids_ref, grad_ref, first_t_ref, mixed_ref, cot_ref, keep_ref, send_ref, bias_ref):
    step = pl.program_id(0)
    grad = grad_ref[0]
    h, b = step // 3, step % 3
    here = h == ids_ref[2]
    part = D // 16
    block = dot(first_t_ref[...], grad).astype(BF16)
    store_block(keep_ref, send_ref, here, block, part, pl.multiple_of(b * part, part))
    bias_ref[...] = jnp.sum(grad.astype(F32), axis=0, keepdims=True)

    @pl.when(b == 0)
    def out_part():
        block = dot(mixed_ref[...], cot_ref[...], 0, 0).astype(BF16)
        store_block(keep_ref, send_ref, here, block, part, 3 * part)


def qkv_grad_call(ids, grads, first_t, mixed_b, cot_b):
    tokens = cot_b.shape[0]
    whole = lambda r, c: pl.BlockSpec((r, c), lambda i: (0, 0))
    pack_spec = pl.BlockSpec((4, 4, D // 4, WIDE), lambda i: (0, 0, 0, 0))
    return pl.pallas_call(
        qkv_grad_body,
        grid=(3 * D // WIDE,),
        out_shape=[
            jax.ShapeDtypeStruct((4, 4, D // 4, WIDE), BF16),
            jax.ShapeDtypeStruct((4, 4, D // 4, WIDE), BF16),
            jax.ShapeDtypeStruct((1, 3 * D), F32),
        ],
        in_specs=[
            SMEM,
            pl.BlockSpec((1, tokens, WIDE), lambda i: (i // 2, 0, i % 2)),
            whole(D, tokens),
            whole(tokens, D),
            pl.BlockSpec((tokens, WIDE), lambda i: (0, i // 3)),
        ],
        out_specs=[pack_spec, pack_spec, pl.BlockSpec((1, WIDE), lambda i: (0, i))],
        compiler_params=compiler_params(56),
        cost_estimate=cost(14),
        name="qkv_grad",
    )(ids, grads, first_t, mixed_b, cot_b)


def mlp_body(
    ids_ref, x_ref, x_t_ref, cot_ref, up_ref, down_ref, bias_ref,
    act_ref, grad_ref, keep_ref, send_ref, bias_grad_ref,
):
    step = pl.program_id(0)
    tokens = x_ref.shape[0]
    rows = min(256, tokens)
    total = jnp.zeros((1, WIDE), F32)
    for first in range(0, tokens, rows):
        block = slice(first, first + rows)
        up = dot(x_ref[block, :], up_ref[...]) + bias_ref[...]
        act_grad = dot(cot_ref[block, :], down_ref[...], 1, 1)
        below = 0.5 + 0.5 * lax.erf(up * (0.5**0.5))
        slope = below + up * (jnp.exp(-0.5 * up * up) * 0.3989422804014327)
        up_grad = (act_grad * slope).astype(BF16)
        act_ref[block, :] = (up * below).astype(BF16)
        grad_ref[block, :] = up_grad
        total += jnp.sum(up_grad.astype(F32), axis=0, keepdims=True)
    bias_grad_ref[...] = total
    part = D // 16
    c = ids_ref[2]
    block = dot(x_t_ref[...], grad_ref[...]).astype(BF16)
    store_block(
        keep_ref, send_ref, step // 2 == c, block, part, pl.multiple_of((step % 2) * part, part)
    )
    down = dot(act_ref[...], cot_ref[...], 0, 0).astype(BF16)
    deep = WIDE // 4

    def store_down(keep, send):
        for q in range(4):
            rows_here = slice(q * deep, (q + 1) * deep)
            keep_ref[q, step, 2 * part :, :] = down[rows_here, keep * WIDE : (keep + 1) * WIDE]
            send_ref[q, step, 2 * part :, :] = down[rows_here, send * WIDE : (send + 1) * WIDE]

    pl.when(c == 0)(lambda: store_down(0, 1))
    pl.when(c == 1)(lambda: store_down(1, 0))


def mlp_call(ids, second_b, second_t, cot_b, up_weight, down_weight, bias, chunk, chunks):
    tokens = cot_b.shape[0]
    whole = lambda r, c: pl.BlockSpec((r, c), lambda i: (0, 0))
    column = pl.BlockSpec((tokens, WIDE), lambda i: (0, i))
    pack_spec = pl.BlockSpec((4, 4, D // 4, WIDE), lambda i: (0, 0, 0, 0))
    return pl.pallas_call(
        mlp_body,
        grid=(4,),
        out_shape=[
            jax.ShapeDtypeStruct((tokens, 4 * WIDE), BF16),
            jax.ShapeDtypeStruct((tokens, 4 * WIDE), BF16),
            jax.ShapeDtypeStruct((4, 4, D // 4, WIDE), BF16),
            jax.ShapeDtypeStruct((4, 4, D // 4, WIDE), BF16),
            jax.ShapeDtypeStruct((1, 4 * WIDE), F32),
        ],
        in_specs=[
            SMEM,
            whole(tokens, D),
            whole(D, tokens),
            whole(tokens, D),
            pl.BlockSpec((D, WIDE), lambda i: (0, i)),
            pl.BlockSpec((WIDE, D), lambda i: (i, 0)),
            pl.BlockSpec((1, WIDE), lambda i: (0, i * chunks + chunk)),
        ],
        out_specs=[column, column, pack_spec, pack_spec, pl.BlockSpec((1, WIDE), lambda i: (0, i))],
        compiler_params=compiler_params(56),
        cost_estimate=cost(20),
        name="mlp",
    )(ids, second_b, second_t, cot_b, up_weight, down_weight, bias)


def output_body(count, gate_ref, hidden_ref, mixed_ref, out_w_ref, out_bias_ref, down_bias_ref, *refs):
    acts, downs, out_ref = refs[:count], refs[count : 2 * count], refs[2 * count]
    wide = dot(acts[0][...], downs[0][...])
    for a, w in zip(acts[1:], downs[1:]):
        wide += dot(a[...], w[...])
    attention = dot(mixed_ref[...], out_w_ref[...]) + out_bias_ref[...]
    out_ref[...] = hidden_ref[...] + attention + (wide + down_bias_ref[...])


def output_call(gate, hidden, mixed_b, out_weight, out_bias, down_bias, acts, downs):
    tokens = hidden.shape[0]
    rows = min(256, tokens)
    row = lambda c: pl.BlockSpec((rows, c), lambda i: (i, 0))
    whole = lambda a: pl.BlockSpec(a.shape, lambda i: (0, 0))
    return pl.pallas_call(
        functools.partial(output_body, len(acts)),
        grid=(tokens // rows,),
        out_shape=jax.ShapeDtypeStruct((tokens, D), F32),
        in_specs=[SMEM, row(D), row(D), whole(out_weight), whole(out_bias), whole(down_bias)]
        + [row(a.shape[1]) for a in acts]
        + [whole(w) for w in downs],
        out_specs=row(D),
        compiler_params=compiler_params(56),
        cost_estimate=cost(10),
        name="output",
    )(gate, hidden, mixed_b, out_weight, out_bias, down_bias, *acts, *downs)


def input_grad_body(count, gate_ref, hidden_ref, cot_ref, grad_ref, w_ref, gain_1_ref, gain_2_ref, *refs):
    ups, weights, out_ref, sums_ref = refs[:count], refs[count : 2 * count], refs[2 * count], refs[2 * count + 1]
    first = dot(grad_ref[0], w_ref[:, :D], 1, 1)
    for n in (1, 2):
        first += dot(grad_ref[n], w_ref[:, n * D : (n + 1) * D], 1, 1)
    second = dot(ups[0][...], weights[0][...], 1, 1)
    for u, w in zip(ups[1:], weights[1:]):
        second += dot(u[...], w[...], 1, 1)
    normed, scale = normalize(hidden_ref[...])
    cot = cot_ref[...]
    inner = first * gain_1_ref[...] + second * gain_2_ref[...]
    out_ref[...] = cot + scale * (
        inner
        - jnp.mean(inner, axis=-1, keepdims=True)
        - normed * jnp.mean(inner * normed, axis=-1, keepdims=True)
    )

    @pl.when(pl.program_id(0) == 0)
    def clear():
        sums_ref[...] = jnp.zeros_like(sums_ref)

    for n, value in enumerate((first * normed, first, second * normed, second, cot)):
        sums_ref[n : n + 1, :] += jnp.sum(value, axis=0, keepdims=True)


def input_grad_call(gate, hidden, cotangent, grads, weight, gain_1, gain_2, ups, weights):
    tokens = hidden.shape[0]
    rows = min(256, tokens)
    row = lambda c: pl.BlockSpec((rows, c), lambda i: (i, 0))
    whole = lambda a: pl.BlockSpec(a.shape, lambda i: (0, 0))
    return pl.pallas_call(
        functools.partial(input_grad_body, len(ups)),
        grid=(tokens // rows,),
        out_shape=[jax.ShapeDtypeStruct((tokens, D), F32), jax.ShapeDtypeStruct((8, D), F32)],
        in_specs=[
            SMEM,
            row(D),
            row(D),
            pl.BlockSpec((3, rows, D), lambda i: (0, i, 0)),
            whole(weight),
            whole(gain_1),
            whole(gain_2),
        ]
        + [row(u.shape[1]) for u in ups]
        + [whole(w) for w in weights],
        out_specs=[row(D), pl.BlockSpec((8, D), lambda i: (0, 0))],
        compiler_params=compiler_params(56),
        cost_estimate=cost(14),
        name="input_grad",
    )(gate, hidden, cotangent, grads, weight, gain_1, gain_2, *ups, *weights)


def normalize(values):
    centre = values - jnp.mean(values, axis=-1, keepdims=True)
    scale = lax.rsqrt(jnp.mean(centre * centre, axis=-1, keepdims=True) + norm_eps)
    return centre * scale, scale


def first_body(
    gate_ref, hidden_ref, cot_ref, seg_col_ref, seg_row_ref, gain_1_ref, shift_1_ref, gain_2_ref, shift_2_ref,
    first_ref, second_ref, first_t_ref, second_t_ref, cot_b_ref, mask_ref, places_ref,
):
    normed, _ = normalize(hidden_ref[...])
    first = (normed * gain_1_ref[...] + shift_1_ref[...]).astype(BF16)
    second = (normed * gain_2_ref[...] + shift_2_ref[...]).astype(BF16)
    first_ref[...] = first
    second_ref[...] = second
    first_t_ref[...] = first.astype(F32).T.astype(BF16)
    second_t_ref[...] = second.astype(F32).T.astype(BF16)
    cot_b_ref[...] = cot_ref[...].astype(BF16)
    rows, tokens = mask_ref.shape
    row = pl.program_id(0) * rows + lax.broadcasted_iota(jnp.int32, (rows, tokens), 0)
    col = lax.broadcasted_iota(jnp.int32, (rows, tokens), 1)
    mine, others = seg_col_ref[...], seg_row_ref[...]
    mask_ref[...] = jnp.where((mine == others) & (col <= row), 0.0, -1e30)
    before = jnp.sum(jnp.where(mine > others, 1.0, 0.0), axis=1, keepdims=True)
    places_ref[...] = row[:, :LANES].astype(F32) - before


def first_call(gate, hidden, cotangent, segments, vectors):
    tokens = hidden.shape[0]
    rows = min(256, tokens)
    row = lambda c: pl.BlockSpec((rows, c), lambda i: (i, 0))
    turned = pl.BlockSpec((D, rows), lambda i: (0, i))
    whole = lambda r, c: pl.BlockSpec((r, c), lambda i: (0, 0))
    wide = jax.ShapeDtypeStruct((tokens, D), BF16)
    tall = jax.ShapeDtypeStruct((D, tokens), BF16)
    return pl.pallas_call(
        first_body,
        grid=(tokens // rows,),
        out_shape=[
            wide,
            wide,
            tall,
            tall,
            wide,
            jax.ShapeDtypeStruct((tokens, tokens), F32),
            jax.ShapeDtypeStruct((tokens, LANES), F32),
        ],
        in_specs=[SMEM, row(D), row(D), row(1), whole(1, tokens)] + [whole(1, D)] * 4,
        out_specs=[row(D), row(D), turned, turned, row(D), row(tokens), row(LANES)],
        compiler_params=compiler_params(40),
        cost_estimate=cost(12),
        name="first",
    )(
        gate,
        hidden,
        cotangent,
        segments[:, None],
        segments[None, :],
        *vectors,
    )


def rotary_tables(places):
    half = ROT // 2
    lane = jnp.arange(LANES, dtype=jnp.int32) % HD
    freqs = 1.0 / 10000.0 ** ((lane % half).astype(F32) * 2.0 / ROT)
    angles = places * freqs[None, :]
    cosine, sine = jnp.cos(angles), jnp.sin(angles)
    turned, early = (lane < ROT)[None, :], (lane < half)[None, :]
    return (
        jnp.where(turned, cosine, 1.0),
        jnp.where(early, -sine, 0.0),
        jnp.where(turned & ~early, sine, 0.0),
    )


def take(array, row, col, rows, cols):
    return lax.dynamic_slice(array, (row, col), (rows, cols))


def body(
    hidden_in,
    cotangent,
    seg_ids,
    first_gain,
    first_shift,
    second_gain,
    second_shift,
    qkv_weight,
    qkv_bias,
    out_weight,
    out_bias,
    up_weight,
    up_bias,
    down_weight,
    down_bias,
):
    z, q, c = place_ids()
    ids = jnp.stack([z, q, c]).astype(jnp.int32)
    own = qkv_weight.shape[0]
    part = own // 4
    hidden_units = up_weight.shape[1]
    own_hidden = down_weight.shape[0]
    chunks = own_hidden // WIDE
    deep = WIDE // 4
    weight_pieces = []
    for j in range(chunks):
        weight_pieces.append(
            jnp.concatenate(
                [take(up_weight, q * part, (2 * c + b) * own_hidden + j * WIDE, part, WIDE) for b in range(2)]
                + [take(down_weight, j * WIDE + q * deep, c * WIDE, deep, WIDE)]
            )
        )
    weight_pieces.append(
        jnp.concatenate(
            [take(qkv_weight, q * part, c * 3 * WIDE + b * WIDE, part, WIDE) for b in range(3)]
            + [take(out_weight, q * part, c * WIDE, part, WIDE)]
        )
    )
    attention_plan = (
        (own, part, 0, 3, 0, tuple(b * WIDE for b in range(6))),
        (own, part, 3 * part, 1, 0, (0, WIDE)),
    )
    far = gather_far(weight_pieces[0])
    parts = gather_plane(far)
    small = gather_small(
        ids,
        [first_gain, first_shift, second_gain, second_shift]
        + [qkv_bias, out_bias, up_bias, down_bias],
        far,
    )
    gain_1, shift_1, gain_2, shift_2, qkv_b0, out_b0, up_b0, down_b0 = small
    weight_pieces = [after(p, far) for p in weight_pieces[1:]]
    near = [swap(p, "shard", 1) for p in weight_pieces]
    onward = [jnp.stack([p, n]) for p, n in zip(weight_pieces, near)]
    first_b, second_b, first_t, second_t, cot_b, mask, places = first_call(
        after(ids, far, *onward), hidden_in, cotangent, seg_ids, small[:4]
    )
    coming = swap(onward[0], "shard", 2)
    done = first_b
    tables = rotary_tables(places)

    acts, ups, downs, up_weights, bias_parts, plane_terms, pending = [], [], [], [], [], [], None
    order = ids
    for j in range(chunks):
        coming = after(coming, done)
        pieces = gather_core([after(p, done, coming) for p in parts])
        far = far_of(near[j], coming)
        parts = gather_plane(far)
        if j + 1 < len(near):
            coming = swap(after(onward[j + 1], far), "shard", 2)
        order = after(order, far)
        mlp_plan = (
            (own, part, 0, 2, 0, tuple(b * own_hidden + j * WIDE for b in range(4))),
            (WIDE, deep, 2 * part, 1, j * WIDE, (0, WIDE)),
        )
        up_full, down_full = assemble(ids, (up_weight, down_weight), mlp_plan, pieces)
        act, up_grad, keep, send, bias_g = mlp_call(
            order,
            second_b,
            second_t,
            cot_b,
            up_full,
            down_full,
            up_b0,
            j,
            chunks,
        )
        done = keep
        acts.append(act)
        ups.append(up_grad)
        downs.append(down_full)
        up_weights.append(up_full)
        bias_parts.append(bias_g.reshape(4, WIDE))
        if pending is not None:
            keep_before, got_before = pending
            sends = plane_sends(after(ids, keep), keep_before, got_before)
            plane_terms.append(plane_swap(sends))
            order_next = sends
        pending = (keep, swap(send, "rep", 1))
        order = after(ids, keep, send)
    pieces = gather_core([after(p, done) for p in parts])
    qkv_full, out_full = assemble(ids, (qkv_weight, out_weight), attention_plan, pieces)
    gate = after(ids, *order_next) if chunks > 1 else order
    qkv_b = qkv_call(gate, first_b, qkv_full, qkv_b0, tables)
    keep, got = pending
    sends = plane_sends(after(ids, qkv_b), keep, got)
    plane_terms.append(plane_swap(sends))

    pairs = D // LANES // 3
    earlier = attention_call(after(ids, *sends), 0, pairs, qkv_b, cot_b, out_full, mask, tables, ())
    earlier = attention_call(ids, pairs, pairs, qkv_b, cot_b, out_full, mask, tables, tuple(earlier))
    gate = earlier[0]
    plane_terms = [[after(terms[0], gate)] + terms[1:] for terms in plane_terms]
    sends = shard_sends(plane_terms, z)
    earlier = attention_call(
        after(ids, *sends), 2 * pairs, pairs, qkv_b, cot_b, out_full, mask, tables, tuple(earlier)
    )
    owned = shard_sum([after(sends[0], earlier[0])] + sends[1:])
    mixed_b, grads = earlier
    keep, send, qkv_bias_g = qkv_grad_call(after(ids, owned), grads, first_t, mixed_b, cot_b)
    owned = after(owned, keep)
    shared = [owned] + [swap(owned, "rep", j * 2) for j in (1, 2, 3)]
    got = swap(send, "rep", 1)
    input_grad, row_sums = input_grad_call(
        after(ids, send, owned),
        hidden_in,
        cotangent,
        grads,
        qkv_full,
        gain_1,
        gain_2,
        ups,
        up_weights,
    )
    sends = plane_sends(after(ids, input_grad), keep, got)
    terms = plane_swap(sends)
    mlp_parts = jnp.stack([after(s, input_grad) for s in shared])
    mlp_other = swap(mlp_parts, "rep", 1)
    output = output_call(
        after(ids, mlp_parts, *sends), hidden_in, mixed_b, out_full, out_b0, down_b0, acts, downs
    )
    terms[0] = after(terms[0], output)
    sends = shard_sends([terms], z)
    row_sums = after(row_sums, *sends)
    up_bias_g = jnp.stack(after(bias_parts, row_sums), axis=1).reshape(-1)
    qkv_bias_g = after(qkv_bias_g, row_sums).reshape(-1)
    sums = [row_sums[0], row_sums[1], row_sums[2], row_sums[3], qkv_bias_g, row_sums[4], up_bias_g]
    total = sum_small(pack(sums)).reshape(-1)

    mlp_place = []
    for j in range(chunks):
        first = j * (D // 4)
        mlp_place.append(
            (0, 0, part, first, tuple((2 * own_hidden, b * own_hidden + j * WIDE) for b in range(2)))
        )
        mlp_place.append((1, j * WIDE, deep, first + 2 * part, ((WIDE, 0),)))
    up_weight_g, down_weight_g = place(
        ids, [(own, hidden_units), (own_hidden, D)], mlp_place, after(mlp_parts, *sends), mlp_other
    )
    attention_place = [
        (0, 0, part, 0, tuple((3 * WIDE, b * WIDE) for b in range(3))),
        (1, 0, part, 3 * part, ((WIDE, 0),)),
    ]
    parts = share_plane(shard_sum(sends))
    qkv_weight_g, out_weight_g = place(
        ids, [(own, 3 * D), (own, D)], attention_place, parts, swap(parts, "rep", 1)
    )
    summed, at_row = [], 0
    for s in sums:
        size = s.shape[0] // 4
        summed.append(lax.dynamic_slice(total, (at_row + z * size,), (size,)))
        at_row += s.shape[0]
    return (
        output,
        input_grad,
        summed[0],
        summed[1],
        summed[2],
        summed[3],
        qkv_weight_g,
        summed[4],
        out_weight_g,
        summed[5],
        up_weight_g,
        summed[6],
        down_weight_g,
        summed[5],
    )


def solution(mesh):
    tokens = P(("rep", "shard"), None)
    matrix, vector = P("shard", None), P("shard")
    params = (vector,) * 4 + (matrix, vector) * 4
    in_specs = (tokens, tokens, P(("rep", "shard"))) + params
    out_specs = (tokens, tokens) + params
    return jax.shard_map(body, mesh=mesh, in_specs=in_specs, out_specs=out_specs, check_vma=False)
```

```python
import functools

import jax
import jax.numpy as jnp
from jax import lax
from jax.experimental import pallas as pl
from jax.experimental.pallas import tpu as pltpu
from jax.sharding import PartitionSpec as P

D = 768
H = 12
HD = 64
ROT = 16
WIDE = 384
LANES = 128
F32, BF16 = jnp.float32, jnp.bfloat16
norm_eps = 1e-05


def compiler_params(mib):
    return pltpu.CompilerParams(vmem_limit_bytes=mib * 2**20)


def cost(microseconds):
    return pl.CostEstimate(
        flops=int(microseconds * 1.1e9), bytes_accessed=int(microseconds * 1e5), transcendentals=0
    )


VMEM = pl.BlockSpec(memory_space=pltpu.VMEM)
SMEM = pl.BlockSpec(memory_space=pltpu.SMEM)


def swap(value, axis, bit):
    size = lax.axis_size(axis)
    return lax.ppermute(value, axis, [(i, i ^ bit) for i in range(size)])


def place_ids():
    rep = lax.axis_index("rep").astype(jnp.uint32)
    return lax.axis_index("shard").astype(jnp.uint32), (rep >> 1) & 3, rep & 1


def after(value, *others):
    return lax.optimization_barrier((value, *others))[0]


def gather_far(piece):
    return jnp.stack([swap(piece, "shard", k) for k in (1, 2, 3)])


def far_of(near, rest):
    return jnp.concatenate([near[None], rest])


def gather_plane(far):
    return [far] + [swap(far, "rep", j * 2) for j in (1, 2, 3)]


def gather_core(parts):
    parts = jnp.stack(parts)
    return parts, swap(parts, "rep", 1)


def total_of(arrays):
    return (
        (arrays[0].astype(F32) + arrays[1].astype(F32))
        + (arrays[2].astype(F32) + arrays[3].astype(F32))
    ).astype(BF16)


def at(block, index):
    return lax.dynamic_index_in_dim(block, index, 0, keepdims=False)


def plane_sum_body(ids_ref, keep_ref, got_ref, *outs):
    q = ids_ref[1]
    for j in range(4):
        total = keep_ref[q ^ j].astype(F32) + got_ref[q ^ j].astype(F32)
        outs[j][...] = total.astype(BF16)


def plane_sends(ids, keep, got):
    rows = keep.shape[2]
    block = pl.BlockSpec((4, 1, rows, WIDE), lambda i: (0, i, 0, 0))
    return pl.pallas_call(
        plane_sum_body,
        grid=(4,),
        out_shape=[jax.ShapeDtypeStruct((4, rows, WIDE), BF16)] * 4,
        in_specs=[SMEM, block, block],
        out_specs=[pl.BlockSpec((1, rows, WIDE), lambda i: (i, 0, 0))] * 4,
        compiler_params=compiler_params(40),
        cost_estimate=cost(3),
        name="plane_sum",
    )(ids, keep, got)


def plane_swap(sends):
    return [sends[0]] + [swap(sends[j], "rep", j * 2) for j in (1, 2, 3)]


def shard_sends(groups, z):
    return [
        jnp.concatenate([total_of([at(term, z ^ k) for term in terms]) for terms in groups])
        for k in range(4)
    ]


def shard_sum(sends):
    owned = total_of([sends[0]] + [swap(sends[k], "shard", k) for k in (1, 2, 3)])
    bit = 8
    while bit < lax.axis_size("rep"):
        owned = (owned.astype(F32) + swap(owned, "rep", bit).astype(F32)).astype(BF16)
        bit *= 2
    return owned


def share_plane(owned):
    return jnp.stack([owned] + [swap(owned, "rep", j * 2) for j in (1, 2, 3)])


def sum_small(vector):
    bit = 1
    while bit < lax.axis_size("rep"):
        if bit not in (2, 4):
            vector = vector + swap(vector, "rep", bit)
        bit *= 2
    vector = (vector + swap(vector, "rep", 2)) + (swap(vector, "rep", 4) + swap(vector, "rep", 6))
    return (vector + swap(vector, "shard", 1)) + (swap(vector, "shard", 2) + swap(vector, "shard", 3))


def pack(vectors):
    flat = jnp.concatenate([v.reshape(-1) for v in vectors])
    fill = -flat.shape[0] % 1024
    return jnp.concatenate([flat, jnp.zeros((fill,), flat.dtype)]).reshape(-1, LANES)


def assemble_body(plan, ids_ref, *refs):
    count = len(plan)
    shards, pieces, outs = refs[:count], refs[count : count + 2], refs[count + 2 :]
    z, q, c = ids_ref[0], ids_ref[1], ids_ref[2]
    for shard_ref, out_ref, (rows, part, first, blocks, row_0, columns) in zip(shards, outs, plan):
        half = blocks * WIDE
        own = pl.ds(pl.multiple_of(z * rows, rows), rows)
        for b, col_0 in enumerate(columns):
            out_ref[own, b * WIDE : (b + 1) * WIDE] = shard_ref[row_0 : row_0 + rows, col_0 : col_0 + WIDE]
        for h, piece in ((c, pieces[0]), (1 - c, pieces[1])):
            for j in range(4):
                for k in (1, 2, 3):
                    row = pl.multiple_of((z ^ k) * rows + (q ^ j) * part, part)
                    for b in range(blocks):
                        col = pl.multiple_of(h * half + b * WIDE, WIDE)
                        start = first + b * part
                        out_ref[pl.ds(row, part), pl.ds(col, WIDE)] = piece[
                            j, k - 1, start : start + part, :
                        ]


def assemble(ids, shards, plan, pieces):
    shapes = [jax.ShapeDtypeStruct((4 * p[0], 2 * p[3] * WIDE), BF16) for p in plan]
    return pl.pallas_call(
        functools.partial(assemble_body, plan),
        out_shape=shapes,
        in_specs=[SMEM] + [VMEM] * (len(shards) + 2),
        out_specs=[VMEM] * len(shards),
        compiler_params=compiler_params(40),
        cost_estimate=cost(3),
        name="assemble",
    )(ids, *shards, *pieces)


def pack_small_body(*refs):
    out_ref = refs[-1]
    out_ref[...] = jnp.zeros_like(out_ref)
    for n, ref in enumerate(refs[:-1]):
        out_ref[n : n + 1, : ref.shape[1]] = ref[...].astype(F32)


def unpack_small_body(lengths, ids_ref, *refs):
    near, outs = refs[:4], refs[4:]
    z = ids_ref[0]
    for shard in range(4):
        rows = near[0][...].astype(F32)
        for k in (1, 2, 3):
            rows = jnp.where((z ^ k) == shard, near[k][...].astype(F32), rows)
        for n, (out_ref, length) in enumerate(zip(outs, lengths)):
            out_ref[:, shard * length : (shard + 1) * length] = rows[n : n + 1, :length]


def gather_small(ids, vectors, gate):
    lengths = [v.shape[0] for v in vectors]
    widest = max(lengths)
    packed = pl.pallas_call(
        pack_small_body,
        out_shape=jax.ShapeDtypeStruct((len(vectors), widest), F32),
        in_specs=[VMEM] * len(vectors),
        out_specs=VMEM,
        cost_estimate=cost(1),
        name="pack_small",
    )(*[v.astype(F32)[None, :] for v in vectors])
    packed = after(packed, gate)
    near = [packed] + [swap(packed, "shard", k) for k in (1, 2, 3)]
    return pl.pallas_call(
        functools.partial(unpack_small_body, lengths),
        out_shape=[jax.ShapeDtypeStruct((1, 4 * n), F32) for n in lengths],
        in_specs=[SMEM] + [VMEM] * 4,
        out_specs=[VMEM] * len(vectors),
        cost_estimate=cost(1),
        name="unpack_small",
    )(ids, *near)


def place_body(plan, ids_ref, parts_ref, other_ref, *outs):
    q, c = ids_ref[1], ids_ref[2]
    for out, rows, part, first, blocks in plan:
        for h, pieces in ((c, parts_ref), (1 - c, other_ref)):
            for j in range(4):
                row = pl.multiple_of(rows + (q ^ j) * part, part)
                for b, (scale, offset) in enumerate(blocks):
                    col = pl.multiple_of(h * scale + offset, WIDE)
                    start = first + b * part
                    outs[out][pl.ds(row, part), pl.ds(col, WIDE)] = pieces[
                        j, start : start + part, :
                    ].astype(F32)


def place(ids, shapes, plan, parts, other):
    return pl.pallas_call(
        functools.partial(place_body, plan),
        out_shape=[jax.ShapeDtypeStruct(s, F32) for s in shapes],
        in_specs=[SMEM, VMEM, VMEM],
        out_specs=[VMEM] * len(shapes),
        compiler_params=compiler_params(40),
        cost_estimate=cost(3),
        name="place",
    )(ids, parts, other)


def dot(left, right, left_dim=1, right_dim=0):
    return lax.dot_general(
        left, right, (((left_dim,), (right_dim,)), ((), ())), preferred_element_type=F32
    )


def turn(values, cosine, early, late):
    width = values.shape[1]
    return (
        values * cosine
        + pltpu.roll(values, width - ROT // 2, 1) * early
        + pltpu.roll(values, ROT // 2, 1) * late
    )


def qkv_body(gate_ref, x_ref, w_ref, bias_ref, cos_ref, early_ref, late_ref, out_ref):
    values = dot(x_ref[...], w_ref[...]) + bias_ref[...]

    @pl.when(pl.program_id(0) < 4)
    def rotate_block():
        for b in range(WIDE // LANES):
            cols = slice(b * LANES, (b + 1) * LANES)
            out_ref[:, cols] = turn(
                values[:, cols], cos_ref[...], early_ref[...], late_ref[...]
            ).astype(BF16)

    @pl.when(pl.program_id(0) >= 4)
    def plain_block():
        out_ref[...] = values.astype(BF16)


def qkv_call(gate, first_b, weight, bias, tables):
    tokens = first_b.shape[0]
    whole = lambda r, c: pl.BlockSpec((r, c), lambda i: (0, 0))
    return pl.pallas_call(
        qkv_body,
        grid=(3 * D // WIDE,),
        out_shape=jax.ShapeDtypeStruct((tokens, 3 * D), BF16),
        in_specs=[
            SMEM,
            whole(tokens, D),
            pl.BlockSpec((D, WIDE), lambda i: (0, i)),
            pl.BlockSpec((1, WIDE), lambda i: (0, i)),
        ]
        + [whole(tokens, LANES)] * 3,
        out_specs=pl.BlockSpec((tokens, WIDE), lambda i: (0, i)),
        compiler_params=compiler_params(40),
        cost_estimate=cost(11),
        name="qkv",
    )(gate, first_b, weight, bias, *tables)


def attention_body(
    first_call, gate_ref, q_ref, k_ref, v_ref, cot_ref, w_ref, mask_ref, cos_ref, early_ref, late_ref, *refs
):
    mixed_ref, grad_ref, key_t_ref, value_t_ref = refs if first_call else refs[2:]
    tokens = q_ref.shape[0]
    step = min(256, tokens)
    out_grad = dot(cot_ref[...], w_ref[...], 1, 1).astype(BF16)
    lane = lax.broadcasted_iota(jnp.int32, (tokens, LANES), 1)
    query_t = q_ref[...].astype(F32).T.astype(BF16)
    out_grad_t = out_grad.astype(F32).T.astype(BF16)
    nothing = jnp.zeros((tokens, LANES), BF16)
    keys = k_ref[...] * BF16(HD**-0.5)
    heads = []
    for h in range(2):
        here = (lane // HD) == h
        heads.append((jnp.where(here, keys, nothing), jnp.where(here, v_ref[...], nothing)))
    key_t_ref[...] = jnp.zeros_like(key_t_ref)
    value_t_ref[...] = jnp.zeros_like(value_t_ref)
    for first in range(0, tokens, step):
        last = first + step
        block = slice(first, last)
        mixed = jnp.zeros((step, LANES), F32)
        query_grad = jnp.zeros((step, LANES), F32)
        both = range(2)
        keys_h = [heads[h][0][:last] for h in both]
        values_h = [heads[h][1][:last] for h in both]
        bias = mask_ref[block, :last]
        scores = [dot(q_ref[block, :], keys_h[h], 1, 1) + bias for h in both]
        probs_grad = [dot(out_grad[block], values_h[h], 1, 1) for h in both]
        expo = [jnp.exp(s - jnp.max(s, axis=1, keepdims=True)) for s in scores]
        probs = [e * (1.0 / jnp.sum(e, axis=1, keepdims=True)) for e in expo]
        probs_b = [p.astype(BF16) for p in probs]
        weighted = [g * p for g, p in zip(probs_grad, probs)]
        scores_grad = [
            (w - p * jnp.sum(w, axis=1, keepdims=True)).astype(BF16)
            for w, p in zip(weighted, probs)
        ]
        for h in both:
            rows = slice(h * HD, (h + 1) * HD)
            mixed += dot(probs_b[h], values_h[h])
            query_grad += dot(scores_grad[h], keys_h[h])
            key_t_ref[rows, :last] += dot(query_t[rows, block], scores_grad[h])
            value_t_ref[rows, :last] += dot(out_grad_t[rows, block], probs_b[h])
        mixed_ref[block, :] = mixed.astype(BF16)
        grad_ref[0, block, :] = turn(
            query_grad, cos_ref[block, :], -early_ref[block, :], -late_ref[block, :]
        ).astype(BF16)
    grad_ref[1, :, :] = turn(
        key_t_ref[...].T * HD**-0.5, cos_ref[...], -early_ref[...], -late_ref[...]
    ).astype(BF16)
    grad_ref[2, :, :] = value_t_ref[...].T.astype(BF16)


def attention_call(gate, start, pairs, qkv_b, cot_b, out_weight, mask, tables, earlier):
    tokens = qkv_b.shape[0]
    every = D // LANES
    whole = lambda r, c: pl.BlockSpec((r, c), lambda i: (0, 0))
    part = lambda n: pl.BlockSpec((tokens, LANES), lambda i: (0, n * every + start + i))
    anywhere = pl.BlockSpec(memory_space=pl.ANY)
    return pl.pallas_call(
        functools.partial(attention_body, not earlier),
        grid=(pairs,),
        out_shape=[
            jax.ShapeDtypeStruct((tokens, D), BF16),
            jax.ShapeDtypeStruct((3, tokens, D), BF16),
        ],
        in_specs=[
            SMEM,
            part(0),
            part(1),
            part(2),
            whole(tokens, D),
            pl.BlockSpec((LANES, D), lambda i: (start + i, 0)),
            whole(tokens, tokens),
        ]
        + [whole(tokens, LANES)] * 3
        + [anywhere] * len(earlier),
        out_specs=[
            pl.BlockSpec((tokens, LANES), lambda i: (0, start + i)),
            pl.BlockSpec((3, tokens, LANES), lambda i: (0, 0, start + i)),
        ],
        scratch_shapes=[
            pltpu.VMEM((LANES, tokens), F32),
            pltpu.VMEM((LANES, tokens), F32),
        ],
        input_output_aliases={10: 0, 11: 1} if earlier else {},
        compiler_params=compiler_params(56),
        cost_estimate=cost(9 * pairs),
        name="attention",
    )(gate, qkv_b, qkv_b, qkv_b, cot_b, out_weight, mask, *tables, *earlier)


def store_block(keep_ref, send_ref, here, block, part, row):
    def store(ref):
        for z in range(4):
            for q in range(4):
                start = (z * 4 + q) * part
                ref[q, z, pl.ds(row, part), :] = block[start : start + part, :]

    pl.when(here)(lambda: store(keep_ref))
    pl.when(jnp.logical_not(here))(lambda: store(send_ref))


def qkv_grad_body(ids_ref, grad_ref, first_t_ref, mixed_ref, cot_ref, keep_ref, send_ref, bias_ref):
    step = pl.program_id(0)
    grad = grad_ref[0]
    h, b = step // 3, step % 3
    here = h == ids_ref[2]
    part = D // 16
    block = dot(first_t_ref[...], grad).astype(BF16)
    store_block(keep_ref, send_ref, here, block, part, pl.multiple_of(b * part, part))
    bias_ref[...] = jnp.sum(grad.astype(F32), axis=0, keepdims=True)

    @pl.when(b == 0)
    def out_part():
        block = dot(mixed_ref[...], cot_ref[...], 0, 0).astype(BF16)
        store_block(keep_ref, send_ref, here, block, part, 3 * part)


def qkv_grad_call(ids, grads, first_t, mixed_b, cot_b):
    tokens = cot_b.shape[0]
    whole = lambda r, c: pl.BlockSpec((r, c), lambda i: (0, 0))
    pack_spec = pl.BlockSpec((4, 4, D // 4, WIDE), lambda i: (0, 0, 0, 0))
    return pl.pallas_call(
        qkv_grad_body,
        grid=(3 * D // WIDE,),
        out_shape=[
            jax.ShapeDtypeStruct((4, 4, D // 4, WIDE), BF16),
            jax.ShapeDtypeStruct((4, 4, D // 4, WIDE), BF16),
            jax.ShapeDtypeStruct((1, 3 * D), F32),
        ],
        in_specs=[
            SMEM,
            pl.BlockSpec((1, tokens, WIDE), lambda i: (i // 2, 0, i % 2)),
            whole(D, tokens),
            whole(tokens, D),
            pl.BlockSpec((tokens, WIDE), lambda i: (0, i // 3)),
        ],
        out_specs=[pack_spec, pack_spec, pl.BlockSpec((1, WIDE), lambda i: (0, i))],
        compiler_params=compiler_params(56),
        cost_estimate=cost(14),
        name="qkv_grad",
    )(ids, grads, first_t, mixed_b, cot_b)


def mlp_body(
    ids_ref, x_ref, x_t_ref, cot_ref, up_ref, down_ref, bias_ref,
    act_ref, grad_ref, keep_ref, send_ref, bias_grad_ref,
):
    step = pl.program_id(0)
    tokens = x_ref.shape[0]
    rows = min(256, tokens)
    total = jnp.zeros((1, WIDE), F32)
    blocks = [slice(first, first + rows) for first in range(0, tokens, rows)]
    ups = [dot(x_ref[block, :], up_ref[...]) + bias_ref[...] for block in blocks]
    act_grads = [dot(cot_ref[block, :], down_ref[...], 1, 1) for block in blocks]
    for block, up, act_grad in zip(blocks, ups, act_grads):
        below = 0.5 + 0.5 * lax.erf(up * (0.5**0.5))
        slope = below + up * (jnp.exp(-0.5 * up * up) * 0.3989422804014327)
        up_grad = (act_grad * slope).astype(BF16)
        act_ref[block, :] = (up * below).astype(BF16)
        grad_ref[block, :] = up_grad
        total += jnp.sum(up_grad.astype(F32), axis=0, keepdims=True)
    bias_grad_ref[...] = total
    part = D // 16
    c = ids_ref[2]
    block = dot(x_t_ref[...], grad_ref[...]).astype(BF16)
    store_block(
        keep_ref, send_ref, step // 2 == c, block, part, pl.multiple_of((step % 2) * part, part)
    )
    down = dot(act_ref[...], cot_ref[...], 0, 0).astype(BF16)
    deep = WIDE // 4

    def store_down(keep, send):
        for q in range(4):
            rows_here = slice(q * deep, (q + 1) * deep)
            keep_ref[q, step, 2 * part :, :] = down[rows_here, keep * WIDE : (keep + 1) * WIDE]
            send_ref[q, step, 2 * part :, :] = down[rows_here, send * WIDE : (send + 1) * WIDE]

    pl.when(c == 0)(lambda: store_down(0, 1))
    pl.when(c == 1)(lambda: store_down(1, 0))


def mlp_call(ids, second_b, second_t, cot_b, up_weight, down_weight, bias, chunk, chunks):
    tokens = cot_b.shape[0]
    whole = lambda r, c: pl.BlockSpec((r, c), lambda i: (0, 0))
    column = pl.BlockSpec((tokens, WIDE), lambda i: (0, i))
    pack_spec = pl.BlockSpec((4, 4, D // 4, WIDE), lambda i: (0, 0, 0, 0))
    return pl.pallas_call(
        mlp_body,
        grid=(4,),
        out_shape=[
            jax.ShapeDtypeStruct((tokens, 4 * WIDE), BF16),
            jax.ShapeDtypeStruct((tokens, 4 * WIDE), BF16),
            jax.ShapeDtypeStruct((4, 4, D // 4, WIDE), BF16),
            jax.ShapeDtypeStruct((4, 4, D // 4, WIDE), BF16),
            jax.ShapeDtypeStruct((1, 4 * WIDE), F32),
        ],
        in_specs=[
            SMEM,
            whole(tokens, D),
            whole(D, tokens),
            whole(tokens, D),
            pl.BlockSpec((D, WIDE), lambda i: (0, i)),
            pl.BlockSpec((WIDE, D), lambda i: (i, 0)),
            pl.BlockSpec((1, WIDE), lambda i: (0, i * chunks + chunk)),
        ],
        out_specs=[column, column, pack_spec, pack_spec, pl.BlockSpec((1, WIDE), lambda i: (0, i))],
        compiler_params=compiler_params(56),
        cost_estimate=cost(20),
        name="mlp",
    )(ids, second_b, second_t, cot_b, up_weight, down_weight, bias)


def output_body(count, gate_ref, hidden_ref, mixed_ref, out_w_ref, out_bias_ref, down_bias_ref, *refs):
    acts, downs, out_ref = refs[:count], refs[count : 2 * count], refs[2 * count]
    wide = dot(acts[0][...], downs[0][...])
    for a, w in zip(acts[1:], downs[1:]):
        wide += dot(a[...], w[...])
    attention = dot(mixed_ref[...], out_w_ref[...]) + out_bias_ref[...]
    out_ref[...] = hidden_ref[...] + attention + (wide + down_bias_ref[...])


def output_call(gate, hidden, mixed_b, out_weight, out_bias, down_bias, acts, downs):
    tokens = hidden.shape[0]
    rows = min(256, tokens)
    row = lambda c: pl.BlockSpec((rows, c), lambda i: (i, 0))
    whole = lambda a: pl.BlockSpec(a.shape, lambda i: (0, 0))
    return pl.pallas_call(
        functools.partial(output_body, len(acts)),
        grid=(tokens // rows,),
        out_shape=jax.ShapeDtypeStruct((tokens, D), F32),
        in_specs=[SMEM, row(D), row(D), whole(out_weight), whole(out_bias), whole(down_bias)]
        + [row(a.shape[1]) for a in acts]
        + [whole(w) for w in downs],
        out_specs=row(D),
        compiler_params=compiler_params(56),
        cost_estimate=cost(10),
        name="output",
    )(gate, hidden, mixed_b, out_weight, out_bias, down_bias, *acts, *downs)


def input_grad_body(count, gate_ref, hidden_ref, cot_ref, grad_ref, w_ref, gain_1_ref, gain_2_ref, *refs):
    ups, weights, out_ref, sums_ref = refs[:count], refs[count : 2 * count], refs[2 * count], refs[2 * count + 1]
    first = dot(grad_ref[0], w_ref[:, :D], 1, 1)
    for n in (1, 2):
        first += dot(grad_ref[n], w_ref[:, n * D : (n + 1) * D], 1, 1)
    second = dot(ups[0][...], weights[0][...], 1, 1)
    for u, w in zip(ups[1:], weights[1:]):
        second += dot(u[...], w[...], 1, 1)
    normed, scale = normalize(hidden_ref[...])
    cot = cot_ref[...]
    inner = first * gain_1_ref[...] + second * gain_2_ref[...]
    out_ref[...] = cot + scale * (
        inner
        - jnp.mean(inner, axis=-1, keepdims=True)
        - normed * jnp.mean(inner * normed, axis=-1, keepdims=True)
    )

    @pl.when(pl.program_id(0) == 0)
    def clear():
        sums_ref[...] = jnp.zeros_like(sums_ref)

    for n, value in enumerate((first * normed, first, second * normed, second, cot)):
        sums_ref[n : n + 1, :] += jnp.sum(value, axis=0, keepdims=True)


def input_grad_call(gate, hidden, cotangent, grads, weight, gain_1, gain_2, ups, weights):
    tokens = hidden.shape[0]
    rows = min(256, tokens)
    row = lambda c: pl.BlockSpec((rows, c), lambda i: (i, 0))
    whole = lambda a: pl.BlockSpec(a.shape, lambda i: (0, 0))
    return pl.pallas_call(
        functools.partial(input_grad_body, len(ups)),
        grid=(tokens // rows,),
        out_shape=[jax.ShapeDtypeStruct((tokens, D), F32), jax.ShapeDtypeStruct((8, D), F32)],
        in_specs=[
            SMEM,
            row(D),
            row(D),
            pl.BlockSpec((3, rows, D), lambda i: (0, i, 0)),
            whole(weight),
            whole(gain_1),
            whole(gain_2),
        ]
        + [row(u.shape[1]) for u in ups]
        + [whole(w) for w in weights],
        out_specs=[row(D), pl.BlockSpec((8, D), lambda i: (0, 0))],
        compiler_params=compiler_params(56),
        cost_estimate=cost(14),
        name="input_grad",
    )(gate, hidden, cotangent, grads, weight, gain_1, gain_2, *ups, *weights)


def normalize(values):
    centre = values - jnp.mean(values, axis=-1, keepdims=True)
    scale = lax.rsqrt(jnp.mean(centre * centre, axis=-1, keepdims=True) + norm_eps)
    return centre * scale, scale


def first_body(
    gate_ref, hidden_ref, cot_ref, seg_col_ref, seg_row_ref, gain_1_ref, shift_1_ref, gain_2_ref, shift_2_ref,
    first_ref, second_ref, first_t_ref, second_t_ref, cot_b_ref, mask_ref, places_ref,
):
    normed, _ = normalize(hidden_ref[...])
    first = (normed * gain_1_ref[...] + shift_1_ref[...]).astype(BF16)
    second = (normed * gain_2_ref[...] + shift_2_ref[...]).astype(BF16)
    first_ref[...] = first
    second_ref[...] = second
    first_t_ref[...] = first.astype(F32).T.astype(BF16)
    second_t_ref[...] = second.astype(F32).T.astype(BF16)
    cot_b_ref[...] = cot_ref[...].astype(BF16)
    rows, tokens = mask_ref.shape
    row = pl.program_id(0) * rows + lax.broadcasted_iota(jnp.int32, (rows, tokens), 0)
    col = lax.broadcasted_iota(jnp.int32, (rows, tokens), 1)
    mine, others = seg_col_ref[...], seg_row_ref[...]
    mask_ref[...] = jnp.where((mine == others) & (col <= row), 0.0, -1e30)
    before = jnp.sum(jnp.where(mine > others, 1.0, 0.0), axis=1, keepdims=True)
    places_ref[...] = row[:, :LANES].astype(F32) - before


def first_call(gate, hidden, cotangent, segments, vectors):
    tokens = hidden.shape[0]
    rows = min(256, tokens)
    row = lambda c: pl.BlockSpec((rows, c), lambda i: (i, 0))
    turned = pl.BlockSpec((D, rows), lambda i: (0, i))
    whole = lambda r, c: pl.BlockSpec((r, c), lambda i: (0, 0))
    wide = jax.ShapeDtypeStruct((tokens, D), BF16)
    tall = jax.ShapeDtypeStruct((D, tokens), BF16)
    return pl.pallas_call(
        first_body,
        grid=(tokens // rows,),
        out_shape=[
            wide,
            wide,
            tall,
            tall,
            wide,
            jax.ShapeDtypeStruct((tokens, tokens), F32),
            jax.ShapeDtypeStruct((tokens, LANES), F32),
        ],
        in_specs=[SMEM, row(D), row(D), row(1), whole(1, tokens)] + [whole(1, D)] * 4,
        out_specs=[row(D), row(D), turned, turned, row(D), row(tokens), row(LANES)],
        compiler_params=compiler_params(40),
        cost_estimate=cost(12),
        name="first",
    )(
        gate,
        hidden,
        cotangent,
        segments[:, None],
        segments[None, :],
        *vectors,
    )


def rotary_tables(places):
    half = ROT // 2
    lane = jnp.arange(LANES, dtype=jnp.int32) % HD
    freqs = 1.0 / 10000.0 ** ((lane % half).astype(F32) * 2.0 / ROT)
    angles = places * freqs[None, :]
    cosine, sine = jnp.cos(angles), jnp.sin(angles)
    turned, early = (lane < ROT)[None, :], (lane < half)[None, :]
    return (
        jnp.where(turned, cosine, 1.0),
        jnp.where(early, -sine, 0.0),
        jnp.where(turned & ~early, sine, 0.0),
    )


def take(array, row, col, rows, cols):
    return lax.dynamic_slice(array, (row, col), (rows, cols))


def body(
    hidden_in,
    cotangent,
    seg_ids,
    first_gain,
    first_shift,
    second_gain,
    second_shift,
    qkv_weight,
    qkv_bias,
    out_weight,
    out_bias,
    up_weight,
    up_bias,
    down_weight,
    down_bias,
):
    z, q, c = place_ids()
    ids = jnp.stack([z, q, c]).astype(jnp.int32)
    own = qkv_weight.shape[0]
    part = own // 4
    hidden_units = up_weight.shape[1]
    own_hidden = down_weight.shape[0]
    chunks = own_hidden // WIDE
    deep = WIDE // 4
    weight_pieces = []
    for j in range(chunks):
        weight_pieces.append(
            jnp.concatenate(
                [take(up_weight, q * part, (2 * c + b) * own_hidden + j * WIDE, part, WIDE) for b in range(2)]
                + [take(down_weight, j * WIDE + q * deep, c * WIDE, deep, WIDE)]
            )
        )
    weight_pieces.append(
        jnp.concatenate(
            [take(qkv_weight, q * part, c * 3 * WIDE + b * WIDE, part, WIDE) for b in range(3)]
            + [take(out_weight, q * part, c * WIDE, part, WIDE)]
        )
    )
    attention_plan = (
        (own, part, 0, 3, 0, tuple(b * WIDE for b in range(6))),
        (own, part, 3 * part, 1, 0, (0, WIDE)),
    )
    far = gather_far(weight_pieces[0])
    parts = gather_plane(far)
    small = gather_small(
        ids,
        [first_gain, first_shift, second_gain, second_shift]
        + [qkv_bias, out_bias, up_bias, down_bias],
        far,
    )
    gain_1, shift_1, gain_2, shift_2, qkv_b0, out_b0, up_b0, down_b0 = small
    weight_pieces = [after(p, far) for p in weight_pieces[1:]]
    near = list(swap(jnp.stack(weight_pieces), "shard", 1))
    onward = [jnp.stack([p, n]) for p, n in zip(weight_pieces, near)]
    first_b, second_b, first_t, second_t, cot_b, mask, places = first_call(
        after(ids, far, *onward), hidden_in, cotangent, seg_ids, small[:4]
    )
    coming = swap(onward[0], "shard", 2)
    done = first_b
    tables = rotary_tables(places)

    acts, ups, downs, up_weights, bias_parts, plane_terms, pending = [], [], [], [], [], [], None
    order = ids
    for j in range(chunks):
        coming = after(coming, done)
        pieces = gather_core([after(p, done, coming) for p in parts])
        far = far_of(near[j], coming)
        parts = gather_plane(far)
        if j + 1 < len(near):
            coming = swap(after(onward[j + 1], far), "shard", 2)
        order = after(order, far)
        mlp_plan = (
            (own, part, 0, 2, 0, tuple(b * own_hidden + j * WIDE for b in range(4))),
            (WIDE, deep, 2 * part, 1, j * WIDE, (0, WIDE)),
        )
        up_full, down_full = assemble(ids, (up_weight, down_weight), mlp_plan, pieces)
        act, up_grad, keep, send, bias_g = mlp_call(
            order,
            second_b,
            second_t,
            cot_b,
            up_full,
            down_full,
            up_b0,
            j,
            chunks,
        )
        done = keep
        acts.append(act)
        ups.append(up_grad)
        downs.append(down_full)
        up_weights.append(up_full)
        bias_parts.append(bias_g.reshape(4, WIDE))
        if pending is not None:
            keep_before, got_before = pending
            sends = plane_sends(after(ids, keep), keep_before, got_before)
            plane_terms.append(plane_swap(sends))
            order_next = sends
            send = after(send, *sends)
            done = sends[0]
        pending = (keep, swap(send, "rep", 1))
        order = after(ids, keep, send)
    pieces = gather_core([after(p, done) for p in parts])
    qkv_full, out_full = assemble(ids, (qkv_weight, out_weight), attention_plan, pieces)
    gate = after(ids, *order_next) if chunks > 1 else order
    qkv_b = qkv_call(gate, first_b, qkv_full, qkv_b0, tables)
    keep, got = pending
    sends = plane_sends(after(ids, qkv_b), keep, got)
    plane_terms.append(plane_swap(sends))

    pairs = D // LANES // 3
    earlier = attention_call(after(ids, *sends), 0, pairs, qkv_b, cot_b, out_full, mask, tables, ())
    earlier = attention_call(ids, pairs, pairs, qkv_b, cot_b, out_full, mask, tables, tuple(earlier))
    gate = earlier[0]
    plane_terms = [[after(terms[0], gate)] + terms[1:] for terms in plane_terms]
    sends = shard_sends(plane_terms, z)
    earlier = attention_call(
        after(ids, *sends), 2 * pairs, pairs, qkv_b, cot_b, out_full, mask, tables, tuple(earlier)
    )
    owned = shard_sum([after(sends[0], earlier[0])] + sends[1:])
    mixed_b, grads = earlier
    keep, send, qkv_bias_g = qkv_grad_call(after(ids, owned), grads, first_t, mixed_b, cot_b)
    owned = after(owned, keep)
    shared = [owned] + [swap(owned, "rep", j * 2) for j in (1, 2, 3)]
    got = swap(send, "rep", 1)
    input_grad, row_sums = input_grad_call(
        after(ids, send, owned),
        hidden_in,
        cotangent,
        grads,
        qkv_full,
        gain_1,
        gain_2,
        ups,
        up_weights,
    )
    sends = plane_sends(after(ids, input_grad), keep, got)
    terms = plane_swap(sends)
    mlp_parts = jnp.stack([after(s, input_grad) for s in shared])
    mlp_other = swap(mlp_parts, "rep", 1)
    output = output_call(
        after(ids, mlp_parts, *sends), hidden_in, mixed_b, out_full, out_b0, down_b0, acts, downs
    )
    terms[0] = after(terms[0], output)
    sends = shard_sends([terms], z)
    row_sums = after(row_sums, *sends)
    up_bias_g = jnp.stack(after(bias_parts, row_sums), axis=1).reshape(-1)
    qkv_bias_g = after(qkv_bias_g, row_sums).reshape(-1)
    sums = [row_sums[0], row_sums[1], row_sums[2], row_sums[3], qkv_bias_g, row_sums[4], up_bias_g]
    total = sum_small(pack(sums)).reshape(-1)

    mlp_place = []
    for j in range(chunks):
        first = j * (D // 4)
        mlp_place.append(
            (0, 0, part, first, tuple((2 * own_hidden, b * own_hidden + j * WIDE) for b in range(2)))
        )
        mlp_place.append((1, j * WIDE, deep, first + 2 * part, ((WIDE, 0),)))
    up_weight_g, down_weight_g = place(
        ids, [(own, hidden_units), (own_hidden, D)], mlp_place, after(mlp_parts, *sends), mlp_other
    )
    attention_place = [
        (0, 0, part, 0, tuple((3 * WIDE, b * WIDE) for b in range(3))),
        (1, 0, part, 3 * part, ((WIDE, 0),)),
    ]
    sends[0] = after(sends[0], up_weight_g, down_weight_g)
    parts = share_plane(shard_sum(sends))
    qkv_weight_g, out_weight_g = place(
        ids, [(own, 3 * D), (own, D)], attention_place, parts, swap(parts, "rep", 1)
    )
    summed, at_row = [], 0
    for s in sums:
        size = s.shape[0] // 4
        summed.append(lax.dynamic_slice(total, (at_row + z * size,), (size,)))
        at_row += s.shape[0]
    return (
        output,
        input_grad,
        summed[0],
        summed[1],
        summed[2],
        summed[3],
        qkv_weight_g,
        summed[4],
        out_weight_g,
        summed[5],
        up_weight_g,
        summed[6],
        down_weight_g,
        summed[5],
    )


def solution(mesh):
    tokens = P(("rep", "shard"), None)
    matrix, vector = P("shard", None), P("shard")
    params = (vector,) * 4 + (matrix, vector) * 4
    in_specs = (tokens, tokens, P(("rep", "shard"))) + params
    out_specs = (tokens, tokens) + params
    return jax.shard_map(body, mesh=mesh, in_specs=in_specs, out_specs=out_specs, check_vma=False)
```

```python
import functools

import jax
import jax.numpy as jnp
from jax import lax
from jax.experimental import pallas as pl
from jax.experimental.pallas import tpu as pltpu
from jax.sharding import PartitionSpec as P

D = 768
H = 12
HD = 64
ROT = 16
WIDE = 384
LANES = 128
F32, BF16 = jnp.float32, jnp.bfloat16
norm_eps = 1e-05


def compiler_params(mib):
    return pltpu.CompilerParams(vmem_limit_bytes=mib * 2**20)


def cost(microseconds):
    return pl.CostEstimate(
        flops=int(microseconds * 1.1e9), bytes_accessed=int(microseconds * 1e5), transcendentals=0
    )


VMEM = pl.BlockSpec(memory_space=pltpu.VMEM)
SMEM = pl.BlockSpec(memory_space=pltpu.SMEM)


def swap(value, axis, bit):
    size = lax.axis_size(axis)
    return lax.ppermute(value, axis, [(i, i ^ bit) for i in range(size)])


def place_ids():
    rep = lax.axis_index("rep").astype(jnp.uint32)
    return lax.axis_index("shard").astype(jnp.uint32), (rep >> 1) & 3, rep & 1


def after(value, *others):
    return lax.optimization_barrier((value, *others))[0]


def gather_far(piece):
    return jnp.stack([swap(piece, "shard", k) for k in (1, 2, 3)])


def far_of(near, rest):
    return jnp.concatenate([near[None], rest])


def gather_plane(far):
    return [far] + [swap(far, "rep", j * 2) for j in (1, 2, 3)]


def gather_core(parts):
    parts = jnp.stack(parts)
    return parts, swap(parts, "rep", 1)


def total_of(arrays):
    return (
        (arrays[0].astype(F32) + arrays[1].astype(F32))
        + (arrays[2].astype(F32) + arrays[3].astype(F32))
    ).astype(BF16)


def at(block, index):
    return lax.dynamic_index_in_dim(block, index, 0, keepdims=False)


def plane_sum_body(ids_ref, keep_ref, got_ref, *outs):
    q = ids_ref[1]
    for j in range(4):
        total = keep_ref[q ^ j].astype(F32) + got_ref[q ^ j].astype(F32)
        outs[j][...] = total.astype(BF16)


def plane_sends(ids, keep, got):
    rows = keep.shape[2]
    block = pl.BlockSpec((4, 1, rows, WIDE), lambda i: (0, i, 0, 0))
    return pl.pallas_call(
        plane_sum_body,
        grid=(4,),
        out_shape=[jax.ShapeDtypeStruct((4, rows, WIDE), BF16)] * 4,
        in_specs=[SMEM, block, block],
        out_specs=[pl.BlockSpec((1, rows, WIDE), lambda i: (i, 0, 0))] * 4,
        compiler_params=compiler_params(40),
        cost_estimate=cost(3),
        name="plane_sum",
    )(ids, keep, got)


def plane_swap(sends):
    return [sends[0]] + [swap(sends[j], "rep", j * 2) for j in (1, 2, 3)]


def shard_sends(groups, z):
    return [
        jnp.concatenate([total_of([at(term, z ^ k) for term in terms]) for terms in groups])
        for k in range(4)
    ]


def shard_sum(sends):
    owned = total_of([sends[0]] + [swap(sends[k], "shard", k) for k in (1, 2, 3)])
    bit = 8
    while bit < lax.axis_size("rep"):
        owned = (owned.astype(F32) + swap(owned, "rep", bit).astype(F32)).astype(BF16)
        bit *= 2
    return owned


def share_plane(owned):
    return jnp.stack([owned] + [swap(owned, "rep", j * 2) for j in (1, 2, 3)])


def sum_small(vector):
    bit = 1
    while bit < lax.axis_size("rep"):
        if bit not in (2, 4):
            vector = vector + swap(vector, "rep", bit)
        bit *= 2
    vector = (vector + swap(vector, "rep", 2)) + (swap(vector, "rep", 4) + swap(vector, "rep", 6))
    return (vector + swap(vector, "shard", 1)) + (swap(vector, "shard", 2) + swap(vector, "shard", 3))


def pack(vectors):
    flat = jnp.concatenate([v.reshape(-1) for v in vectors])
    fill = -flat.shape[0] % 1024
    return jnp.concatenate([flat, jnp.zeros((fill,), flat.dtype)]).reshape(-1, LANES)


def assemble_body(plan, ids_ref, *refs):
    count = len(plan)
    shards, pieces, outs = refs[:count], refs[count : count + 2], refs[count + 2 :]
    z, q, c = ids_ref[0], ids_ref[1], ids_ref[2]
    for shard_ref, out_ref, (rows, part, first, blocks, row_0, columns) in zip(shards, outs, plan):
        half = blocks * WIDE
        own = pl.ds(pl.multiple_of(z * rows, rows), rows)
        for b, col_0 in enumerate(columns):
            out_ref[own, b * WIDE : (b + 1) * WIDE] = shard_ref[row_0 : row_0 + rows, col_0 : col_0 + WIDE]
        for h, piece in ((c, pieces[0]), (1 - c, pieces[1])):
            for j in range(4):
                for k in (1, 2, 3):
                    row = pl.multiple_of((z ^ k) * rows + (q ^ j) * part, part)
                    for b in range(blocks):
                        col = pl.multiple_of(h * half + b * WIDE, WIDE)
                        start = first + b * part
                        out_ref[pl.ds(row, part), pl.ds(col, WIDE)] = piece[
                            j, k - 1, start : start + part, :
                        ]


def assemble(ids, shards, plan, pieces):
    shapes = [jax.ShapeDtypeStruct((4 * p[0], 2 * p[3] * WIDE), BF16) for p in plan]
    return pl.pallas_call(
        functools.partial(assemble_body, plan),
        out_shape=shapes,
        in_specs=[SMEM] + [VMEM] * (len(shards) + 2),
        out_specs=[VMEM] * len(shards),
        compiler_params=compiler_params(40),
        cost_estimate=cost(3),
        name="assemble",
    )(ids, *shards, *pieces)


def pack_small_body(*refs):
    out_ref = refs[-1]
    out_ref[...] = jnp.zeros_like(out_ref)
    for n, ref in enumerate(refs[:-1]):
        out_ref[n : n + 1, : ref.shape[1]] = ref[...].astype(F32)


def unpack_small_body(lengths, ids_ref, *refs):
    near, outs = refs[:4], refs[4:]
    z = ids_ref[0]
    for shard in range(4):
        rows = near[0][...].astype(F32)
        for k in (1, 2, 3):
            rows = jnp.where((z ^ k) == shard, near[k][...].astype(F32), rows)
        for n, (out_ref, length) in enumerate(zip(outs, lengths)):
            out_ref[:, shard * length : (shard + 1) * length] = rows[n : n + 1, :length]


def gather_small(ids, vectors, gate):
    lengths = [v.shape[0] for v in vectors]
    widest = max(lengths)
    packed = pl.pallas_call(
        pack_small_body,
        out_shape=jax.ShapeDtypeStruct((len(vectors), widest), F32),
        in_specs=[VMEM] * len(vectors),
        out_specs=VMEM,
        cost_estimate=cost(1),
        name="pack_small",
    )(*[v.astype(F32)[None, :] for v in vectors])
    packed = after(packed, gate)
    near = [packed] + [swap(packed, "shard", k) for k in (1, 2, 3)]
    return pl.pallas_call(
        functools.partial(unpack_small_body, lengths),
        out_shape=[jax.ShapeDtypeStruct((1, 4 * n), F32) for n in lengths],
        in_specs=[SMEM] + [VMEM] * 4,
        out_specs=[VMEM] * len(vectors),
        cost_estimate=cost(1),
        name="unpack_small",
    )(ids, *near)


def place_body(plan, ids_ref, parts_ref, other_ref, *outs):
    q, c = ids_ref[1], ids_ref[2]
    for out, rows, part, first, blocks in plan:
        for h, pieces in ((c, parts_ref), (1 - c, other_ref)):
            for j in range(4):
                row = pl.multiple_of(rows + (q ^ j) * part, part)
                for b, (scale, offset) in enumerate(blocks):
                    col = pl.multiple_of(h * scale + offset, WIDE)
                    start = first + b * part
                    outs[out][pl.ds(row, part), pl.ds(col, WIDE)] = pieces[
                        j, start : start + part, :
                    ].astype(F32)


def place(ids, shapes, plan, parts, other):
    return pl.pallas_call(
        functools.partial(place_body, plan),
        out_shape=[jax.ShapeDtypeStruct(s, F32) for s in shapes],
        in_specs=[SMEM, VMEM, VMEM],
        out_specs=[VMEM] * len(shapes),
        compiler_params=compiler_params(40),
        cost_estimate=cost(3),
        name="place",
    )(ids, parts, other)


def dot(left, right, left_dim=1, right_dim=0):
    return lax.dot_general(
        left, right, (((left_dim,), (right_dim,)), ((), ())), preferred_element_type=F32
    )


def turn(values, cosine, early, late):
    width = values.shape[1]
    return (
        values * cosine
        + pltpu.roll(values, width - ROT // 2, 1) * early
        + pltpu.roll(values, ROT // 2, 1) * late
    )


def qkv_body(gate_ref, x_ref, w_ref, bias_ref, cos_ref, early_ref, late_ref, out_ref):
    values = dot(x_ref[...], w_ref[...]) + bias_ref[...]

    @pl.when(pl.program_id(0) < 4)
    def rotate_block():
        for b in range(WIDE // LANES):
            cols = slice(b * LANES, (b + 1) * LANES)
            out_ref[:, cols] = turn(
                values[:, cols], cos_ref[...], early_ref[...], late_ref[...]
            ).astype(BF16)

    @pl.when(pl.program_id(0) >= 4)
    def plain_block():
        out_ref[...] = values.astype(BF16)


def qkv_call(gate, first_b, weight, bias, tables):
    tokens = first_b.shape[0]
    whole = lambda r, c: pl.BlockSpec((r, c), lambda i: (0, 0))
    return pl.pallas_call(
        qkv_body,
        grid=(3 * D // WIDE,),
        out_shape=jax.ShapeDtypeStruct((tokens, 3 * D), BF16),
        in_specs=[
            SMEM,
            whole(tokens, D),
            pl.BlockSpec((D, WIDE), lambda i: (0, i)),
            pl.BlockSpec((1, WIDE), lambda i: (0, i)),
        ]
        + [whole(tokens, LANES)] * 3,
        out_specs=pl.BlockSpec((tokens, WIDE), lambda i: (0, i)),
        compiler_params=compiler_params(40),
        cost_estimate=cost(11),
        name="qkv",
    )(gate, first_b, weight, bias, *tables)


def attention_body(
    first_call, gate_ref, q_ref, k_ref, v_ref, cot_ref, w_ref, mask_ref, cos_ref, early_ref, late_ref, *refs
):
    mixed_ref, grad_ref, key_t_ref, value_t_ref = refs if first_call else refs[2:]
    tokens = q_ref.shape[0]
    step = min(256, tokens)
    out_grad = dot(cot_ref[...], w_ref[...], 1, 1).astype(BF16)
    lane = lax.broadcasted_iota(jnp.int32, (tokens, LANES), 1)
    query_t = q_ref[...].astype(F32).T.astype(BF16)
    out_grad_t = out_grad.astype(F32).T.astype(BF16)
    nothing = jnp.zeros((tokens, LANES), BF16)
    keys = k_ref[...] * BF16(HD**-0.5)
    heads = []
    for h in range(2):
        here = (lane // HD) == h
        heads.append((jnp.where(here, keys, nothing), jnp.where(here, v_ref[...], nothing)))
    key_t_ref[...] = jnp.zeros_like(key_t_ref)
    value_t_ref[...] = jnp.zeros_like(value_t_ref)
    for first in range(0, tokens, step):
        last = first + step
        block = slice(first, last)
        mixed = jnp.zeros((step, LANES), F32)
        query_grad = jnp.zeros((step, LANES), F32)
        both = range(2)
        keys_h = [heads[h][0][:last] for h in both]
        values_h = [heads[h][1][:last] for h in both]
        bias = mask_ref[block, :last]
        scores = [dot(q_ref[block, :], keys_h[h], 1, 1) + bias for h in both]
        probs_grad = [dot(out_grad[block], values_h[h], 1, 1) for h in both]
        expo = [jnp.exp(s - jnp.max(s, axis=1, keepdims=True)) for s in scores]
        probs = [e * (1.0 / jnp.sum(e, axis=1, keepdims=True)) for e in expo]
        probs_b = [p.astype(BF16) for p in probs]
        weighted = [g * p for g, p in zip(probs_grad, probs)]
        scores_grad = [
            (w - p * jnp.sum(w, axis=1, keepdims=True)).astype(BF16)
            for w, p in zip(weighted, probs)
        ]
        for h in both:
            rows = slice(h * HD, (h + 1) * HD)
            mixed += dot(probs_b[h], values_h[h])
            query_grad += dot(scores_grad[h], keys_h[h])
            key_t_ref[rows, :last] += dot(query_t[rows, block], scores_grad[h])
            value_t_ref[rows, :last] += dot(out_grad_t[rows, block], probs_b[h])
        mixed_ref[block, :] = mixed.astype(BF16)
        grad_ref[0, block, :] = turn(
            query_grad, cos_ref[block, :], -early_ref[block, :], -late_ref[block, :]
        ).astype(BF16)
    grad_ref[1, :, :] = turn(
        key_t_ref[...].T * HD**-0.5, cos_ref[...], -early_ref[...], -late_ref[...]
    ).astype(BF16)
    grad_ref[2, :, :] = value_t_ref[...].T.astype(BF16)


def attention_call(gate, start, pairs, qkv_b, cot_b, out_weight, mask, tables, earlier):
    tokens = qkv_b.shape[0]
    every = D // LANES
    whole = lambda r, c: pl.BlockSpec((r, c), lambda i: (0, 0))
    part = lambda n: pl.BlockSpec((tokens, LANES), lambda i: (0, n * every + start + i))
    anywhere = pl.BlockSpec(memory_space=pl.ANY)
    return pl.pallas_call(
        functools.partial(attention_body, not earlier),
        grid=(pairs,),
        out_shape=[
            jax.ShapeDtypeStruct((tokens, D), BF16),
            jax.ShapeDtypeStruct((3, tokens, D), BF16),
        ],
        in_specs=[
            SMEM,
            part(0),
            part(1),
            part(2),
            whole(tokens, D),
            pl.BlockSpec((LANES, D), lambda i: (start + i, 0)),
            whole(tokens, tokens),
        ]
        + [whole(tokens, LANES)] * 3
        + [anywhere] * len(earlier),
        out_specs=[
            pl.BlockSpec((tokens, LANES), lambda i: (0, start + i)),
            pl.BlockSpec((3, tokens, LANES), lambda i: (0, 0, start + i)),
        ],
        scratch_shapes=[
            pltpu.VMEM((LANES, tokens), F32),
            pltpu.VMEM((LANES, tokens), F32),
        ],
        input_output_aliases={10: 0, 11: 1} if earlier else {},
        compiler_params=compiler_params(56),
        cost_estimate=cost(9 * pairs),
        name="attention",
    )(gate, qkv_b, qkv_b, qkv_b, cot_b, out_weight, mask, *tables, *earlier)


def store_block(keep_ref, send_ref, here, block, part, row):
    def store(ref):
        for z in range(4):
            for q in range(4):
                start = (z * 4 + q) * part
                ref[q, z, pl.ds(row, part), :] = block[start : start + part, :]

    pl.when(here)(lambda: store(keep_ref))
    pl.when(jnp.logical_not(here))(lambda: store(send_ref))


def qkv_grad_body(ids_ref, grad_ref, first_t_ref, mixed_ref, cot_ref, keep_ref, send_ref, bias_ref):
    step = pl.program_id(0)
    grad = grad_ref[0]
    h, b = step // 3, step % 3
    here = h == ids_ref[2]
    part = D // 16
    block = dot(first_t_ref[...], grad).astype(BF16)
    store_block(keep_ref, send_ref, here, block, part, pl.multiple_of(b * part, part))
    bias_ref[...] = jnp.sum(grad.astype(F32), axis=0, keepdims=True)

    @pl.when(b == 0)
    def out_part():
        block = dot(mixed_ref[...], cot_ref[...], 0, 0).astype(BF16)
        store_block(keep_ref, send_ref, here, block, part, 3 * part)


def qkv_grad_call(ids, grads, first_t, mixed_b, cot_b):
    tokens = cot_b.shape[0]
    whole = lambda r, c: pl.BlockSpec((r, c), lambda i: (0, 0))
    pack_spec = pl.BlockSpec((4, 4, D // 4, WIDE), lambda i: (0, 0, 0, 0))
    return pl.pallas_call(
        qkv_grad_body,
        grid=(3 * D // WIDE,),
        out_shape=[
            jax.ShapeDtypeStruct((4, 4, D // 4, WIDE), BF16),
            jax.ShapeDtypeStruct((4, 4, D // 4, WIDE), BF16),
            jax.ShapeDtypeStruct((1, 3 * D), F32),
        ],
        in_specs=[
            SMEM,
            pl.BlockSpec((1, tokens, WIDE), lambda i: (i // 2, 0, i % 2)),
            whole(D, tokens),
            whole(tokens, D),
            pl.BlockSpec((tokens, WIDE), lambda i: (0, i // 3)),
        ],
        out_specs=[pack_spec, pack_spec, pl.BlockSpec((1, WIDE), lambda i: (0, i))],
        compiler_params=compiler_params(56),
        cost_estimate=cost(14),
        name="qkv_grad",
    )(ids, grads, first_t, mixed_b, cot_b)


def mlp_body(
    ids_ref, x_ref, x_t_ref, cot_ref, up_ref, down_ref, bias_ref,
    act_ref, grad_ref, keep_ref, send_ref, bias_grad_ref,
):
    step = pl.program_id(0)
    tokens = x_ref.shape[0]
    rows = min(256, tokens)
    total = jnp.zeros((1, WIDE), F32)
    blocks = [slice(first, first + rows) for first in range(0, tokens, rows)]
    ups = [dot(x_ref[block, :], up_ref[...]) + bias_ref[...] for block in blocks]
    act_grads = [dot(cot_ref[block, :], down_ref[...], 1, 1) for block in blocks]
    for block, up, act_grad in zip(blocks, ups, act_grads):
        below = 0.5 + 0.5 * lax.erf(up * (0.5**0.5))
        slope = below + up * (jnp.exp(-0.5 * up * up) * 0.3989422804014327)
        up_grad = (act_grad * slope).astype(BF16)
        act_ref[block, :] = (up * below).astype(BF16)
        grad_ref[block, :] = up_grad
        total += jnp.sum(up_grad.astype(F32), axis=0, keepdims=True)
    bias_grad_ref[...] = total
    part = D // 16
    c = ids_ref[2]
    block = dot(x_t_ref[...], grad_ref[...]).astype(BF16)
    store_block(
        keep_ref, send_ref, step // 2 == c, block, part, pl.multiple_of((step % 2) * part, part)
    )
    down = dot(act_ref[...], cot_ref[...], 0, 0).astype(BF16)
    deep = WIDE // 4

    def store_down(keep, send):
        for q in range(4):
            rows_here = slice(q * deep, (q + 1) * deep)
            keep_ref[q, step, 2 * part :, :] = down[rows_here, keep * WIDE : (keep + 1) * WIDE]
            send_ref[q, step, 2 * part :, :] = down[rows_here, send * WIDE : (send + 1) * WIDE]

    pl.when(c == 0)(lambda: store_down(0, 1))
    pl.when(c == 1)(lambda: store_down(1, 0))


def mlp_call(ids, second_b, second_t, cot_b, up_weight, down_weight, bias, chunk, chunks):
    tokens = cot_b.shape[0]
    whole = lambda r, c: pl.BlockSpec((r, c), lambda i: (0, 0))
    column = pl.BlockSpec((tokens, WIDE), lambda i: (0, i))
    pack_spec = pl.BlockSpec((4, 4, D // 4, WIDE), lambda i: (0, 0, 0, 0))
    return pl.pallas_call(
        mlp_body,
        grid=(4,),
        out_shape=[
            jax.ShapeDtypeStruct((tokens, 4 * WIDE), BF16),
            jax.ShapeDtypeStruct((tokens, 4 * WIDE), BF16),
            jax.ShapeDtypeStruct((4, 4, D // 4, WIDE), BF16),
            jax.ShapeDtypeStruct((4, 4, D // 4, WIDE), BF16),
            jax.ShapeDtypeStruct((1, 4 * WIDE), F32),
        ],
        in_specs=[
            SMEM,
            whole(tokens, D),
            whole(D, tokens),
            whole(tokens, D),
            pl.BlockSpec((D, WIDE), lambda i: (0, i)),
            pl.BlockSpec((WIDE, D), lambda i: (i, 0)),
            pl.BlockSpec((1, WIDE), lambda i: (0, i * chunks + chunk)),
        ],
        out_specs=[column, column, pack_spec, pack_spec, pl.BlockSpec((1, WIDE), lambda i: (0, i))],
        compiler_params=compiler_params(56),
        cost_estimate=cost(20),
        name="mlp",
    )(ids, second_b, second_t, cot_b, up_weight, down_weight, bias)


def output_body(count, gate_ref, hidden_ref, mixed_ref, out_w_ref, out_bias_ref, down_bias_ref, *refs):
    acts, downs, out_ref = refs[:count], refs[count : 2 * count], refs[2 * count]
    wide = dot(acts[0][...], downs[0][...])
    for a, w in zip(acts[1:], downs[1:]):
        wide += dot(a[...], w[...])
    attention = dot(mixed_ref[...], out_w_ref[...]) + out_bias_ref[...]
    out_ref[...] = hidden_ref[...] + attention + (wide + down_bias_ref[...])


def output_call(gate, hidden, mixed_b, out_weight, out_bias, down_bias, acts, downs):
    tokens = hidden.shape[0]
    rows = min(256, tokens)
    row = lambda c: pl.BlockSpec((rows, c), lambda i: (i, 0))
    whole = lambda a: pl.BlockSpec(a.shape, lambda i: (0, 0))
    return pl.pallas_call(
        functools.partial(output_body, len(acts)),
        grid=(tokens // rows,),
        out_shape=jax.ShapeDtypeStruct((tokens, D), F32),
        in_specs=[SMEM, row(D), row(D), whole(out_weight), whole(out_bias), whole(down_bias)]
        + [row(a.shape[1]) for a in acts]
        + [whole(w) for w in downs],
        out_specs=row(D),
        compiler_params=compiler_params(56),
        cost_estimate=cost(10),
        name="output",
    )(gate, hidden, mixed_b, out_weight, out_bias, down_bias, *acts, *downs)


def input_grad_body(count, gate_ref, hidden_ref, cot_ref, grad_ref, w_ref, gain_1_ref, gain_2_ref, *refs):
    ups, weights, out_ref, sums_ref = refs[:count], refs[count : 2 * count], refs[2 * count], refs[2 * count + 1]
    first = dot(grad_ref[0], w_ref[:, :D], 1, 1)
    for n in (1, 2):
        first += dot(grad_ref[n], w_ref[:, n * D : (n + 1) * D], 1, 1)
    second = dot(ups[0][...], weights[0][...], 1, 1)
    for u, w in zip(ups[1:], weights[1:]):
        second += dot(u[...], w[...], 1, 1)
    normed, scale = normalize(hidden_ref[...])
    cot = cot_ref[...]
    inner = first * gain_1_ref[...] + second * gain_2_ref[...]
    out_ref[...] = cot + scale * (
        inner
        - jnp.mean(inner, axis=-1, keepdims=True)
        - normed * jnp.mean(inner * normed, axis=-1, keepdims=True)
    )

    @pl.when(pl.program_id(0) == 0)
    def clear():
        sums_ref[...] = jnp.zeros_like(sums_ref)

    for n, value in enumerate((first * normed, first, second * normed, second, cot)):
        sums_ref[n : n + 1, :] += jnp.sum(value, axis=0, keepdims=True)


def input_grad_call(gate, hidden, cotangent, grads, weight, gain_1, gain_2, ups, weights):
    tokens = hidden.shape[0]
    rows = min(256, tokens)
    row = lambda c: pl.BlockSpec((rows, c), lambda i: (i, 0))
    whole = lambda a: pl.BlockSpec(a.shape, lambda i: (0, 0))
    return pl.pallas_call(
        functools.partial(input_grad_body, len(ups)),
        grid=(tokens // rows,),
        out_shape=[jax.ShapeDtypeStruct((tokens, D), F32), jax.ShapeDtypeStruct((8, D), F32)],
        in_specs=[
            SMEM,
            row(D),
            row(D),
            pl.BlockSpec((3, rows, D), lambda i: (0, i, 0)),
            whole(weight),
            whole(gain_1),
            whole(gain_2),
        ]
        + [row(u.shape[1]) for u in ups]
        + [whole(w) for w in weights],
        out_specs=[row(D), pl.BlockSpec((8, D), lambda i: (0, 0))],
        compiler_params=compiler_params(56),
        cost_estimate=cost(14),
        name="input_grad",
    )(gate, hidden, cotangent, grads, weight, gain_1, gain_2, *ups, *weights)


def normalize(values):
    centre = values - jnp.mean(values, axis=-1, keepdims=True)
    scale = lax.rsqrt(jnp.mean(centre * centre, axis=-1, keepdims=True) + norm_eps)
    return centre * scale, scale


def first_body(
    gate_ref, hidden_ref, cot_ref, seg_col_ref, seg_row_ref, gain_1_ref, shift_1_ref, gain_2_ref, shift_2_ref,
    first_ref, second_ref, first_t_ref, second_t_ref, cot_b_ref, mask_ref, places_ref,
):
    normed, _ = normalize(hidden_ref[...])
    first = (normed * gain_1_ref[...] + shift_1_ref[...]).astype(BF16)
    second = (normed * gain_2_ref[...] + shift_2_ref[...]).astype(BF16)
    first_ref[...] = first
    second_ref[...] = second
    first_t_ref[...] = first.astype(F32).T.astype(BF16)
    second_t_ref[...] = second.astype(F32).T.astype(BF16)
    cot_b_ref[...] = cot_ref[...].astype(BF16)
    rows, tokens = mask_ref.shape
    row = pl.program_id(0) * rows + lax.broadcasted_iota(jnp.int32, (rows, tokens), 0)
    col = lax.broadcasted_iota(jnp.int32, (rows, tokens), 1)
    mine, others = seg_col_ref[...], seg_row_ref[...]
    mask_ref[...] = jnp.where((mine == others) & (col <= row), 0.0, -1e30)
    before = jnp.sum(jnp.where(mine > others, 1.0, 0.0), axis=1, keepdims=True)
    places_ref[...] = row[:, :LANES].astype(F32) - before


def first_call(gate, hidden, cotangent, segments, vectors):
    tokens = hidden.shape[0]
    rows = min(256, tokens)
    row = lambda c: pl.BlockSpec((rows, c), lambda i: (i, 0))
    turned = pl.BlockSpec((D, rows), lambda i: (0, i))
    whole = lambda r, c: pl.BlockSpec((r, c), lambda i: (0, 0))
    wide = jax.ShapeDtypeStruct((tokens, D), BF16)
    tall = jax.ShapeDtypeStruct((D, tokens), BF16)
    return pl.pallas_call(
        first_body,
        grid=(tokens // rows,),
        out_shape=[
            wide,
            wide,
            tall,
            tall,
            wide,
            jax.ShapeDtypeStruct((tokens, tokens), F32),
            jax.ShapeDtypeStruct((tokens, LANES), F32),
        ],
        in_specs=[SMEM, row(D), row(D), row(1), whole(1, tokens)] + [whole(1, D)] * 4,
        out_specs=[row(D), row(D), turned, turned, row(D), row(tokens), row(LANES)],
        compiler_params=compiler_params(40),
        cost_estimate=cost(12),
        name="first",
    )(
        gate,
        hidden,
        cotangent,
        segments[:, None],
        segments[None, :],
        *vectors,
    )


def rotary_tables(places):
    half = ROT // 2
    lane = jnp.arange(LANES, dtype=jnp.int32) % HD
    freqs = 1.0 / 10000.0 ** ((lane % half).astype(F32) * 2.0 / ROT)
    angles = places * freqs[None, :]
    cosine, sine = jnp.cos(angles), jnp.sin(angles)
    turned, early = (lane < ROT)[None, :], (lane < half)[None, :]
    return (
        jnp.where(turned, cosine, 1.0),
        jnp.where(early, -sine, 0.0),
        jnp.where(turned & ~early, sine, 0.0),
    )


def take(array, row, col, rows, cols):
    return lax.dynamic_slice(array, (row, col), (rows, cols))


def body(
    hidden_in,
    cotangent,
    seg_ids,
    first_gain,
    first_shift,
    second_gain,
    second_shift,
    qkv_weight,
    qkv_bias,
    out_weight,
    out_bias,
    up_weight,
    up_bias,
    down_weight,
    down_bias,
):
    z, q, c = place_ids()
    ids = jnp.stack([z, q, c]).astype(jnp.int32)
    own = qkv_weight.shape[0]
    part = own // 4
    hidden_units = up_weight.shape[1]
    own_hidden = down_weight.shape[0]
    chunks = own_hidden // WIDE
    deep = WIDE // 4
    weight_pieces = []
    for j in range(chunks):
        weight_pieces.append(
            jnp.concatenate(
                [take(up_weight, q * part, (2 * c + b) * own_hidden + j * WIDE, part, WIDE) for b in range(2)]
                + [take(down_weight, j * WIDE + q * deep, c * WIDE, deep, WIDE)]
            )
        )
    weight_pieces.append(
        jnp.concatenate(
            [take(qkv_weight, q * part, c * 3 * WIDE + b * WIDE, part, WIDE) for b in range(3)]
            + [take(out_weight, q * part, c * WIDE, part, WIDE)]
        )
    )
    attention_plan = (
        (own, part, 0, 3, 0, tuple(b * WIDE for b in range(6))),
        (own, part, 3 * part, 1, 0, (0, WIDE)),
    )
    far = gather_far(weight_pieces[0])
    parts = gather_plane(far)
    small = gather_small(
        ids,
        [first_gain, first_shift, second_gain, second_shift]
        + [qkv_bias, out_bias, up_bias, down_bias],
        far,
    )
    gain_1, shift_1, gain_2, shift_2, qkv_b0, out_b0, up_b0, down_b0 = small
    weight_pieces = [after(p, far) for p in weight_pieces[1:]]
    near = list(swap(jnp.stack(weight_pieces), "shard", 1))
    onward = [jnp.stack([p, n]) for p, n in zip(weight_pieces, near)]
    first_b, second_b, first_t, second_t, cot_b, mask, places = first_call(
        after(ids, far, *onward), hidden_in, cotangent, seg_ids, small[:4]
    )
    coming = swap(onward[0], "shard", 2)
    done = first_b
    tables = rotary_tables(places)

    acts, ups, downs, up_weights, bias_parts, plane_terms, pending = [], [], [], [], [], [], None
    order = ids
    for j in range(chunks):
        coming = after(coming, done)
        pieces = gather_core([after(p, done, coming) for p in parts])
        far = far_of(near[j], coming)
        parts = gather_plane(far)
        if j + 1 < len(near):
            coming = swap(after(onward[j + 1], far), "shard", 2)
        order = after(order, far)
        mlp_plan = (
            (own, part, 0, 2, 0, tuple(b * own_hidden + j * WIDE for b in range(4))),
            (WIDE, deep, 2 * part, 1, j * WIDE, (0, WIDE)),
        )
        up_full, down_full = assemble(ids, (up_weight, down_weight), mlp_plan, pieces)
        act, up_grad, keep, send, bias_g = mlp_call(
            order,
            second_b,
            second_t,
            cot_b,
            up_full,
            down_full,
            up_b0,
            j,
            chunks,
        )
        done = keep
        acts.append(act)
        ups.append(up_grad)
        downs.append(down_full)
        up_weights.append(up_full)
        bias_parts.append(bias_g.reshape(4, WIDE))
        if pending is not None:
            keep_before, got_before = pending
            sends = plane_sends(after(ids, keep), keep_before, got_before)
            plane_terms.append(plane_swap(sends))
            order_next = sends
            send = after(send, *sends)
            done = sends[0]
        pending = (keep, swap(send, "rep", 1))
        order = after(ids, keep, send)
    pieces = gather_core([after(p, done) for p in parts])
    qkv_full, out_full = assemble(ids, (qkv_weight, out_weight), attention_plan, pieces)
    gate = after(ids, *order_next) if chunks > 1 else order
    qkv_b = qkv_call(gate, first_b, qkv_full, qkv_b0, tables)
    keep, got = pending
    sends = plane_sends(after(ids, qkv_b), keep, got)
    plane_terms.append(plane_swap(sends))

    pairs = D // LANES // 3
    earlier = attention_call(after(ids, *sends), 0, pairs, qkv_b, cot_b, out_full, mask, tables, ())
    earlier = attention_call(ids, pairs, pairs, qkv_b, cot_b, out_full, mask, tables, tuple(earlier))
    gate = earlier[0]
    plane_terms = [[after(terms[0], gate)] + terms[1:] for terms in plane_terms]
    sends = shard_sends(plane_terms, z)
    earlier = attention_call(
        after(ids, *sends), 2 * pairs, pairs, qkv_b, cot_b, out_full, mask, tables, tuple(earlier)
    )
    owned = shard_sum([after(sends[0], earlier[0])] + sends[1:])
    mixed_b, grads = earlier
    keep, send, qkv_bias_g = qkv_grad_call(after(ids, owned), grads, first_t, mixed_b, cot_b)
    owned = after(owned, keep)
    shared = [owned] + [swap(owned, "rep", j * 2) for j in (1, 2, 3)]
    got = swap(send, "rep", 1)
    output = output_call(
        after(ids, send, owned), hidden_in, mixed_b, out_full, out_b0, down_b0, acts, downs
    )
    sends = plane_sends(after(ids, output), keep, got)
    terms = plane_swap(sends)
    mlp_parts = jnp.stack([after(s, output) for s in shared])
    mlp_other = swap(mlp_parts, "rep", 1)
    input_grad, row_sums = input_grad_call(
        after(ids, mlp_parts, *sends),
        hidden_in,
        cotangent,
        grads,
        qkv_full,
        gain_1,
        gain_2,
        ups,
        up_weights,
    )
    terms[0] = after(terms[0], input_grad)
    sends = shard_sends([terms], z)
    row_sums = after(row_sums, *sends)
    up_bias_g = jnp.stack(after(bias_parts, row_sums), axis=1).reshape(-1)
    qkv_bias_g = after(qkv_bias_g, row_sums).reshape(-1)
    sums = [row_sums[0], row_sums[1], row_sums[2], row_sums[3], qkv_bias_g, row_sums[4], up_bias_g]
    total = sum_small(pack(sums)).reshape(-1)

    mlp_place = []
    for j in range(chunks):
        first = j * (D // 4)
        mlp_place.append(
            (0, 0, part, first, tuple((2 * own_hidden, b * own_hidden + j * WIDE) for b in range(2)))
        )
        mlp_place.append((1, j * WIDE, deep, first + 2 * part, ((WIDE, 0),)))
    up_weight_g, down_weight_g = place(
        ids, [(own, hidden_units), (own_hidden, D)], mlp_place, after(mlp_parts, *sends), mlp_other
    )
    attention_place = [
        (0, 0, part, 0, tuple((3 * WIDE, b * WIDE) for b in range(3))),
        (1, 0, part, 3 * part, ((WIDE, 0),)),
    ]
    sends[0] = after(sends[0], up_weight_g, down_weight_g)
    parts = share_plane(shard_sum(sends))
    qkv_weight_g, out_weight_g = place(
        ids, [(own, 3 * D), (own, D)], attention_place, parts, swap(parts, "rep", 1)
    )
    summed, at_row = [], 0
    for s in sums:
        size = s.shape[0] // 4
        summed.append(lax.dynamic_slice(total, (at_row + z * size,), (size,)))
        at_row += s.shape[0]
    return (
        output,
        input_grad,
        summed[0],
        summed[1],
        summed[2],
        summed[3],
        qkv_weight_g,
        summed[4],
        out_weight_g,
        summed[5],
        up_weight_g,
        summed[6],
        down_weight_g,
        summed[5],
    )


def solution(mesh):
    tokens = P(("rep", "shard"), None)
    matrix, vector = P("shard", None), P("shard")
    params = (vector,) * 4 + (matrix, vector) * 4
    in_specs = (tokens, tokens, P(("rep", "shard"))) + params
    out_specs = (tokens, tokens) + params
    return jax.shard_map(body, mesh=mesh, in_specs=in_specs, out_specs=out_specs, check_vma=False)
```
